32 devices in a mesh: wide: 8 (over z, x), narrow: 4 (over y, core).
Axes of the slice: x: 2, y: 2, z: 4, core: 2. Of those that a mesh axis runs over, the one named last changes fastest.
Arguments:
- tokens: bfloat16 [4096, 2048], P('wide', 'narrow'), may hold values from -6 to 6
- cotangent: bfloat16 [4096, 2048], P('wide', 'narrow'), may hold values from -6 to 6
- block_ids: int32 [8, 512], P('wide'), may hold values from 0 to 2, never falling along the last dimension, each value on 1 to 256 neighbouring positions
- routes: int32 [4096, 8], P('wide'), may hold values from 0 to 15, all different within a row; in each aligned block of 512 rows (0 to 511, 512 to 1023, ...) at most 272 rows name the same one
- norm_attn: bfloat16 [2048], P('narrow'), may hold values from 0.5 to 1.5
- w_query: bfloat16 [2048, 2048], P('wide', 'narrow'), may hold values from -0.125 to 0.125
- w_key: bfloat16 [2048, 2048], P('wide', 'narrow'), may hold values from -0.125 to 0.125
- w_value: bfloat16 [2048, 2048], P('wide', 'narrow'), may hold values from -0.125 to 0.125
- norm_query: bfloat16 [2048], P('narrow'), may hold values from 0.5 to 1.5
- norm_key: bfloat16 [2048], P('narrow'), may hold values from 0.5 to 1.5
- w_out: bfloat16 [2048, 2048], P('wide', 'narrow'), may hold values from -1 to 1
- norm_ffn: bfloat16 [2048], P('narrow'), may hold values from 0.5 to 1.5
- w_router: bfloat16 [2048, 16], replicated, may hold values from -0.0625 to 0.0625
- w_gate: bfloat16 [2048, 16, 1024], P('wide', None, 'narrow'), may hold values from -0.125 to 0.125
- w_up: bfloat16 [2048, 16, 1024], P('wide', None, 'narrow'), may hold values from -0.125 to 0.125
- w_down: bfloat16 [2048, 16, 1024], P('wide', None, 'narrow'), may hold values from -1.5 to 1.5
Outputs:
- block_out: bfloat16 [4096, 2048], P('wide', 'narrow')
- grad_tokens: float32 [4096, 2048], P('wide', 'narrow')
- grad_norm_attn: float32 [2048], P('narrow')
- grad_query: float32 [2048, 2048], P('wide', 'narrow')
- grad_key: float32 [2048, 2048], P('wide', 'narrow')
- grad_value: float32 [2048, 2048], P('wide', 'narrow')
- grad_norm_query: float32 [2048], P('narrow')
- grad_norm_key: float32 [2048], P('narrow')
- grad_out: float32 [2048, 2048], P('wide', 'narrow')
- grad_norm_ffn: float32 [2048], P('narrow')
- grad_router: float32 [2048, 16], replicated
- grad_gate: float32 [2048, 16, 1024], P('wide', None, 'narrow')
- grad_up: float32 [2048, 16, 1024], P('wide', None, 'narrow')
- grad_down: float32 [2048, 16, 1024], P('wide', None, 'narrow')
The draws below stay inside these ranges and needn't reach their ends.
Inputs may be any that keep to these rules, and one draw needn't show every extreme that they name: `block_ids`: block numbers never fall along a sequence; each block has 1 to 256 tokens and some block exactly 256. `routes`: each row names 8 different experts; among the tokens of one sequence no expert is named more than 272 times, a bound that some block reaches.
All inputs are finite; a program needn't handle non-finite values.
Results may differ from the reference program's by a relative error of at most 0.025.
Values may be sent and summed in bfloat16 or wider, within the bound.
No kernel may reach another device: no remote copies, remote signals or barrier semaphores. Data moves between devices by JAX's collectives and lax.ppermute only.
A program may use at most 384 MiB of HBM per device.

```python
import math
import jax
import jax.numpy as jnp
import numpy as np
from jax import lax

D = 2048
HEADS = 16
HD = 128
FF = 1024
EXPERTS = 16
TOP = 8
BLK = 256
TOK_DEV = 512
SEQS = 8
TOKENS = 4096
CAP = 272


def block_scale(stream_key, shape, split, smallest, top_value):
    level, own = 1.0, jax.random.fold_in(stream_key, 6)
    for axis_at, parts in split:
        heights = jnp.exp(jax.random.uniform(jax.random.fold_in(own, axis_at), (parts,), jnp.float32, smallest / len(split), top_value / len(split)))
        level = level * jnp.repeat(heights, shape[axis_at] // parts).reshape([-1 if axis == axis_at else 1 for axis in range(len(shape))])
    return level


def split_up(number_of, total, most, skew):
    weights = [(1 << 20) // math.isqrt(standing ** skew) + 1 for standing in range(2, number_of + 1)]
    rest, holding = total - most - (number_of - 1), [1] * (number_of - 1)
    while rest > 0:
        free = [i for i in range(number_of - 1) if holding[i] < most]
        whole, budget = sum([weights[i] for i in free]), rest
        for i in free:
            addition = min(most - holding[i], max(1, budget * weights[i] // whole), rest)
            holding[i] = holding[i] + addition
            rest = rest - addition
    return np.array([most] + holding)


def ragged(stream_key, amount, total, most, lean):
    if amount == 2:
        one = jax.random.randint(stream_key, (), max(1, total - most), min(most, total - 1) + 1)
        return jnp.stack([one, total - one])
    lengths = jnp.asarray(split_up(amount, total, most, lean), jnp.int32)
    couples = (amount - 1) // 2
    giver, receiver = lengths[1:1 + 2 * couples:2], lengths[2:2 + 2 * couples:2]
    room = jnp.minimum(giver - 1, most - receiver)
    passed = jax.random.randint(jax.random.fold_in(stream_key, 1), (couples,), 0, 1 << 20) % (room + 1)
    lengths = lengths.at[1:1 + 2 * couples:2].set(giver - passed).at[2:2 + 2 * couples:2].set(receiver + passed)
    return lengths[jax.random.permutation(jax.random.fold_in(stream_key, 2), amount)]


def routed_block(key, own, number, rows, count, top, bound, lean):
    ranking = jax.random.permutation(key, count)
    packed, ordinary = portions_of(count, rows * top, bound, lean, True), portions_of(count, rows * top, bound, lean, False)
    places = jnp.arange(count)

    def named(sizes, turn):
        used = int((sizes > 0).sum())
        fixed = max(1, used // 4)
        moved = fixed + (places - fixed + turn * (used - fixed)) % max(1, count - fixed)
        return jnp.zeros((count,), jnp.int32).at[ranking[jnp.where(places < fixed, places, moved)]].set(jnp.asarray(sizes, jnp.int32))

    sizes = jnp.where(number % 4 == 0, named(packed, number // 4), named(ordinary, number - number // 4 - 1))
    mixed = jax.random.permutation(jax.random.fold_in(own, 3), count)
    donor, sink = mixed[0:count // 2 * 2:2], mixed[1:count // 2 * 2:2]
    margin = jnp.minimum(sizes[donor] - 1, bound - sizes[sink]) // 2
    margin = jnp.where((donor == ranking[0]) | (sink == ranking[0]) | (sizes[sink] == 0), 0, jnp.maximum(margin, 0))
    moved = jax.random.randint(jax.random.fold_in(own, 4), (count // 2,), 0, 1 << 20) % (margin + 1)
    sizes = sizes.at[donor].add(-moved).at[sink].add(moved)
    items = jnp.searchsorted(jnp.cumsum(sizes), jnp.arange(rows * top), side="right").astype(jnp.int32)
    grid = items.reshape(top, rows).T
    grid = grid[jax.random.permutation(jax.random.fold_in(own, 1), rows)]
    turn = jax.random.randint(jax.random.fold_in(own, 2), (rows, 1), 0, top)
    return jnp.take_along_axis(grid, (jnp.arange(top)[None, :] + turn) % top, axis=1)


def portions_of(amount, total, bound, slope, full):
    weights = [(1 << 20) // math.isqrt(grade ** slope) + 1 for grade in range(1, amount + 1)]
    largest = bound if full else min(bound, max(-(-total // amount), total * weights[0] // sum(weights)))
    least = 1 if total - largest >= amount - 1 else 0
    given, surplus = [largest] + [least] * (amount - 1), total - largest - least * (amount - 1)
    while surplus > 0:
        free = [i for i in range(1, amount) if given[i] < largest] or [i for i in range(1, amount) if given[i] < bound]
        mass, left = sum([weights[i] for i in free]), surplus
        for i in free:
            extra = min(bound - given[i], max(1, left * weights[i] // mass), surplus)
            given[i] = given[i] + extra
            surplus = surplus - extra
    return np.array(given)


def scatter_about(own_key, shape, width, limit, shards=(), kind=jnp.bfloat16):
    values = width * jax.random.normal(own_key, shape, jnp.float32)
    if shards:
        values = values * block_scale(own_key, shape, shards, -0.22, 0.18)
    return jnp.clip(values, -limit, limit).astype(kind)


def setup_inputs(seed: int = 0) -> dict:
    key_list = jax.random.split(jax.random.key(seed), 17)
    tokens = scatter_about(key_list[0], (TOKENS, D), 1.0, 6.0, ((0, 8), (1, 4)))
    cotangent = scatter_about(key_list[1], (TOKENS, D), 1.0, 6.0, ((0, 8), (1, 4)))
    block_ids = jax.vmap(lambda own: jnp.searchsorted(jnp.cumsum(ragged(own, TOK_DEV // BLK + 1, TOK_DEV, BLK, 0)), jnp.arange(TOK_DEV), side="right"))(jax.random.split(key_list[2], SEQS)).reshape((SEQS, TOK_DEV)).astype(jnp.int32)
    routes_keys = jax.random.split(jax.random.fold_in(key_list[3], 1), TOKENS // TOK_DEV)
    routes_turns = jax.random.permutation(jax.random.fold_in(key_list[3], 3), TOKENS // TOK_DEV)
    routes = jax.vmap(lambda own, number: routed_block(jax.random.fold_in(key_list[3], 2), own, number, TOK_DEV, EXPERTS, TOP, CAP, 0))(routes_keys, routes_turns).reshape((TOKENS, TOP))
    norm_attn = jnp.clip(1.0 + 0.1 * jax.random.normal(key_list[4], (D,), jnp.float32), 0.5, 1.5).astype(jnp.bfloat16)
    w_query = scatter_about(key_list[5], (D, D), D ** -0.5, 0.125, ((0, 8), (1, 4)))
    w_key = scatter_about(key_list[6], (D, D), D ** -0.5, 0.125, ((0, 8), (1, 4)))
    w_value = scatter_about(key_list[7], (D, D), D ** -0.5, 0.125, ((0, 8), (1, 4)))
    norm_query = jnp.clip(1.0 + 0.1 * jax.random.normal(key_list[8], (D,), jnp.float32), 0.5, 1.5).astype(jnp.bfloat16)
    norm_key = jnp.clip(1.0 + 0.1 * jax.random.normal(key_list[9], (D,), jnp.float32), 0.5, 1.5).astype(jnp.bfloat16)
    w_out = scatter_about(key_list[10], (D, D), (max(D // 64, 1)) ** -0.5, 1.0, ((0, 8), (1, 4)))
    norm_ffn = jnp.clip(1.0 + 0.1 * jax.random.normal(key_list[11], (D,), jnp.float32), 0.5, 1.5).astype(jnp.bfloat16)
    w_router = scatter_about(key_list[12], (D, EXPERTS), (4 * D) ** -0.5, 0.0625)
    w_gate = scatter_about(key_list[13], (D, EXPERTS, FF), D ** -0.5, 0.125, ((0, 8), (2, 4)))
    w_up = scatter_about(key_list[14], (D, EXPERTS, FF), D ** -0.5, 0.125, ((0, 8), (2, 4)))
    w_down = scatter_about(key_list[15], (D, EXPERTS, FF), (max(FF // 64, 1)) ** -0.5, 1.5, ((0, 8), (2, 4)))
    return dict(tokens=tokens, cotangent=cotangent, block_ids=block_ids, routes=routes, norm_attn=norm_attn, w_query=w_query, w_key=w_key, w_value=w_value, norm_query=norm_query, norm_key=norm_key, w_out=w_out, norm_ffn=norm_ffn, w_router=w_router, w_gate=w_gate, w_up=w_up, w_down=w_down)


@jax.custom_vjp
def low(v):
    return lax.optimization_barrier(v.astype(jnp.bfloat16)).astype(jnp.float32)

@jax.custom_vjp
def low_back(v):
    return v

def low_keep(v):
    return (low(v), None)

def low_pass(kept, grad):
    return (grad,)

def back_keep(v):
    return (v, None)

def back_low(kept, grad):
    return (low(grad),)
low.defvjp(low_keep, low_pass)
low_back.defvjp(back_keep, back_low)
EPS = 1e-05
HIGHEST = lax.Precision.HIGHEST

def rms_scale(values, scales):
    return values * lax.rsqrt(lax.optimization_barrier(jnp.mean(values * values, axis=-1, keepdims=True)) + EPS) * scales

def rope_tables(length, head_dim):
    exponent = jnp.arange(0, head_dim, 2, dtype=jnp.float32) / head_dim
    angles = jnp.arange(length, dtype=jnp.float32)[:, None] * (10000.0 ** (-exponent))[None, :]
    angles = jnp.concatenate([angles, angles], axis=-1)
    return (jnp.cos(angles)[:, None, :], jnp.sin(angles)[:, None, :])

def rotate_half(values, cosines, sine_table):
    middle = values.shape[-1] // 2
    turned = jnp.concatenate([-values[..., middle:], values[..., :middle]], axis=-1)
    return values * cosines + turned * sine_table

def slot_tables(routes, experts, capacity):
    token_count, top_count = routes.shape
    flat_routes = routes.reshape(-1)
    onehot = (flat_routes[:, None] == jnp.arange(experts, dtype=jnp.int32)[None, :]).astype(jnp.int32)
    earlier = (jnp.cumsum(onehot, axis=0) - onehot).astype(jnp.int32)
    within = lax.optimization_barrier(jnp.sum(earlier * onehot, axis=1)).astype(jnp.int32)
    destination = (flat_routes * capacity + within).astype(jnp.int32)
    pair_ids = jnp.arange(token_count * top_count, dtype=jnp.int32)
    owners = jnp.full((experts * capacity,), token_count * top_count, jnp.int32).at[destination].set(pair_ids)
    return (destination.reshape(token_count, top_count), owners)

def one_sequence(seq_rows, seq_blocks, seq_routes, weights):
    gain_attn, w_query, w_key, w_value, gain_query, gain_key, w_out, gain_ffn, w_router, w_gate, w_up, w_down = weights
    length = seq_rows.shape[0]
    normed = low(rms_scale(seq_rows, gain_attn))
    queries = low_back(jnp.dot(normed, w_query, precision=HIGHEST))
    keys_raw = low_back(jnp.dot(normed, w_key, precision=HIGHEST))
    values_raw = low(low_back(jnp.dot(normed, w_value, precision=HIGHEST)))
    cosines, sine_table = rope_tables(length, HD)
    query_rot = low(rotate_half(rms_scale(queries, gain_query).reshape(length, HEADS, HD), cosines, sine_table))
    key_rot = low(rotate_half(rms_scale(keys_raw, gain_key).reshape(length, HEADS, HD), cosines, sine_table))
    scores = low_back(jnp.einsum('qhd,khd->hqk', query_rot, key_rot, precision=HIGHEST) * HD ** (-0.5))
    allowed = seq_blocks[None, :] <= seq_blocks[:, None]
    attention_weights = jax.nn.softmax(jnp.where(allowed[None], scores, -1e+30), axis=-1)
    attended = jnp.einsum('hqk,khd->qhd', low(attention_weights), values_raw.reshape(length, HEADS, HD), precision=HIGHEST)
    attended = low(low_back(attended.reshape(length, D)))
    residual = seq_rows + low_back(jnp.dot(attended, w_out.T, precision=HIGHEST))
    ffn_in = low(rms_scale(residual, gain_ffn))
    logits = low_back(jnp.dot(ffn_in, w_router, precision=HIGHEST))
    gate_values = jnp.take_along_axis(jax.nn.softmax(logits, axis=-1), seq_routes, axis=1)
    destination, owners = slot_tables(seq_routes, EXPERTS, CAP)
    slot_tokens = owners // TOP
    padded_in = jnp.concatenate([ffn_in, jnp.zeros((1, D), ffn_in.dtype)], axis=0)
    expert_rows = padded_in[slot_tokens].reshape(EXPERTS, CAP, D)
    gate_pre = low_back(jnp.einsum('ecd,def->ecf', expert_rows, w_gate, precision=HIGHEST))
    up_pre = low_back(jnp.einsum('ecd,def->ecf', expert_rows, w_up, precision=HIGHEST))
    hidden = low(jax.nn.silu(gate_pre) * up_pre)
    expert_out = low_back(jnp.einsum('ecf,def->ecd', hidden, w_down, precision=HIGHEST)).reshape(EXPERTS * CAP, D)
    moe_out = lax.optimization_barrier(jnp.sum(gate_values[:, :, None] * expert_out[destination], axis=1))
    return residual + moe_out

def reference(tokens, cotangent, block_ids, routes, norm_attn, w_query, w_key, w_value, norm_query, norm_key, w_out, norm_ffn, w_router, w_gate, w_up, w_down):
    weights = tuple((member.astype(jnp.float32) for member in (norm_attn, w_query, w_key, w_value, norm_query, norm_key, w_out, norm_ffn, w_router, w_gate, w_up, w_down)))

    def forward(rows_all, weight_set):

        def sequence_step(carried, inputs):
            return (carried, jax.checkpoint(one_sequence)(inputs[0], inputs[1], inputs[2], weight_set))
        _, outputs = lax.scan(sequence_step, jnp.zeros((), jnp.float32), (rows_all.reshape(SEQS, TOK_DEV, D), block_ids, routes.reshape(SEQS, TOK_DEV, TOP)))
        return outputs.reshape(SEQS * TOK_DEV, D)
    result, pullback = jax.vjp(forward, tokens.astype(jnp.float32), weights)
    grad_rows, grad_weights = pullback(cotangent.astype(jnp.float32))
    return (result.astype(jnp.bfloat16), grad_rows, grad_weights[0], grad_weights[1], grad_weights[2], grad_weights[3], grad_weights[4], grad_weights[5], grad_weights[6], grad_weights[7], grad_weights[8], grad_weights[9], grad_weights[10], grad_weights[11])
```

```python
import jax
import jax.numpy as jnp
from jax import lax
from jax.sharding import Mesh
from jax.sharding import PartitionSpec as P

HD = 128
EPS = 1e-05
WIDE = ("t", "g", "p")
NARROW = ("y", "c")
GROUP = ("g", "p", "c")
ALL = ("t", "g", "p", "y", "c")
BF = jnp.bfloat16
F32 = jnp.float32


def rms_scale(values, scales):
    return values * lax.rsqrt(jnp.mean(values * values, axis=-1, keepdims=True) + EPS) * scales


def rope_tables(length, head_dim):
    exponent = jnp.arange(0, head_dim, 2, dtype=F32) / head_dim
    angles = jnp.arange(length, dtype=F32)[:, None] * (10000.0 ** (-exponent))[None, :]
    angles = jnp.concatenate([angles, angles], axis=-1)
    return (jnp.cos(angles)[:, None, :], jnp.sin(angles)[:, None, :])


def rotate_half(values, cosines, sine_table):
    middle = values.shape[-1] // 2
    turned = jnp.concatenate([-values[..., middle:], values[..., :middle]], axis=-1)
    return values * cosines + turned * sine_table


def dot(a, b, contract):
    return lax.dot_general(a, b, (contract, ((), ())), preferred_element_type=F32)


def swap(values, axis, step=1):
    count = lax.axis_size(axis)
    return lax.ppermute(values, axis, [(i, i ^ step) for i in range(count)])


def gather_four(block, axis):
    count = lax.axis_size("y") * lax.axis_size("c")
    size = block.shape[axis]
    here = lax.axis_index("y") * lax.axis_size("c") + lax.axis_index("c")
    other = swap(block, "y")
    near = swap(block, "c")
    far = swap(other, "c")
    shape = list(block.shape)
    shape[axis] = size * count
    whole = jnp.zeros(shape, block.dtype)
    for piece, place in ((block, 0), (near, 1), (other, 2), (far, 3)):
        whole = lax.dynamic_update_slice_in_dim(whole, piece, (here ^ place) * size, axis)
    return whole


def sum_four(partial):
    length, width = partial.shape
    rows = length // 4
    y, c = lax.axis_index("y"), lax.axis_index("c")
    parts = partial.reshape(2, 2, rows, width)
    mine = lax.dynamic_index_in_dim(parts, c, 1, False)
    theirs = lax.dynamic_index_in_dim(parts, 1 - c, 1, False)
    mine = mine + swap(theirs.astype(BF), "c").astype(F32)
    keep = lax.dynamic_index_in_dim(mine, y, 0, False)
    send = lax.dynamic_index_in_dim(mine, 1 - y, 0, False)
    return keep + swap(send.astype(BF), "y").astype(F32)


def spread(block):
    count = lax.axis_size("g")
    far = [block] + [swap(block, "g", step) for step in range(1, count)]
    near = [swap(piece, "p") for piece in far]
    first = jnp.concatenate(far + near, axis=0)
    return jnp.concatenate([first, swap(first, "c")], axis=0)


def collect(partial):
    count = lax.axis_size("g")
    rows = partial.shape[0] // (4 * count)
    parts = partial.reshape(2, 2, count, rows, partial.shape[1])
    halves = parts[0] + swap(parts[1].astype(BF), "c").astype(F32)
    total = None
    order = list(range(1, count)) + [0]
    quarters = {s: halves[0, s] + swap(halves[1, s].astype(BF), "p").astype(F32) for s in order}
    total = quarters[0]
    for s in order[:-1]:
        total = total + swap(quarters[s].astype(BF), "g", s).astype(F32)
    return total


def by_distance(values):
    count = lax.axis_size("g")
    tail = values.shape[1:]
    v = values.reshape((count // 2, 2, 2, 2) + tail)
    g, p, c = lax.axis_index("g"), lax.axis_index("p"), lax.axis_index("c")
    for axis, bit in enumerate((g // 2, g % 2, p, c)):
        v = jnp.where(bit == 1, jnp.flip(v, axis), v)
    return v


def to_experts(columns):
    sent = lax.all_to_all(columns.T, GROUP, 0, 0, tiled=True)
    v = by_distance(sent)
    v = jnp.transpose(v, (3, 2, 0, 1, 4))
    return v.reshape(-1)


def to_owners(values, rows):
    count = lax.axis_size("g")
    v = values.reshape(2, 2, count // 2, 2, rows)
    v = jnp.transpose(v, (2, 3, 1, 0, 4)).reshape(4 * count, rows)
    v = by_distance(v).reshape(4 * count, rows)
    return lax.all_to_all(v, GROUP, 0, 0, tiled=True).T


def own_expert(weight):
    depth, experts, units = weight.shape
    got = lax.all_to_all(jnp.transpose(weight, (1, 0, 2)), GROUP, 0, 0, tiled=True)
    both = jnp.stack([got, swap(got, "y")])
    both = both.reshape(2, experts // 2, 2, depth, units)
    whole = jnp.transpose(both, (1, 3, 0, 2, 4)).reshape(experts // 2 * depth, 4 * units)
    if lax.axis_size("t") > 1:
        whole = lax.all_gather(whole, "t", axis=0, tiled=True)
    return whole


def to_slices(grad, experts):
    model, hidden = grad.shape
    units = hidden // 4
    parts = grad.reshape(model, 2, 2 * units)
    mine = parts[:, 0] + swap(parts[:, 1].astype(BF), "y").astype(F32)
    if lax.axis_size("t") > 1:
        mine = lax.psum_scatter(mine.astype(BF), "t", scatter_dimension=0, tiled=True)
    depth = mine.shape[0] * 2 // experts
    mine = mine.astype(BF).reshape(experts // 2, depth, 2, units)
    sent = jnp.transpose(mine, (0, 2, 1, 3)).reshape(experts, depth, units)
    got = lax.all_to_all(sent, GROUP, 0, 0, tiled=True)
    return jnp.transpose(got, (1, 0, 2)).astype(F32)


def per_device(
    tokens,
    cotangent,
    block_ids,
    routes,
    norm_attn,
    w_query,
    w_key,
    w_value,
    norm_query,
    norm_key,
    w_out,
    norm_ffn,
    w_router,
    w_gate,
    w_up,
    w_down,
):
    experts = w_router.shape[1]
    lane_index = lax.axis_index("y") * lax.axis_size("c") + lax.axis_index("c")
    lanes = lax.axis_size("y") * lax.axis_size("c")
    length, head_cols = tokens.shape
    model_width = head_cols * lanes
    rows = length // lanes
    heads_here = head_cols // HD
    score_scale = HD ** (-0.5)

    rows_full = gather_four(tokens, 1)
    gains = lax.all_gather(jnp.stack([norm_attn, norm_ffn]), NARROW, axis=1, tiled=True)
    attn_gain = gains[0].astype(F32)
    ffn_gain = gains[1].astype(F32)
    qkv_full = lax.all_gather(
        jnp.concatenate([w_query, w_key, w_value], axis=1), WIDE, axis=0, tiled=True
    )
    query_full = qkv_full[:, :head_cols]
    key_full = qkv_full[:, head_cols : 2 * head_cols]
    value_full = qkv_full[:, 2 * head_cols :]
    out_full = lax.all_gather(w_out, WIDE, axis=0, tiled=True)

    cot_rows = lax.all_to_all(cotangent.reshape(lanes, rows, head_cols), NARROW, 0, 0, tiled=True)
    cot_rows = jnp.transpose(cot_rows, (1, 0, 2)).reshape(rows, model_width)
    cot_all = spread(cot_rows)

    gate_own = own_expert(w_gate)
    up_own = own_expert(w_up)
    down_own = own_expert(w_down)

    rows_float = rows_full.astype(F32)
    normed = rms_scale(rows_float, attn_gain).astype(BF)
    query_raw = jnp.dot(normed, query_full, preferred_element_type=F32)
    key_raw = jnp.dot(normed, key_full, preferred_element_type=F32)
    value_raw = jnp.dot(normed, value_full, preferred_element_type=F32)
    square_query, square_key = lax.psum(
        (jnp.sum(query_raw * query_raw, axis=1), jnp.sum(key_raw * key_raw, axis=1)), NARROW
    )
    query_scale = lax.rsqrt(square_query / model_width + EPS)[:, None]
    key_scale = lax.rsqrt(square_key / model_width + EPS)[:, None]
    query_gain = norm_query.astype(F32)
    key_gain = norm_key.astype(F32)
    cosines, sine_table = rope_tables(length, HD)
    query_normed = query_raw * query_scale * query_gain
    key_normed = key_raw * key_scale * key_gain

    def rotate_both(query_in, key_in):
        return (
            rotate_half(query_in.reshape(length, heads_here, HD), cosines, sine_table),
            rotate_half(key_in.reshape(length, heads_here, HD), cosines, sine_table),
        )

    (query_rot, key_rot), rotate_pull = jax.vjp(rotate_both, query_normed, key_normed)
    query_bf = query_rot.astype(BF)
    key_bf = key_rot.astype(BF)
    value_bf = value_raw.astype(BF).reshape(length, heads_here, HD)
    seq_blocks = block_ids[0]

    def block_scores():
        scores = (
            jnp.einsum("qhd,khd->hqk", query_bf, key_bf, preferred_element_type=F32) * score_scale
        )
        allowed = seq_blocks[None, :] <= seq_blocks[:, None]
        return jnp.where(allowed[None], scores, -1e30)

    scores = block_scores()
    highest = jnp.max(scores, axis=-1, keepdims=True)
    shifted = jnp.exp(scores - highest)
    totals = jnp.sum(shifted, axis=-1, keepdims=True)
    attn_probs = (shifted / totals).astype(BF)
    attended = (
        jnp.einsum("hqk,khd->qhd", attn_probs, value_bf, preferred_element_type=F32)
        .astype(BF)
        .reshape(length, head_cols)
    )
    log_totals = highest + jnp.log(totals)
    out_partial = dot(attended, out_full, ((1,), (1,)))

    first_row = lane_index * rows
    x_rows = lax.dynamic_slice_in_dim(rows_full, first_row, rows, 0).astype(F32)
    residual = x_rows + sum_four(out_partial)
    ffn_in = rms_scale(residual, ffn_gain).astype(BF)
    x_all = spread(ffn_in)
    logits = jnp.dot(ffn_in, w_router, preferred_element_type=F32)
    gate_probs = jax.nn.softmax(logits, axis=-1)
    routes_rows = lax.dynamic_slice_in_dim(routes, first_row, rows, 0)
    chosen = jnp.any(
        routes_rows[:, :, None] == jnp.arange(experts, dtype=jnp.int32)[None, None, :], axis=1
    )
    own_gate = to_experts(jnp.where(chosen, gate_probs, 0.0))[:, None]

    gate_pre = jnp.dot(x_all, gate_own, preferred_element_type=F32)
    up_pre = jnp.dot(x_all, up_own, preferred_element_type=F32)
    sig = jax.nn.sigmoid(gate_pre)
    hidden = gate_pre * sig * up_pre
    hidden_gated = (own_gate * hidden).astype(BF)
    down_grad = jnp.dot(cot_all, down_own, preferred_element_type=F32)
    own_dots = jnp.sum(hidden * down_grad, axis=1)
    hidden_grad = own_gate * down_grad
    gate_grad = (hidden_grad * up_pre * (sig * (1.0 + gate_pre * (1.0 - sig)))).astype(BF)
    up_grad = (hidden_grad * gate_pre * sig).astype(BF)
    input_partial = dot(gate_grad, gate_own, ((1,), (1,))) + dot(up_grad, up_own, ((1,), (1,)))
    input_sum = collect(input_partial)
    moe_partial = dot(hidden_gated, down_own, ((1,), (1,)))
    moe_sum = collect(moe_partial)
    pair_dots = jnp.where(chosen, to_owners(own_dots, rows), 0.0)

    grad_down = to_slices(dot(cot_all, hidden_gated, ((0,), (0,))), experts)
    grad_gate = to_slices(dot(x_all, gate_grad, ((0,), (0,))), experts)
    grad_up = to_slices(dot(x_all, up_grad, ((0,), (0,))), experts)

    block_rows = (residual + moe_sum).astype(BF)

    def to_features(values):
        parts = jnp.transpose(values.reshape(rows, lanes, head_cols), (1, 0, 2))
        return lax.all_to_all(parts, NARROW, 0, 0, tiled=True).reshape(length, head_cols)

    block_out = to_features(block_rows)

    logit_grad = (
        gate_probs * (pair_dots - jnp.sum(gate_probs * pair_dots, axis=1, keepdims=True))
    ).astype(BF)
    ffn_grad = input_sum + dot(logit_grad, w_router, ((1,), (1,)))
    router_grad = dot(logit_grad, ffn_in, ((0,), (0,)))
    _, ffn_norm_pull = jax.vjp(rms_scale, residual, ffn_gain)
    residual_norm_grad, ffn_gain_grad = ffn_norm_pull(ffn_grad)
    residual_grad = cot_rows.astype(F32) + residual_norm_grad
    out_cot = gather_four(residual_grad.astype(BF), 0)

    attended_grad = (
        jnp.dot(out_cot, out_full, preferred_element_type=F32)
        .astype(BF)
        .reshape(length, heads_here, HD)
    )
    out_term = dot(out_cot, attended, ((0,), (0,)))
    grad_out = lax.psum_scatter(out_term.astype(BF), WIDE, scatter_dimension=0, tiled=True)
    attn_probs = jnp.exp(block_scores() - log_totals)
    prob_grad = jnp.einsum("qhd,khd->hqk", attended_grad, value_bf, preferred_element_type=F32)
    centre = jnp.sum(attn_probs * prob_grad, axis=-1, keepdims=True)
    score_grad = (attn_probs * (prob_grad - centre)).astype(BF)
    query_grad = (
        jnp.einsum("hqk,khd->qhd", score_grad, key_bf, preferred_element_type=F32) * score_scale
    )
    key_grad = (
        jnp.einsum("hqk,qhd->khd", score_grad, query_bf, preferred_element_type=F32) * score_scale
    )
    value_grad = jnp.einsum(
        "hqk,qhd->khd", attn_probs.astype(BF), attended_grad, preferred_element_type=F32
    )
    query_normed_grad, key_normed_grad = rotate_pull((query_grad, key_grad))
    dot_query, dot_key = lax.psum(
        (
            jnp.sum(query_gain * query_normed_grad * query_raw, axis=1),
            jnp.sum(key_gain * key_normed_grad * key_raw, axis=1),
        ),
        NARROW,
    )
    query_pre_grad = (
        query_scale * query_gain * query_normed_grad
        - query_raw * query_scale**3 * dot_query[:, None] / model_width
    )
    key_pre_grad = (
        key_scale * key_gain * key_normed_grad
        - key_raw * key_scale**3 * dot_key[:, None] / model_width
    )
    query_gain_grad = jnp.sum(query_normed_grad * query_raw * query_scale, axis=0)
    key_gain_grad = jnp.sum(key_normed_grad * key_raw * key_scale, axis=0)
    qkv_grad = jnp.concatenate(
        [
            query_pre_grad.astype(BF),
            key_pre_grad.astype(BF),
            value_grad.reshape(length, head_cols).astype(BF),
        ],
        axis=1,
    )
    normed_grad = sum_four(dot(qkv_grad, qkv_full, ((1,), (1,))))
    qkv_term = dot(normed, qkv_grad, ((0,), (0,)))
    grad_qkv = lax.psum_scatter(qkv_term.astype(BF), WIDE, scatter_dimension=0, tiled=True)
    grad_query = grad_qkv[:, :head_cols]
    grad_key = grad_qkv[:, head_cols : 2 * head_cols]
    grad_value = grad_qkv[:, 2 * head_cols :]
    _, attn_norm_pull = jax.vjp(rms_scale, x_rows, attn_gain)
    rows_norm_grad, attn_gain_grad = attn_norm_pull(normed_grad)
    grad_tokens = to_features(residual_grad + rows_norm_grad)

    place = (jnp.arange(lanes) == lane_index).astype(F32)[:, None]
    small = jnp.concatenate(
        [
            router_grad,
            attn_gain_grad[None],
            ffn_gain_grad[None],
            (place * query_gain_grad[None]).reshape(1, model_width),
            (place * key_gain_grad[None]).reshape(1, model_width),
        ],
        axis=0,
    )
    small = lax.psum(small, ALL)
    grad_router = small[:experts].T
    four = lax.dynamic_slice_in_dim(small[experts:], lane_index * head_cols, head_cols, 1)
    return (
        block_out,
        grad_tokens,
        four[0],
        grad_query.astype(F32),
        grad_key.astype(F32),
        grad_value.astype(F32),
        four[2],
        four[3],
        grad_out.astype(F32),
        four[1],
        grad_router,
        grad_gate,
        grad_up,
        grad_down,
    )


def solution(mesh):
    wide, narrow = mesh.shape["wide"], mesh.shape["narrow"]
    near = 2
    middle = min(wide // near, 4)
    inner = Mesh(mesh.devices.reshape(wide // (near * middle), middle, near, narrow // 2, 2), ALL)
    both = P(WIDE, NARROW)
    cube = P(WIDE, None, NARROW)
    lane = P(NARROW)
    row = P(WIDE, None)
    return jax.shard_map(
        per_device,
        mesh=inner,
        in_specs=(
            both, both, row, row, lane, both, both, both, lane, lane, both, lane, P(),
            cube, cube, cube,
        ),
        out_specs=(
            both, both, lane, both, both, both, lane, lane, both, lane, P(), cube, cube, cube,
        ),
        check_vma=False,
    )
```

```python
import functools

import jax
import jax.numpy as jnp
from jax import lax
from jax.experimental import pallas as pl
from jax.experimental.pallas import tpu as pltpu
from jax.sharding import Mesh
from jax.sharding import PartitionSpec as P

HD = 128
EPS = 1e-05
WIDE = ("t", "g", "p")
NARROW = ("y", "c")
GROUP = ("g", "p", "c")
ALL = ("t", "g", "p", "y", "c")
BF = jnp.bfloat16
F32 = jnp.float32
ROWS = 512
COLS = 256
COST = pl.CostEstimate(flops=1000, transcendentals=0, bytes_accessed=1000)


def rms_scale(values, scales):
    return values * lax.rsqrt(jnp.mean(values * values, axis=-1, keepdims=True) + EPS) * scales


def rope_tables(length, head_dim):
    exponent = jnp.arange(0, head_dim, 2, dtype=F32) / head_dim
    angles = jnp.arange(length, dtype=F32)[:, None] * (10000.0 ** (-exponent))[None, :]
    cosines, sines = jnp.cos(angles), jnp.sin(angles)
    return (
        jnp.concatenate([cosines, cosines], axis=-1),
        jnp.concatenate([-sines, sines], axis=-1),
    )


def dot(a, b, contract):
    return lax.dot_general(a, b, (contract, ((), ())), preferred_element_type=F32)


def call(body, outs, scratch, args, flops, vmem, moved):
    return pl.pallas_call(
        body,
        out_shape=outs,
        in_specs=[pl.BlockSpec(memory_space=pl.ANY)] * len(args),
        out_specs=jax.tree.map(lambda _: pl.BlockSpec(memory_space=pl.ANY), outs),
        scratch_shapes=scratch,
        compiler_params=pltpu.CompilerParams(vmem_limit_bytes=vmem << 20),
        cost_estimate=COST,
    )(*args)


def start_all(copies):
    for one in copies:
        one.start()
    return copies


def wait_all(copies):
    for one in copies:
        one.wait()


def weight_copies(pieces, whole, sems):
    units = whole.shape[2] // 4
    copies = []
    for half, piece in enumerate(pieces):
        for c in range(2):
            k = half * 2 + c
            copies.append(
                pltpu.make_async_copy(
                    piece.at[:, c], whole.at[:, :, pl.ds(k * units, units)], sems.at[k]
                )
            )
    return copies


def block_copies(blocks, whole, sems):
    rows = blocks[0].shape[0]
    return [
        pltpu.make_async_copy(b, whole.at[pl.ds(i * rows, rows)], sems.at[i])
        for i, b in enumerate(blocks)
    ]


def arrived(view, sem):
    pltpu.make_async_copy(view, view, sem).wait()


def await_weight(whole, sems, k, now):
    units = whole.shape[2] // 4

    @pl.when(now)
    def _():
        arrived(whole.at[:, :, pl.ds(pl.multiple_of(k * units, units), units)], sems.at[k])


def await_rows(whole, sems, count, r):
    rows = whole.shape[0] // count
    each = max(1, ROWS // rows)
    if rows <= ROWS:
        for i in range(each):
            b = r * each + i
            arrived(whole.at[pl.ds(pl.multiple_of(b * rows, rows), rows)], sems.at[b])
    else:

        @pl.when(r % (rows // ROWS) == 0)
        def _():
            b = r // (rows // ROWS)
            arrived(whole.at[pl.ds(pl.multiple_of(b * rows, rows), rows)], sems.at[b])


def to_column(line):
    return jnp.transpose(jnp.broadcast_to(line, (128, 128)))


def to_line(column):
    return jnp.transpose(jnp.broadcast_to(column, (128, 128)))[:1]


def take(ref, k):
    part = ref[:, :, pl.ds(pl.multiple_of(k * COLS, COLS), COLS)]
    return part.reshape(-1, COLS)


def take_rows(ref, n):
    each = COLS // ref.shape[1]
    return ref[pl.ds(n * each, each)].reshape(COLS, ref.shape[2])


def project_body(count, *refs):
    blocks, pieces, out = refs[:count], refs[count : count + 2], refs[count + 2]
    rows_v, weight_v, out_v, sem_b, sem_w, sem_o = refs[count + 3 :]
    cw = weight_copies(pieces, weight_v, sem_w)
    cb = block_copies(blocks, rows_v, sem_b)
    ahead = max(1, count * ROWS // rows_v.shape[0])
    start_all(cb[:ahead] + cw + cb[ahead:])
    steps = rows_v.shape[0] // ROWS

    def row_step(r, carry):
        here = pl.ds(pl.multiple_of(r * ROWS, ROWS), ROWS)
        await_rows(rows_v, sem_b, count, r)

        def col_step(k, carry):
            await_weight(weight_v, sem_w, k, r == 0)
            cols = pl.ds(pl.multiple_of(k * COLS, COLS), COLS)
            out_v[here, cols] = dot(rows_v[here, :], take(weight_v, k), ((1,), (0,))).astype(BF)
            return carry

        lax.fori_loop(0, out_v.shape[1] // COLS, col_step, 0)
        pltpu.make_async_copy(out_v.at[here], out.at[here], sem_o.at[r]).start()
        return carry

    lax.fori_loop(0, steps, row_step, 0)
    for r in range(steps):
        here = pl.ds(r * ROWS, ROWS)
        pltpu.make_async_copy(out_v.at[here], out.at[here], sem_o.at[r]).wait()


def project(blocks, got, other):
    rows = blocks[0].shape[0] * len(blocks)
    model = blocks[0].shape[1]
    w, _, depth, units = got.shape
    hidden = 4 * units
    return call(
        functools.partial(project_body, len(blocks)),
        jax.ShapeDtypeStruct((rows, hidden), BF),
        [
            pltpu.VMEM((rows, model), BF),
            pltpu.VMEM((w, depth, hidden), BF),
            pltpu.VMEM((rows, hidden), BF),
            pltpu.SemaphoreType.DMA((len(blocks),)),
            pltpu.SemaphoreType.DMA((4,)),
            pltpu.SemaphoreType.DMA((rows // ROWS,)),
        ],
        (*blocks, got, other),
        2 * rows * model * hidden,
        40,
        2 * (rows * model + model * hidden + rows * hidden),
    )


def expert_body(count, *refs):
    blocks = refs[:count]
    gate_p, up_p = refs[count : count + 2], refs[count + 2 : count + 4]
    down_grad, own_gate = refs[count + 4 : count + 6]
    gg, ug, hs, dots = refs[count + 6 : count + 10]
    (rows_v, gate_v, up_v, grad_v, own_v, gg_v, ug_v, hs_v, dots_v, sem_b, sem_w, sem_i, sem_o) = (
        refs[count + 10 :]
    )
    ci = start_all(
        [
            pltpu.make_async_copy(down_grad, grad_v, sem_i.at[0]),
            pltpu.make_async_copy(own_gate, own_v, sem_i.at[1]),
        ]
    )
    cg = weight_copies(gate_p, gate_v, sem_w.at[0])
    cu = weight_copies(up_p, up_v, sem_w.at[1])
    cb = block_copies(blocks, rows_v, sem_b)
    ahead = max(1, count * ROWS // rows_v.shape[0])
    start_all(cb[:ahead] + [c for two in zip(cg, cu) for c in two] + cb[ahead:])
    wait_all(ci)
    steps = rows_v.shape[0] // ROWS
    lines = ROWS // 128
    outs = ((gg_v, gg, 0), (ug_v, ug, 1), (hs_v, hs, 2))

    def row_step(r, carry):
        here = pl.ds(pl.multiple_of(r * ROWS, ROWS), ROWS)
        await_rows(rows_v, sem_b, count, r)
        mine = own_v[pl.ds(pl.multiple_of(r * lines, lines), lines), :]
        own = jnp.concatenate([to_column(mine[i : i + 1])[:, :1] for i in range(lines)], axis=0)

        def col_step(k, total):
            await_weight(gate_v, sem_w.at[0], k, r == 0)
            await_weight(up_v, sem_w.at[1], k, r == 0)
            cols = pl.ds(pl.multiple_of(k * COLS, COLS), COLS)
            x = rows_v[here, :]
            gate = dot(x, take(gate_v, k), ((1,), (0,)))
            up = dot(x, take(up_v, k), ((1,), (0,)))
            grad = grad_v[here, cols].astype(F32)
            sig = 1.0 / (1.0 + jnp.exp(-gate))
            act = gate * sig
            hidden = act * up
            total = total + jnp.sum(hidden * grad, axis=1, keepdims=True)
            hs_v[here, cols] = (own * hidden).astype(BF)
            grad = own * grad
            gg_v[here, cols] = (grad * up * (sig + act * (1.0 - sig))).astype(BF)
            ug_v[here, cols] = (grad * act).astype(BF)
            return total

        total = lax.fori_loop(
            0, gg_v.shape[1] // COLS, col_step, jnp.zeros((ROWS, 1), F32)
        )
        dots_v[pl.ds(pl.multiple_of(r * lines, lines), lines), :] = jnp.concatenate(
            [to_line(total[i * 128 : (i + 1) * 128]) for i in range(lines)], axis=0
        )
        for src, dst, i in outs:
            pltpu.make_async_copy(src.at[here], dst.at[here], sem_o.at[i, r]).start()
        return carry

    lax.fori_loop(0, steps, row_step, 0)
    last = pltpu.make_async_copy(dots_v, dots, sem_i.at[2])
    last.start()
    for r in range(steps):
        here = pl.ds(r * ROWS, ROWS)
        for src, dst, i in outs:
            pltpu.make_async_copy(src.at[here], dst.at[here], sem_o.at[i, r]).wait()
    last.wait()


def expert(blocks, gate_p, up_p, down_grad, own_gate):
    rows = blocks[0].shape[0] * len(blocks)
    model = blocks[0].shape[1]
    w, _, depth, units = gate_p[0].shape
    hidden = 4 * units
    steps = rows // ROWS
    out = jax.ShapeDtypeStruct((rows, hidden), BF)
    wide = jax.ShapeDtypeStruct(own_gate.shape, F32)
    return call(
        functools.partial(expert_body, len(blocks)),
        (out, out, out, wide),
        [
            pltpu.VMEM((rows, model), BF),
            pltpu.VMEM((w, depth, hidden), BF),
            pltpu.VMEM((w, depth, hidden), BF),
            pltpu.VMEM((rows, hidden), BF),
            pltpu.VMEM(own_gate.shape, F32),
            pltpu.VMEM((rows, hidden), BF),
            pltpu.VMEM((rows, hidden), BF),
            pltpu.VMEM((rows, hidden), BF),
            pltpu.VMEM(own_gate.shape, F32),
            pltpu.SemaphoreType.DMA((len(blocks),)),
            pltpu.SemaphoreType.DMA((2, 4)),
            pltpu.SemaphoreType.DMA((3,)),
            pltpu.SemaphoreType.DMA((3, steps)),
        ],
        (*blocks, *gate_p, *up_p, down_grad, own_gate),
        4 * rows * model * hidden,
        56,
        2 * (rows * model + 2 * model * hidden + 4 * rows * hidden),
    )


def back_body(first, pairs, tail, *refs):
    refs = list(refs)
    ins = [refs[3 * i : 3 * i + 3] for i in range(pairs)]
    at = 3 * pairs
    if tail:
        dots, place = refs[at : at + 2]
        at += 2
    out = refs[at]
    scratch = refs[at + 1 :]
    if tail:
        dots_v, place_v, sem_t = scratch[-3:]
        scratch = scratch[:-3]
        side = start_all(
            [
                pltpu.make_async_copy(dots, dots_v, sem_t.at[0]),
                pltpu.make_async_copy(place, place_v, sem_t.at[1]),
            ]
        )
    grads, weights = scratch[:pairs], scratch[pairs : 2 * pairs]
    out_v, sem_g, sem_w, sem_o = scratch[2 * pairs :]
    rows = out_v.shape[0]
    steps = rows // ROWS
    each = COLS // weights[0].shape[1]
    parts = weights[0].shape[0] // each
    for i, (grad, got, other) in enumerate(ins):
        pltpu.make_async_copy(grad.at[pl.ds(first, ROWS)], grads[i].at[pl.ds(0, ROWS)], sem_g.at[i, 0]).start()
    for n in range(parts):
        place = pl.ds(n * each, each)
        for i, (grad, got, other) in enumerate(ins):
            start_all(weight_copies((got.at[place], other.at[place]), weights[i].at[place], sem_w.at[i, n]))
    for r in range(1, steps):
        for i, (grad, got, other) in enumerate(ins):
            here = pl.ds(r * ROWS, ROWS)
            pltpu.make_async_copy(grad.at[pl.ds(first + r * ROWS, ROWS)], grads[i].at[here], sem_g.at[i, r]).start()

    def row_step(r, carry):
        here = pl.ds(pl.multiple_of(r * ROWS, ROWS), ROWS)
        for i in range(pairs):
            arrived(grads[i].at[here], sem_g.at[i, r])

        def col_step(n, carry):
            for i in range(pairs):
                place = weights[i].at[pl.ds(n * each, each)]
                for k in range(4):
                    await_weight(place, sem_w.at[i, n], k, r == 0)
            cols = pl.ds(pl.multiple_of(n * COLS, COLS), COLS)
            total = dot(grads[0][here, :], take_rows(weights[0], n), ((1,), (1,)))
            for i in range(1, pairs):
                total += dot(grads[i][here, :], take_rows(weights[i], n), ((1,), (1,)))
            out_v[here, cols] = total.astype(BF)
            return carry

        lax.fori_loop(0, parts, col_step, 0)
        pltpu.make_async_copy(out_v.at[here], out.at[here], sem_o.at[r]).start()
        return carry

    if tail:
        wait_all(side)
        for i in range(rows // 128):
            line = dots_v[first // 128 + i : first // 128 + i + 1, :]
            out_v[i * 128 : (i + 1) * 128, parts * COLS :] = (to_column(line) * place_v[...]).astype(BF)
    lax.fori_loop(0, steps, row_step, 0)
    for r in range(steps):
        here = pl.ds(r * ROWS, ROWS)
        pltpu.make_async_copy(out_v.at[here], out.at[here], sem_o.at[r]).wait()


def back(triples, first, rows, tail=()):
    w, _, depth, units = triples[0][1].shape
    model, hidden = w * depth, 4 * units
    n = len(triples)
    full = model + 128 if tail else model
    return call(
        functools.partial(back_body, first, n, bool(tail)),
        jax.ShapeDtypeStruct((rows, full), BF),
        [pltpu.VMEM((rows, hidden), BF)] * n
        + [pltpu.VMEM((w, depth, hidden), BF)] * n
        + [
            pltpu.VMEM((rows, full), BF),
            pltpu.SemaphoreType.DMA((n, rows // ROWS)),
            pltpu.SemaphoreType.DMA((n, model // COLS, 4)),
            pltpu.SemaphoreType.DMA((rows // ROWS,)),
        ]
        + [pltpu.VMEM(t.shape, F32) for t in tail]
        + [pltpu.SemaphoreType.DMA((2,))] * bool(tail),
        [a for t in triples for a in t] + list(tail),
        2 * n * rows * model * hidden,
        40,
        2 * (n * rows * hidden + n * model * hidden + rows * model),
    )


def weight_body(count, depth, *refs):
    blocks, grad, mine, theirs = refs[:count], refs[count], refs[count + 1], refs[count + 2]
    rows_v, grad_v, out_v, sem_b, sem_g, sem_o = refs[count + 3 :]
    cg = pltpu.make_async_copy(grad, grad_v, sem_g.at[0])
    wait_all(start_all(block_copies(blocks, rows_v, sem_b) + [cg]))
    units = COLS
    each = COLS // depth
    steps = rows_v.shape[1] // COLS

    def step(n, carry):
        cols = pl.ds(pl.multiple_of(n * COLS, COLS), COLS)
        got = dot(rows_v[:, cols], grad_v[...], ((0,), (0,))).astype(BF)
        for k in range(4):
            part = got[:, k * units : (k + 1) * units].reshape(each, depth, units)
            out_v[k // 2, pl.ds(n * each, each), k % 2] = part
        place = pl.ds(n * each, each)
        pltpu.make_async_copy(out_v.at[0, place], mine.at[place], sem_o.at[0, n]).start()
        pltpu.make_async_copy(out_v.at[1, place], theirs.at[place], sem_o.at[1, n]).start()
        return carry

    lax.fori_loop(0, steps, step, 0)
    for n in range(steps):
        place = pl.ds(n * each, each)
        pltpu.make_async_copy(out_v.at[0, place], mine.at[place], sem_o.at[0, n]).wait()
        pltpu.make_async_copy(out_v.at[1, place], theirs.at[place], sem_o.at[1, n]).wait()


def weight_grad(blocks, grad, depth):
    rows = blocks[0].shape[0] * len(blocks)
    model = blocks[0].shape[1]
    hidden = grad.shape[1]
    w = model // depth
    piece = jax.ShapeDtypeStruct((w, 2, depth, hidden // 4), BF)
    steps = model // COLS
    return call(
        functools.partial(weight_body, len(blocks), depth),
        (piece, piece),
        [
            pltpu.VMEM((rows, model), BF),
            pltpu.VMEM((rows, hidden), BF),
            pltpu.VMEM((2, w, 2, depth, hidden // 4), BF),
            pltpu.SemaphoreType.DMA((len(blocks),)),
            pltpu.SemaphoreType.DMA((1,)),
            pltpu.SemaphoreType.DMA((2, steps)),
        ],
        (*blocks, grad),
        2 * rows * model * hidden,
        40,
        2 * (rows * model + model * hidden + rows * hidden),
    )


def terms_body(pairs, *refs):
    ins, me, outs = refs[: 2 * pairs], refs[2 * pairs], refs[2 * pairs + 1 : 2 * pairs + 3]
    scratch = refs[2 * pairs + 3 :]
    held, out_v, sems, out_sem = scratch[: 2 * pairs], scratch[-3], scratch[-2], scratch[-1]
    wait_all(
        start_all(
            [pltpu.make_async_copy(ins[i], held[i], sems.at[i]) for i in range(2 * pairs)]
        )
    )
    _, count, _, depth, _ = out_v.shape
    mine = me[0]

    each = COLS // depth

    def step(n, carry):
        rows = pl.ds(pl.multiple_of(n * COLS, COLS), COLS)
        at = 0
        for i in range(pairs):
            wide = held[2 * i + 1].shape[1]
            got = dot(held[2 * i][:, rows], held[2 * i + 1][...], ((0,), (0,))).astype(BF)
            for j in range(each):
                b = n * each + j
                distance = jnp.bitwise_xor(b % 8, mine)
                half = distance % 2
                far = distance // 2
                place = (far % 2) * 2 + far // 2
                out_v[half, b // 8, place, :, at : at + wide] = got[j * depth : (j + 1) * depth]
            at += wide
        return carry

    lax.fori_loop(0, count * 8 // each, step, 0)
    wait_all(
        start_all([pltpu.make_async_copy(out_v.at[i], outs[i], out_sem.at[i]) for i in range(2)])
    )


def block_terms(pairs, me, depth):
    length, model = pairs[0][0].shape
    count = model // (8 * depth)
    n = sum(c.shape[1] for _, c in pairs)
    piece = jax.ShapeDtypeStruct((count, 4, depth, n), BF)
    flat = [x for two in pairs for x in two]
    return pl.pallas_call(
        functools.partial(terms_body, len(pairs)),
        out_shape=(piece, piece),
        in_specs=[pl.BlockSpec(memory_space=pl.ANY)] * len(flat)
        + [pl.BlockSpec(memory_space=pltpu.SMEM)],
        out_specs=(pl.BlockSpec(memory_space=pl.ANY),) * 2,
        scratch_shapes=[pltpu.VMEM(x.shape, BF) for x in flat]
        + [
            pltpu.VMEM((2,) + piece.shape, BF),
            pltpu.SemaphoreType.DMA((len(flat),)),
            pltpu.SemaphoreType.DMA((2,)),
        ],
        compiler_params=pltpu.CompilerParams(vmem_limit_bytes=24 << 20),
        cost_estimate=COST,
    )(*flat, me)


def to_columns(line):
    return jnp.concatenate(
        [to_column(line[:, i : i + 128])[:, :1] for i in range(0, line.shape[1], 128)], axis=0
    )


def to_lines(column):
    return jnp.concatenate(
        [to_line(column[i : i + 128]) for i in range(0, column.shape[0], 128)], axis=1
    )


def bring(ins, held, sems):
    wait_all(
        start_all([pltpu.make_async_copy(a, b, sems.at[i]) for i, (a, b) in enumerate(zip(ins, held))])
    )


def send_out(held, outs, sems):
    wait_all(
        start_all([pltpu.make_async_copy(a, b, sems.at[i]) for i, (a, b) in enumerate(zip(held, outs))])
    )


def raw_body(normed, weights, query, key, value, squares, *scratch):
    normed_v, weights_v, query_v, key_v, value_v, squares_v, sem_i, sem_o = scratch
    wide = query_v.shape[1]
    bring((normed, weights.at[:, pl.ds(0, 3 * wide)]), (normed_v, weights_v), sem_i)
    length = query_v.shape[0]
    for place, ref in ((0, query_v), (1, key_v)):

        def step(j, total):
            cols = pl.ds(pl.multiple_of(j * COLS, COLS), COLS)
            w = weights_v[:, pl.ds(pl.multiple_of(place * wide + j * COLS, COLS), COLS)]
            got = dot(normed_v[...], w, ((1,), (0,)))
            ref[:, cols] = got
            return total + jnp.sum(got * got, axis=1, keepdims=True)

        total = lax.fori_loop(0, wide // COLS, step, jnp.zeros((length, 1), F32))
        squares_v[place : place + 1, :] = to_lines(total)

    def step(j, carry):
        cols = pl.ds(pl.multiple_of(j * COLS, COLS), COLS)
        w = weights_v[:, pl.ds(pl.multiple_of(2 * wide + j * COLS, COLS), COLS)]
        value_v[:, cols] = dot(normed_v[...], w, ((1,), (0,))).astype(BF)
        return carry

    lax.fori_loop(0, wide // COLS, step, 0)
    send_out((query_v, key_v, value_v, squares_v), (query, key, value, squares), sem_o)


def raw_heads(normed, weights, wide):
    length, model = normed.shape
    shapes = [((length, wide), F32), ((length, wide), F32), ((length, wide), BF), ((2, length), F32)]
    return call(
        raw_body,
        tuple(jax.ShapeDtypeStruct(*one) for one in shapes),
        [pltpu.VMEM((length, model), BF), pltpu.VMEM((model, 3 * wide), BF)]
        + [pltpu.VMEM(*one) for one in shapes]
        + [pltpu.SemaphoreType.DMA((2,)), pltpu.SemaphoreType.DMA((4,))],
        (normed, weights),
        0,
        32,
        0,
    )


def half_turn(values):
    return pltpu.roll(values, HD // 2, 1)


def attend_body(*refs):
    ins, outs, scratch = refs[:10], refs[10:15], refs[15:]
    held, made, sem_i, sem_o = scratch[:10], scratch[10:15], scratch[15], scratch[16]
    query, key, value, scales, gains, cosines, sines, ids, weights = ins[:9]
    wide = query.shape[1]
    views = list(ins[:9])
    views[8] = weights.at[:, pl.ds(3 * wide, wide)]
    bring(views, held[:9], sem_i)
    query_v, key_v, value_v, scales_v, gains_v, cos_v, sin_v, ids_v, weights_v = held[:9]
    query_o, key_o, attended_o, log_o, out_o = made
    line = ids_v[...]
    allowed = line <= to_columns(line)
    scale_q, scale_k = to_columns(scales_v[0:1, :]), to_columns(scales_v[1:2, :])

    def step(h, carry):
        cols = pl.ds(pl.multiple_of(h * HD, HD), HD)
        cosines, sines = cos_v[...], sin_v[...]
        q = query_v[:, cols] * scale_q * gains_v[0:1, cols]
        k = key_v[:, cols] * scale_k * gains_v[1:2, cols]
        q = (q * cosines + half_turn(q) * sines).astype(BF)
        k = (k * cosines + half_turn(k) * sines).astype(BF)
        query_o[:, cols] = q
        key_o[:, cols] = k
        scores = jnp.where(allowed, dot(q, k, ((1,), (1,))) * HD**-0.5, -1e30)
        highest = jnp.max(scores, axis=1, keepdims=True)
        shifted = jnp.exp(scores - highest)
        totals = jnp.sum(shifted, axis=1, keepdims=True)
        probs = (shifted / totals).astype(BF)
        attended_o[:, cols] = dot(probs, value_v[:, cols], ((1,), (0,))).astype(BF)
        log_o[pl.ds(h, 1), :] = to_lines(highest + jnp.log(totals))
        return carry

    lax.fori_loop(0, wide // HD, step, 0)

    def out_step(j, carry):
        cols = pl.ds(pl.multiple_of(j * COLS, COLS), COLS)
        out_o[:, cols] = dot(attended_o[...], weights_v[cols, :], ((1,), (1,))).astype(BF)
        return carry

    lax.fori_loop(0, out_o.shape[1] // COLS, out_step, 0)
    send_out(made, outs, sem_o)


def attend(query, key, value, scales, gains, tables, ids, weights):
    length, wide = query.shape
    model = weights.shape[0]
    args = (query, key, value, scales, gains, *tables, ids, weights, ids)
    held = [pltpu.VMEM(x.shape, x.dtype) for x in args[:8]]
    held += [pltpu.VMEM((model, wide), BF), pltpu.VMEM(ids.shape, ids.dtype)]
    shapes = [
        ((length, wide), BF),
        ((length, wide), BF),
        ((length, wide), BF),
        ((wide // HD, length), F32),
        ((length, model), BF),
    ]
    return call(
        attend_body,
        tuple(jax.ShapeDtypeStruct(*one) for one in shapes),
        held
        + [pltpu.VMEM(*one) for one in shapes]
        + [pltpu.SemaphoreType.DMA((9,)), pltpu.SemaphoreType.DMA((5,))],
        args,
        0,
        32,
        0,
    )


def unattend_body(*refs):
    ins, outs, scratch = refs[:12], refs[12:16], refs[16:]
    held, grad_v, made, sem_i, sem_o = (
        scratch[:12], scratch[12], scratch[13:17], scratch[17], scratch[18],
    )
    wide = ins[2].shape[1]
    views = list(ins)
    views[1] = ins[1].at[:, pl.ds(3 * wide, wide)]
    bring(views, held, sem_i)
    cot_v, weights_v, query_v, key_v, value_v, log_v, ids_v, cos_v, sin_v, gains_v, raw_q, raw_k = held
    query_o, key_o, value_o, dots_o = made
    grad_v[...] = dot(cot_v[...], weights_v[...], ((1,), (0,))).astype(BF)
    line = ids_v[...]
    allowed = line <= to_columns(line)
    length = cot_v.shape[0]
    zero = jnp.zeros((length, 1), F32)

    def step(h, carry):
        dot_q, dot_k = carry
        cols = pl.ds(pl.multiple_of(h * HD, HD), HD)
        cosines, sines = cos_v[...], sin_v[...]
        q, k, v, grad = query_v[:, cols], key_v[:, cols], value_v[:, cols], grad_v[:, cols]
        scores = jnp.where(allowed, dot(q, k, ((1,), (1,))) * HD**-0.5, -1e30)
        probs = jnp.exp(scores - to_columns(log_v[pl.ds(h, 1), :]))
        prob_grad = dot(grad, v, ((1,), (1,)))
        centre = jnp.sum(probs * prob_grad, axis=1, keepdims=True)
        score_grad = (probs * (prob_grad - centre)).astype(BF)
        value_o[:, cols] = dot(probs.astype(BF), grad, ((0,), (0,))).astype(BF)
        back_q = dot(score_grad, k, ((1,), (0,))) * HD**-0.5
        back_k = dot(score_grad, q, ((0,), (0,))) * HD**-0.5
        back_q = back_q * cosines + half_turn(back_q * sines)
        back_k = back_k * cosines + half_turn(back_k * sines)
        query_o[:, cols] = back_q
        key_o[:, cols] = back_k
        dot_q += jnp.sum(gains_v[0:1, cols] * back_q * raw_q[:, cols], axis=1, keepdims=True)
        dot_k += jnp.sum(gains_v[1:2, cols] * back_k * raw_k[:, cols], axis=1, keepdims=True)
        return dot_q, dot_k

    dot_q, dot_k = lax.fori_loop(0, wide // HD, step, (zero, zero))
    dots_o[0:1, :] = to_lines(dot_q)
    dots_o[1:2, :] = to_lines(dot_k)
    send_out(made, outs, sem_o)


def unattend(out_cot, weights, query, key, value, logs, ids, tables, gains, raw_q, raw_k):
    length, wide = query.shape
    args = (out_cot, weights, query, key, value, logs, ids, *tables, gains, raw_q, raw_k)
    held = [pltpu.VMEM(x.shape, x.dtype) for x in args]
    held[1] = pltpu.VMEM((weights.shape[0], wide), BF)
    shapes = [((length, wide), F32), ((length, wide), F32), ((length, wide), BF), ((2, length), F32)]
    return call(
        unattend_body,
        tuple(jax.ShapeDtypeStruct(*one) for one in shapes),
        held
        + [pltpu.VMEM((length, wide), BF)]
        + [pltpu.VMEM(*one) for one in shapes]
        + [pltpu.SemaphoreType.DMA((12,)), pltpu.SemaphoreType.DMA((4,))],
        args,
        0,
        40,
        0,
    )


def unnorm_body(*refs):
    ins, outs, scratch = refs[:7], refs[7:9], refs[9:]
    held, made, sem_i, sem_o = scratch[:7], scratch[7:9], scratch[9], scratch[10]
    bring(ins, held, sem_i)
    back_q, back_k, raw_q, raw_k, scales_v, dots_v, gains_v = held
    grads_o, gains_o = made
    wide = raw_q.shape[1]
    for i, (back, raw) in enumerate(((back_q, raw_q), (back_k, raw_k))):
        scale = to_columns(scales_v[i : i + 1, :])
        push = to_columns(dots_v[i : i + 1, :]) * scale * scale * scale
        grad = scale * gains_v[i : i + 1, :] * back[...] - raw[...] * push
        grads_o[:, i * wide : (i + 1) * wide] = grad.astype(BF)
        gains_o[i : i + 1, :] = jnp.sum(back[...] * raw[...] * scale, axis=0, keepdims=True)
    send_out(made, outs, sem_o)


def unnorm(back_q, back_k, raw_q, raw_k, scales, dots, gains):
    length, wide = raw_q.shape
    args = (back_q, back_k, raw_q, raw_k, scales, dots, gains)
    shapes = [((length, 2 * wide), BF), ((2, wide), F32)]
    return call(
        unnorm_body,
        tuple(jax.ShapeDtypeStruct(*one) for one in shapes),
        [pltpu.VMEM(x.shape, x.dtype) for x in args]
        + [pltpu.VMEM(*one) for one in shapes]
        + [pltpu.SemaphoreType.DMA((7,)), pltpu.SemaphoreType.DMA((2,))],
        args,
        0,
        24,
        0,
    )


def after(values, *earlier):
    return lax.optimization_barrier((values, earlier))[0]


def stage(*values):
    return lax.optimization_barrier(values)


def swap(values, axis, step=1):
    count = lax.axis_size(axis)
    return lax.ppermute(values, axis, [(i, i ^ step) for i in range(count)])


def gather_four(block, axis):
    count = lax.axis_size("y") * lax.axis_size("c")
    size = block.shape[axis]
    here = lax.axis_index("y") * lax.axis_size("c") + lax.axis_index("c")
    other = swap(block, "y")
    near = swap(block, "c")
    far = swap(other, "c")
    shape = list(block.shape)
    shape[axis] = size * count
    whole = jnp.zeros(shape, block.dtype)
    for piece, place in ((block, 0), (near, 1), (other, 2), (far, 3)):
        whole = lax.dynamic_update_slice_in_dim(whole, piece, (here ^ place) * size, axis)
    return whole


def sum_near(partial):
    length, width = partial.shape
    y, c = lax.axis_index("y"), lax.axis_index("c")
    parts = partial.reshape(2, 2, length // 4, width)
    mine = lax.dynamic_index_in_dim(parts, c, 1, False)
    theirs = lax.dynamic_index_in_dim(parts, 1 - c, 1, False)
    mine = mine.astype(F32) + swap(theirs.astype(BF), "c").astype(F32)
    keep = lax.dynamic_index_in_dim(mine, y, 0, False)
    send = lax.dynamic_index_in_dim(mine, 1 - y, 0, False)
    return keep, send.astype(BF)


def add(*pieces):
    total = pieces[0].astype(F32)
    for piece in pieces[1:]:
        total = total + piece.astype(F32)
    return total


def to_experts(columns):
    sent = lax.all_to_all(columns.T, GROUP, 0, 0, tiled=True)
    v = sent.reshape((-1, 2) + sent.shape[1:])
    c = lax.axis_index("c")
    own = lax.dynamic_index_in_dim(v, c, 1, False)
    other = lax.dynamic_index_in_dim(v, 1 - c, 1, False)
    return jnp.concatenate([own, other]).reshape(sent.shape[0], -1)


def to_group(weight):
    got = lax.all_to_all(weight, GROUP, 0, 0, tiled=True)
    return got.reshape((got.shape[0] // 2, 2) + got.shape[1:])


def over_sequences(*terms):
    if lax.axis_size("t") > 1:
        terms = [lax.psum_scatter(x, "t", scatter_dimension=0, tiled=True) for x in terms]
    return [x[0] for x in terms]


def over_groups(piece):
    if lax.axis_size("t") > 1:
        piece = lax.all_gather(piece, "t", axis=0, tiled=True)
    return piece


def sum_over(values, axis):
    step = 1
    while step < lax.axis_size(axis):
        values = values + swap(values, axis, step)
        step *= 2
    return values


def to_slices(mine, theirs):
    total = (mine.astype(F32) + theirs.astype(F32)).astype(BF)
    if lax.axis_size("t") > 1:
        total = lax.psum_scatter(total, "t", scatter_dimension=0, tiled=True)
    sent = total.reshape((-1,) + total.shape[2:])
    return lax.all_to_all(sent, GROUP, 0, 0, tiled=True)


def as_output(got):
    return jnp.transpose(got, (1, 0, 2)).astype(F32)


def per_device(
    tokens,
    cotangent,
    block_ids,
    routes,
    norm_attn,
    w_query,
    w_key,
    w_value,
    norm_query,
    norm_key,
    w_out,
    norm_ffn,
    w_router,
    w_gate,
    w_up,
    w_down,
):
    experts = w_router.shape[1]
    lane_index = lax.axis_index("y") * lax.axis_size("c") + lax.axis_index("c")
    lanes = lax.axis_size("y") * lax.axis_size("c")
    length, head_cols = tokens.shape
    model_width = head_cols * lanes
    rows = length // lanes

    all_full = lax.all_gather(
        jnp.concatenate([w_query, w_key, w_value, w_out], axis=1), WIDE, axis=0, tiled=True
    )

    rows_full = gather_four(tokens, 1)
    gains = lax.all_gather(jnp.stack([norm_attn, norm_ffn]), NARROW, axis=1, tiled=True)
    down_got = to_group(jnp.transpose(w_down, (1, 0, 2)))
    gate_sent = jnp.transpose(w_gate, (1, 0, 2))
    up_sent = jnp.transpose(w_up, (1, 0, 2))
    cot_rows = lax.all_to_all(cotangent.reshape(lanes, rows, head_cols), NARROW, 0, 0, tiled=True)
    cot_rows = jnp.transpose(cot_rows, (1, 0, 2)).reshape(rows, model_width)
    rows_full, cot_rows, gate_sent, up_sent, gains = stage(
        rows_full, cot_rows, gate_sent, up_sent, gains
    )
    attn_gain = gains[0].astype(F32)
    ffn_gain = gains[1].astype(F32)
    rows_float = rows_full.astype(F32)
    normed = rms_scale(rows_float, attn_gain).astype(BF)
    down_got, gate_sent, normed, cot_sent = stage(down_got, gate_sent, normed, cot_rows)

    down_other = swap(down_got, "y")
    all_full, normed, cot_sent, gate_sent, down_other = stage(
        all_full, normed, cot_sent, gate_sent, down_other
    )

    gate_got = to_group(gate_sent)
    cot_mine = lax.all_gather(cot_sent, ("g", "p"), axis=0, tiled=True)
    qkv_full = all_full[:, : 3 * head_cols]
    raw_query, raw_key, value_bf, squares = raw_heads(normed, all_full, head_cols)
    scales = lax.rsqrt(lax.psum(squares, NARROW) / model_width + EPS)
    scales, gate_got, up_sent = stage(scales, gate_got, up_sent)
    up_got = to_group(up_sent)
    cut = gate_got.shape[0] // 2
    gate_first = swap(gate_got[:cut], "y")
    gains_here = jnp.stack([norm_query, norm_key]).astype(F32)
    tables = rope_tables(length, HD)
    ids = block_ids.astype(F32)
    query_bf, key_bf, attended, log_totals, out_partial = attend(
        raw_query, raw_key, value_bf, scales, gains_here, tables, ids, all_full
    )

    first_row = lane_index * rows
    x_rows = lax.dynamic_slice_in_dim(rows_full, first_row, rows, 0).astype(F32)
    keep, send = sum_near(out_partial)
    keep, send, gate_first = stage(keep, send, gate_first)
    residual = x_rows + keep + swap(send, "y").astype(F32)
    ffn_in = rms_scale(residual, ffn_gain).astype(BF)
    ffn_in, up_got, gate_got, cot_mine = stage(ffn_in, up_got, gate_got, cot_mine)

    up_other = swap(up_got, "y")
    gate_last = swap(gate_got[cut:], "y")
    x_mine = lax.all_gather(ffn_in, ("g", "p"), axis=0, tiled=True)
    cot_all = [cot_mine, swap(cot_mine, "c")]
    down_own = (over_groups(down_got), over_groups(down_other))
    down_grad = project(cot_all, *down_own)
    logits = jnp.dot(ffn_in, w_router, preferred_element_type=F32)
    gate_probs = jax.nn.softmax(logits, axis=-1)
    routes_rows = lax.dynamic_slice_in_dim(routes, first_row, rows, 0)
    chosen = jnp.any(
        routes_rows[:, :, None] == jnp.arange(experts, dtype=jnp.int32)[None, None, :], axis=1
    )
    own_gate = to_experts(jnp.where(chosen, gate_probs, 0.0))
    x_mine, down_grad, own_gate, up_other, gate_last = stage(
        x_mine, down_grad, own_gate, up_other, gate_last
    )
    gate_other = jnp.concatenate([gate_first, gate_last])
    x_all = [x_mine, swap(x_mine, "c")]
    gate_own = (over_groups(gate_got), over_groups(gate_other))
    up_own = (over_groups(up_got), over_groups(up_other))

    gate_grad, up_grad, hidden_gated, own_dots = expert(
        x_all, gate_own, up_own, down_grad, own_gate
    )
    half = gate_grad.shape[0] // 2
    own_index = lax.axis_index("g") * 4 + lax.axis_index("p") * 2 + lax.axis_index("c")
    depth = down_own[0].shape[2]
    own_place = (jnp.arange(128) == own_index).astype(F32)[None]
    depth = down_own[0].shape[2]
    pairs = ((gate_grad, *gate_own), (up_grad, *up_own))
    theirs = back(pairs, half, half, (own_dots, own_place))
    gate_grad, up_grad, own_dots, theirs = stage(gate_grad, up_grad, own_dots, theirs)
    pairs = ((gate_grad, *gate_own), (up_grad, *up_own))
    mine = back(pairs, 0, half, (own_dots, own_place))
    sent = add(mine, swap(theirs, "c")).astype(BF)
    sent, hidden_gated, gate_grad, up_grad = stage(sent, hidden_gated, gate_grad, up_grad)

    input_sum = lax.psum_scatter(sent, ("g", "p"), scatter_dimension=0, tiled=True)
    down_mine, down_theirs = weight_grad(cot_all, hidden_gated, depth)
    down_theirs, gate_grad, hidden_gated, up_grad = stage(
        down_theirs, gate_grad, hidden_gated, up_grad
    )
    down_theirs = swap(down_theirs, "y")
    gate_mine, gate_theirs = weight_grad(x_all, gate_grad, depth)
    up_mine, up_theirs = weight_grad(x_all, up_grad, depth)
    moe_pair = ((hidden_gated, *down_own),)
    moe_theirs = back(moe_pair, half, half)
    moe_mine = back(moe_pair, 0, half)
    down_theirs, gate_theirs, up_theirs, moe_theirs, moe_mine = stage(
        down_theirs, gate_theirs, up_theirs, moe_theirs, moe_mine
    )
    gate_theirs = swap(gate_theirs, "y")
    down_got = to_slices(down_mine, down_theirs)
    moe_sent = add(moe_mine, swap(moe_theirs, "c")).astype(BF)
    input_sum, moe_sent, gate_theirs = stage(input_sum, moe_sent, gate_theirs)
    moe_sum = lax.psum_scatter(moe_sent, ("g", "p"), scatter_dimension=0, tiled=True)
    gate_got = to_slices(gate_mine, gate_theirs)
    input_sum = input_sum.astype(F32)
    pair_dots = jnp.where(chosen, input_sum[:, model_width : model_width + experts], 0.0)
    input_sum = input_sum[:, :model_width]

    logit_grad = (
        gate_probs * (pair_dots - jnp.sum(gate_probs * pair_dots, axis=1, keepdims=True))
    ).astype(BF)
    ffn_grad = input_sum + dot(logit_grad, w_router, ((1,), (1,)))
    router_grad = dot(logit_grad, ffn_in, ((0,), (0,)))
    _, ffn_norm_pull = jax.vjp(rms_scale, residual, ffn_gain)
    residual_norm_grad, ffn_gain_grad = ffn_norm_pull(ffn_grad)
    residual_grad = cot_rows.astype(F32) + residual_norm_grad
    out_cot = gather_four(residual_grad.astype(BF), 0)
    out_cot, up_theirs, down_got = stage(out_cot, up_theirs, down_got)

    back_query, back_key, value_grad, dots = unattend(
        out_cot, all_full, query_bf, key_bf, value_bf, log_totals, ids, tables, gains_here,
        raw_query, raw_key,
    )
    group_index = (lax.axis_index("g") * 2 + lax.axis_index("p")).astype(jnp.int32)[None]
    two_keep, two_near = over_sequences(
        *block_terms(((out_cot, attended), (normed, value_grad)), group_index, depth)
    )
    dots, two_near, two_keep = stage(dots, two_near, two_keep)
    two_near = swap(two_near, "p")
    dots = lax.psum(dots, NARROW) / model_width
    dots, up_theirs = stage(dots, up_theirs)

    up_theirs = swap(up_theirs, "y")
    pair_pre, pair_gains = unnorm(
        back_query, back_key, raw_query, raw_key, scales, dots, gains_here
    )
    qkv_grad = jnp.concatenate([pair_pre, value_grad], axis=1)
    pair_keep, pair_near = over_sequences(*block_terms(((normed, pair_pre),), group_index, depth))
    qkv_grad, pair_keep, pair_near = stage(qkv_grad, pair_keep, pair_near)
    pair_near = swap(pair_near, "p")
    keep, send = sum_near(dot(qkv_grad, qkv_full, ((1,), (1,))))
    keep, send, two_near, two_keep, up_theirs, gate_got = stage(
        keep, send, two_near, two_keep, up_theirs, gate_got
    )
    up_got = to_slices(up_mine, up_theirs)
    send = swap(send, "y")
    normed_grad = add(keep, send)
    two_parts = add(two_keep, two_near)
    two_far = swap(two_parts[2:].astype(BF), "g", 1)
    _, attn_norm_pull = jax.vjp(rms_scale, x_rows, attn_gain)
    rows_norm_grad, attn_gain_grad = attn_norm_pull(normed_grad)
    grad_rows = (residual_grad + rows_norm_grad).astype(BF)
    place = (jnp.arange(lanes) == lane_index).astype(F32)[:, None]
    small = jnp.concatenate(
        [
            router_grad,
            attn_gain_grad[None],
            ffn_gain_grad[None],
            (place * pair_gains[:1]).reshape(1, model_width),
            (place * pair_gains[1:]).reshape(1, model_width),
        ],
        axis=0,
    )
    small = sum_over(small, "c")
    small = sum_over(small, "y")
    grad_rows, two_far, two_parts, pair_near, pair_keep, small, moe_sum = stage(
        grad_rows, two_far, two_parts, pair_near, pair_keep, small, moe_sum
    )

    pair_parts = add(pair_keep, pair_near)
    pair_far = swap(pair_parts[2:].astype(BF), "g", 1)
    two_parts = add(two_parts[:2], two_far)
    two_far = swap(two_parts[1].astype(BF), "g", 2)
    small = sum_over(small, "p")
    pair_far, pair_parts, two_far, two_parts, small, up_got, grad_rows, moe_sum = stage(
        pair_far, pair_parts, two_far, two_parts, small, up_got, grad_rows, moe_sum
    )

    pair_parts = add(pair_parts[:2], pair_far)
    pair_far = swap(pair_parts[1].astype(BF), "g", 2)
    small = sum_over(sum_over(small, "g"), "t")
    grad_two = add(two_parts[0], two_far)
    both_rows = jnp.stack([(residual + moe_sum.astype(F32)).astype(BF), grad_rows])
    both_rows = jnp.transpose(both_rows.reshape(2, rows, lanes, head_cols), (2, 0, 1, 3))
    both_rows = lax.all_to_all(both_rows, NARROW, 0, 0, tiled=True)
    block_out = both_rows[:, 0].reshape(length, head_cols)
    grad_tokens = both_rows[:, 1].reshape(length, head_cols).astype(F32)
    grad_gate = as_output(gate_got)
    grad_down = as_output(down_got)
    grad_up = as_output(up_got)
    grad_pair = add(pair_parts[0], pair_far)
    grad_out, grad_value = grad_two[:, :head_cols], grad_two[:, head_cols:]
    grad_query, grad_key = grad_pair[:, :head_cols], grad_pair[:, head_cols:]
    grad_router = small[:experts].T
    four = lax.dynamic_slice_in_dim(small[experts:], lane_index * head_cols, head_cols, 1)
    return (
        block_out,
        grad_tokens,
        four[0],
        grad_query.astype(F32),
        grad_key.astype(F32),
        grad_value.astype(F32),
        four[2],
        four[3],
        grad_out.astype(F32),
        four[1],
        grad_router,
        grad_gate,
        grad_up,
        grad_down,
    )


def solution(mesh):
    wide, narrow = mesh.shape["wide"], mesh.shape["narrow"]
    near = 2
    middle = min(wide // near, 4)
    inner = Mesh(mesh.devices.reshape(wide // (near * middle), middle, near, narrow // 2, 2), ALL)
    both = P(WIDE, NARROW)
    cube = P(WIDE, None, NARROW)
    lane = P(NARROW)
    row = P(WIDE, None)
    return jax.shard_map(
        per_device,
        mesh=inner,
        in_specs=(
            both, both, row, row, lane, both, both, both, lane, lane, both, lane, P(),
            cube, cube, cube,
        ),
        out_specs=(
            both, both, lane, both, both, both, lane, lane, both, lane, P(), cube, cube, cube,
        ),
        check_vma=False,
    )
```

```python
import functools

import jax
import jax.numpy as jnp
from jax import lax
from jax.experimental import pallas as pl
from jax.experimental.pallas import tpu as pltpu
from jax.sharding import Mesh
from jax.sharding import PartitionSpec as P

HD = 128
EPS = 1e-05
WIDE = ("t", "g", "p")
NARROW = ("y", "c")
GROUP = ("g", "p", "c")
ALL = ("t", "g", "p", "y", "c")
BF = jnp.bfloat16
F32 = jnp.float32
ROWS = 1024
COLS = 256
WIDE_COLS = 512
COST = pl.CostEstimate(flops=1000, transcendentals=0, bytes_accessed=1000)


def rms_scale(values, scales):
    return values * lax.rsqrt(jnp.mean(values * values, axis=-1, keepdims=True) + EPS) * scales


def rope_tables(length, head_dim):
    exponent = jnp.arange(0, head_dim, 2, dtype=F32) / head_dim
    angles = jnp.arange(length, dtype=F32)[:, None] * (10000.0 ** (-exponent))[None, :]
    cosines, sines = jnp.cos(angles), jnp.sin(angles)
    return (
        jnp.concatenate([cosines, cosines], axis=-1),
        jnp.concatenate([-sines, sines], axis=-1),
    )


def dot(a, b, contract):
    return lax.dot_general(a, b, (contract, ((), ())), preferred_element_type=F32)


def place_of(array):
    large = array.size * array.dtype.itemsize > 1 << 20
    return pl.BlockSpec(memory_space=pltpu.HBM if large else pl.ANY)


def call(body, outs, scratch, args, flops, vmem, moved):
    return pl.pallas_call(
        body,
        out_shape=outs,
        in_specs=[place_of(a) for a in args],
        out_specs=jax.tree.map(lambda _: pl.BlockSpec(memory_space=pl.ANY), outs),
        scratch_shapes=scratch,
        compiler_params=pltpu.CompilerParams(vmem_limit_bytes=vmem << 20),
        cost_estimate=COST,
    )(*args)


def start_all(copies):
    for one in copies:
        one.start()
    return copies


def wait_all(copies):
    for one in copies:
        one.wait()


def weight_copies(pieces, whole, sems, stride=1, at=0):
    units = pieces[0].shape[3]
    copies = []
    for half, piece in enumerate(pieces):
        for c in range(2):
            k = half * 2 + c
            there = pl.ds((k * stride + at) * units, units)
            copies.append(
                pltpu.make_async_copy(piece.at[:, c], whole.at[:, :, there], sems.at[k])
            )
    return copies


def block_copies(blocks, whole, sems):
    rows = blocks[0].shape[0]
    return [
        pltpu.make_async_copy(b, whole.at[pl.ds(i * rows, rows)], sems.at[i])
        for i, b in enumerate(blocks)
    ]


def arrived(view, sem):
    pltpu.make_async_copy(view, view, sem).wait()


def await_weight(whole, sems, k, now):
    units = whole.shape[2] // 4

    @pl.when(now)
    def _():
        arrived(whole.at[:, :, pl.ds(pl.multiple_of(k * units, units), units)], sems.at[k])


def await_rows(whole, sems, count, r):
    rows = whole.shape[0] // count
    each = max(1, ROWS // rows)
    if rows <= ROWS:
        for i in range(each):
            b = r * each + i
            arrived(whole.at[pl.ds(pl.multiple_of(b * rows, rows), rows)], sems.at[b])
    else:

        @pl.when(r % (rows // ROWS) == 0)
        def _():
            b = r // (rows // ROWS)
            arrived(whole.at[pl.ds(pl.multiple_of(b * rows, rows), rows)], sems.at[b])


def to_column(line):
    return jnp.transpose(jnp.broadcast_to(line, (128, 128)))


def to_line(column):
    return jnp.transpose(jnp.broadcast_to(column, (128, 128)))[:1]


def take(ref, k, size=COLS):
    part = ref[:, :, pl.ds(pl.multiple_of(k * size, size), size)]
    return part.reshape(-1, size)


def take_rows(ref, n, size=COLS):
    each = size // ref.shape[1]
    return ref[pl.ds(n * each, each)].reshape(size, ref.shape[2])


def project_body(count, *refs):
    blocks, pieces, out = refs[:count], refs[count : count + 2], refs[count + 2]
    rows_v, weight_v, out_v, sem_b, sem_w, sem_o = refs[count + 3 :]
    cw = weight_copies(pieces, weight_v, sem_w)
    cb = block_copies(blocks, rows_v, sem_b)
    ahead = max(1, count * ROWS // rows_v.shape[0])
    start_all(cb[:ahead] + cw + cb[ahead:])
    steps = rows_v.shape[0] // ROWS

    def row_step(r, carry):
        here = pl.ds(pl.multiple_of(r * ROWS, ROWS), ROWS)
        await_rows(rows_v, sem_b, count, r)

        def col_step(k, carry):
            for n in range(WIDE_COLS // COLS):
                await_weight(weight_v, sem_w, k * (WIDE_COLS // COLS) + n, r == 0)
            cols = pl.ds(pl.multiple_of(k * WIDE_COLS, WIDE_COLS), WIDE_COLS)
            got = dot(rows_v[here, :], take(weight_v, k, WIDE_COLS), ((1,), (0,)))
            out_v[here, cols] = got.astype(BF)
            return carry

        lax.fori_loop(0, out_v.shape[1] // WIDE_COLS, col_step, 0)
        pltpu.make_async_copy(out_v.at[here], out.at[here], sem_o.at[r]).start()
        return carry

    lax.fori_loop(0, steps, row_step, 0)
    for r in range(steps):
        here = pl.ds(r * ROWS, ROWS)
        pltpu.make_async_copy(out_v.at[here], out.at[here], sem_o.at[r]).wait()


def project(blocks, got, other):
    rows = blocks[0].shape[0] * len(blocks)
    model = blocks[0].shape[1]
    w, _, depth, units = got.shape
    hidden = 4 * units
    return call(
        functools.partial(project_body, len(blocks)),
        jax.ShapeDtypeStruct((rows, hidden), BF),
        [
            pltpu.VMEM((rows, model), BF),
            pltpu.VMEM((w, depth, hidden), BF),
            pltpu.VMEM((rows, hidden), BF),
            pltpu.SemaphoreType.DMA((len(blocks),)),
            pltpu.SemaphoreType.DMA((4,)),
            pltpu.SemaphoreType.DMA((rows // ROWS,)),
        ],
        (*blocks, got, other),
        2 * rows * model * hidden,
        40,
        2 * (rows * model + model * hidden + rows * hidden),
    )


def expert_body(count, *refs):
    blocks = refs[:count]
    gate_p, up_p = refs[count : count + 2], refs[count + 2 : count + 4]
    down_grad, own_gate = refs[count + 4 : count + 6]
    gg, ug, hs, dots = refs[count + 6 : count + 10]
    rows_v, pair_v, grad_v, own_v, gg_v, ug_v, hs_v, dots_v = refs[count + 10 : count + 18]
    own_c, pair_a, pair_b, sem_b, sem_w, sem_i, sem_o = refs[count + 18 :]
    ci = start_all(
        [
            pltpu.make_async_copy(down_grad, grad_v, sem_i.at[0]),
            pltpu.make_async_copy(own_gate, own_v, sem_i.at[1]),
        ]
    )
    cg = weight_copies(gate_p, pair_v, sem_w.at[0], 2, 0)
    cu = weight_copies(up_p, pair_v, sem_w.at[1], 2, 1)
    cb = block_copies(blocks, rows_v, sem_b)
    ahead = max(1, count * ROWS // rows_v.shape[0])
    start_all(cb[:ahead] + [c for two in zip(cg, cu) for c in two] + cb[ahead:])
    wait_all(ci)
    steps = rows_v.shape[0] // ROWS
    lines = ROWS // 128
    outs = ((gg_v, gg, 0), (ug_v, ug, 1), (hs_v, hs, 2))
    chunks = gg_v.shape[1] // COLS
    for i in range(own_v.shape[0]):
        own_c[i * 128 : (i + 1) * 128, :] = to_column(own_v[i : i + 1, :])

    def ready(i):
        k = i % chunks

        @pl.when(k == 0)
        def _():
            await_rows(rows_v, sem_b, count, i // chunks)

        @pl.when(i < chunks)
        def _():
            for n in range(2):
                there = pl.ds(pl.multiple_of((2 * k + n) * COLS, COLS), COLS)
                arrived(pair_v.at[:, :, there], sem_w.at[n, k])

    def rows_at(i):
        return pl.ds(pl.multiple_of((i // chunks) * ROWS, ROWS), ROWS)

    def products(i, pair_s):
        pair_s[...] = dot(
            rows_v[rows_at(i), :], take(pair_v, i % chunks, 2 * COLS), ((1,), (0,))
        )

    def activate(i, pair_s, total):
        here, k = rows_at(i), i % chunks
        cols = pl.ds(pl.multiple_of(k * COLS, COLS), COLS)
        own = own_c[here, :1]
        gate, up = pair_s[:, :COLS], pair_s[:, COLS:]
        grad = grad_v[here, cols].astype(F32)
        sig = 1.0 / (1.0 + jnp.exp(-gate))
        act = gate * sig
        hidden = act * up
        hs_v[here, cols] = (own * hidden).astype(BF)
        part = jnp.sum(hidden * grad, axis=1, keepdims=True)
        grad = own * grad
        gg_v[here, cols] = (grad * up * (sig + act * (1.0 - sig))).astype(BF)
        ug_v[here, cols] = (grad * act).astype(BF)
        return jnp.where(k == 0, 0.0, total) + part

    ready(0)
    products(0, pair_a)
    most = steps * chunks - 1

    def step(j, total):
        i = 2 * j
        ready(i + 1)
        after_next = jnp.minimum(i + 2, most)

        @pl.when(i + 2 <= most)
        def _():
            ready(i + 2)

        products(i + 1, pair_b)
        total = activate(i, pair_a, total)
        products(after_next, pair_a)
        total = activate(i + 1, pair_b, total)

        @pl.when((i + 1) % chunks == chunks - 1)
        def _():
            r = i // chunks
            dots_v[pl.ds(pl.multiple_of(r * lines, lines), lines), :] = jnp.concatenate(
                [to_line(total[n * 128 : (n + 1) * 128]) for n in range(lines)], axis=0
            )
            for src, dst, n in outs:
                here = rows_at(i)
                pltpu.make_async_copy(src.at[here], dst.at[here], sem_o.at[n, r]).start()

        return total

    lax.fori_loop(0, steps * chunks // 2, step, jnp.zeros((ROWS, 1), F32))
    last = pltpu.make_async_copy(dots_v, dots, sem_i.at[2])
    last.start()
    for r in range(steps):
        here = pl.ds(r * ROWS, ROWS)
        for src, dst, i in outs:
            pltpu.make_async_copy(src.at[here], dst.at[here], sem_o.at[i, r]).wait()
    last.wait()


def expert(blocks, gate_p, up_p, down_grad, own_gate):
    rows = blocks[0].shape[0] * len(blocks)
    model = blocks[0].shape[1]
    w, _, depth, units = gate_p[0].shape
    hidden = 4 * units
    steps = rows // ROWS
    out = jax.ShapeDtypeStruct((rows, hidden), BF)
    wide = jax.ShapeDtypeStruct(own_gate.shape, F32)
    return call(
        functools.partial(expert_body, len(blocks)),
        (out, out, out, wide),
        [
            pltpu.VMEM((rows, model), BF),
            pltpu.VMEM((w, depth, 2 * hidden), BF),
            pltpu.VMEM((rows, hidden), BF),
            pltpu.VMEM(own_gate.shape, F32),
            pltpu.VMEM((rows, hidden), BF),
            pltpu.VMEM((rows, hidden), BF),
            pltpu.VMEM((rows, hidden), BF),
            pltpu.VMEM(own_gate.shape, F32),
            pltpu.VMEM((rows, 128), F32),
        ]
        + [pltpu.VMEM((ROWS, 2 * COLS), F32)] * 2
        + [
            pltpu.SemaphoreType.DMA((len(blocks),)),
            pltpu.SemaphoreType.DMA((2, 4)),
            pltpu.SemaphoreType.DMA((3,)),
            pltpu.SemaphoreType.DMA((3, steps)),
        ],
        (*blocks, *gate_p, *up_p, down_grad, own_gate),
        4 * rows * model * hidden,
        56,
        2 * (rows * model + 2 * model * hidden + 4 * rows * hidden),
    )


def back_body(first, pairs, tail, *refs):
    refs = list(refs)
    ins = [refs[3 * i : 3 * i + 3] for i in range(pairs)]
    at = 3 * pairs
    if tail:
        dots, place = refs[at : at + 2]
        at += 2
    out = refs[at]
    scratch = refs[at + 1 :]
    if tail:
        dots_v, place_v, sem_t = scratch[-3:]
        scratch = scratch[:-3]
        side = start_all(
            [
                pltpu.make_async_copy(dots, dots_v, sem_t.at[0]),
                pltpu.make_async_copy(place, place_v, sem_t.at[1]),
            ]
        )
    grads, weights = scratch[:pairs], scratch[pairs : 2 * pairs]
    out_v, sem_g, sem_w, sem_o = scratch[2 * pairs :]
    rows = out_v.shape[0]
    each = WIDE_COLS // weights[0].shape[1]
    parts = weights[0].shape[0] // each
    for i, (grad, got, other) in enumerate(ins):
        pltpu.make_async_copy(grad.at[pl.ds(first, rows)], grads[i], sem_g.at[i]).start()
    for n in range(parts):
        place = pl.ds(n * each, each)
        for i, (grad, got, other) in enumerate(ins):
            pieces = (got.at[place], other.at[place])
            start_all(weight_copies(pieces, weights[i].at[place], sem_w.at[i, n]))
    for i in range(pairs):
        arrived(grads[i], sem_g.at[i])

    def col_step(n, carry):
        for i in range(pairs):
            block = weights[i].at[pl.ds(n * each, each)]
            for k in range(4):
                await_weight(block, sem_w.at[i, n], k, n >= 0)
        cols = pl.ds(pl.multiple_of(n * WIDE_COLS, WIDE_COLS), WIDE_COLS)
        total = dot(grads[0][...], take_rows(weights[0], n, WIDE_COLS), ((1,), (1,)))
        for i in range(1, pairs):
            total += dot(grads[i][...], take_rows(weights[i], n, WIDE_COLS), ((1,), (1,)))
        out_v[:, cols] = total.astype(BF)
        pltpu.make_async_copy(out_v.at[:, cols], out.at[:, cols], sem_o.at[n]).start()
        return carry

    if tail:
        wait_all(side)
        cols = pl.ds(parts * WIDE_COLS, 128)
        for i in range(rows // 128):
            line = dots_v[first // 128 + i : first // 128 + i + 1, :]
            value = (to_column(line) * place_v[...]).astype(BF)
            out_v[i * 128 : (i + 1) * 128, parts * WIDE_COLS :] = value
        last = pltpu.make_async_copy(out_v.at[:, cols], out.at[:, cols], sem_o.at[parts])
        last.start()
    lax.fori_loop(0, parts, col_step, 0)
    for n in range(parts):
        cols = pl.ds(n * WIDE_COLS, WIDE_COLS)
        pltpu.make_async_copy(out_v.at[:, cols], out.at[:, cols], sem_o.at[n]).wait()
    if tail:
        last.wait()


def back(triples, first, rows, tail=()):
    w, _, depth, units = triples[0][1].shape
    model, hidden = w * depth, 4 * units
    n = len(triples)
    full = model + 128 if tail else model
    return call(
        functools.partial(back_body, first, n, bool(tail)),
        jax.ShapeDtypeStruct((rows, full), BF),
        [pltpu.VMEM((rows, hidden), BF)] * n
        + [pltpu.VMEM((w, depth, hidden), BF)] * n
        + [
            pltpu.VMEM((rows, full), BF),
            pltpu.SemaphoreType.DMA((n,)),
            pltpu.SemaphoreType.DMA((n, model // WIDE_COLS, 4)),
            pltpu.SemaphoreType.DMA((model // WIDE_COLS + 1,)),
        ]
        + [pltpu.VMEM(t.shape, F32) for t in tail]
        + [pltpu.SemaphoreType.DMA((2,))] * bool(tail),
        [a for t in triples for a in t] + list(tail),
        2 * n * rows * model * hidden,
        40,
        2 * (n * rows * hidden + n * model * hidden + rows * model),
    )


def weight_body(count, depth, *refs):
    blocks, grad, mine, theirs = refs[:count], refs[count], refs[count + 1], refs[count + 2]
    rows_v, grad_v, out_v, sem_b, sem_g, sem_o = refs[count + 3 :]
    cg = pltpu.make_async_copy(grad, grad_v, sem_g.at[0])
    wait_all(start_all(block_copies(blocks, rows_v, sem_b) + [cg]))
    units = COLS
    each = COLS // depth
    steps = rows_v.shape[1] // COLS

    def step(n, carry):
        cols = pl.ds(pl.multiple_of(n * COLS, COLS), COLS)
        got = dot(rows_v[:, cols], grad_v[...], ((0,), (0,))).astype(BF)
        for k in range(4):
            part = got[:, k * units : (k + 1) * units].reshape(each, depth, units)
            out_v[k // 2, pl.ds(n * each, each), k % 2] = part
        place = pl.ds(n * each, each)
        pltpu.make_async_copy(out_v.at[0, place], mine.at[place], sem_o.at[0, n]).start()
        pltpu.make_async_copy(out_v.at[1, place], theirs.at[place], sem_o.at[1, n]).start()
        return carry

    lax.fori_loop(0, steps, step, 0)
    for n in range(steps):
        place = pl.ds(n * each, each)
        pltpu.make_async_copy(out_v.at[0, place], mine.at[place], sem_o.at[0, n]).wait()
        pltpu.make_async_copy(out_v.at[1, place], theirs.at[place], sem_o.at[1, n]).wait()


def weight_grad(blocks, grad, depth):
    rows = blocks[0].shape[0] * len(blocks)
    model = blocks[0].shape[1]
    hidden = grad.shape[1]
    w = model // depth
    piece = jax.ShapeDtypeStruct((w, 2, depth, hidden // 4), BF)
    steps = model // COLS
    return call(
        functools.partial(weight_body, len(blocks), depth),
        (piece, piece),
        [
            pltpu.VMEM((rows, model), BF),
            pltpu.VMEM((rows, hidden), BF),
            pltpu.VMEM((2, w, 2, depth, hidden // 4), BF),
            pltpu.SemaphoreType.DMA((len(blocks),)),
            pltpu.SemaphoreType.DMA((1,)),
            pltpu.SemaphoreType.DMA((2, steps)),
        ],
        (*blocks, grad),
        2 * rows * model * hidden,
        40,
        2 * (rows * model + model * hidden + rows * hidden),
    )


def terms_body(pairs, *refs):
    ins, me, outs = refs[: 2 * pairs], refs[2 * pairs], refs[2 * pairs + 1 : 2 * pairs + 3]
    scratch = refs[2 * pairs + 3 :]
    held, out_v, sems, out_sem = scratch[: 2 * pairs], scratch[-3], scratch[-2], scratch[-1]
    wait_all(
        start_all(
            [pltpu.make_async_copy(ins[i], held[i], sems.at[i]) for i in range(2 * pairs)]
        )
    )
    _, count, _, depth, _ = out_v.shape
    mine = me[0]

    each = COLS // depth

    def step(n, carry):
        rows = pl.ds(pl.multiple_of(n * COLS, COLS), COLS)
        at = 0
        for i in range(pairs):
            wide = held[2 * i + 1].shape[1]
            got = dot(held[2 * i][:, rows], held[2 * i + 1][...], ((0,), (0,))).astype(BF)
            for j in range(each):
                b = n * each + j
                distance = jnp.bitwise_xor(b % 8, mine)
                half = distance % 2
                far = distance // 2
                place = (far % 2) * 2 + far // 2
                out_v[half, b // 8, place, :, at : at + wide] = got[j * depth : (j + 1) * depth]
            at += wide
        return carry

    lax.fori_loop(0, count * 8 // each, step, 0)
    wait_all(
        start_all([pltpu.make_async_copy(out_v.at[i], outs[i], out_sem.at[i]) for i in range(2)])
    )


def block_terms(pairs, me, depth):
    length, model = pairs[0][0].shape
    count = model // (8 * depth)
    n = sum(c.shape[1] for _, c in pairs)
    piece = jax.ShapeDtypeStruct((count, 4, depth, n), BF)
    flat = [x for two in pairs for x in two]
    return pl.pallas_call(
        functools.partial(terms_body, len(pairs)),
        out_shape=(piece, piece),
        in_specs=[place_of(a) for a in flat]
        + [pl.BlockSpec(memory_space=pltpu.SMEM)],
        out_specs=(pl.BlockSpec(memory_space=pl.ANY),) * 2,
        scratch_shapes=[pltpu.VMEM(x.shape, BF) for x in flat]
        + [
            pltpu.VMEM((2,) + piece.shape, BF),
            pltpu.SemaphoreType.DMA((len(flat),)),
            pltpu.SemaphoreType.DMA((2,)),
        ],
        compiler_params=pltpu.CompilerParams(vmem_limit_bytes=24 << 20),
        cost_estimate=COST,
    )(*flat, me)


def to_columns(line):
    return jnp.concatenate(
        [to_column(line[:, i : i + 128])[:, :1] for i in range(0, line.shape[1], 128)], axis=0
    )


def to_lines(column):
    return jnp.concatenate(
        [to_line(column[i : i + 128]) for i in range(0, column.shape[0], 128)], axis=1
    )


def bring(ins, held, sems):
    wait_all(
        start_all([pltpu.make_async_copy(a, b, sems.at[i]) for i, (a, b) in enumerate(zip(ins, held))])
    )


def send_out(held, outs, sems):
    wait_all(
        start_all([pltpu.make_async_copy(a, b, sems.at[i]) for i, (a, b) in enumerate(zip(held, outs))])
    )


def raw_body(normed, weights, query, key, value, squares, *scratch):
    normed_v, weights_v, query_v, key_v, value_v, squares_v, sem_i, sem_o = scratch
    wide = query_v.shape[1]
    bring((normed, weights.at[:, pl.ds(0, 3 * wide)]), (normed_v, weights_v), sem_i)
    length = query_v.shape[0]
    for place, ref in ((0, query_v), (1, key_v)):

        def step(j, total):
            cols = pl.ds(pl.multiple_of(j * COLS, COLS), COLS)
            w = weights_v[:, pl.ds(pl.multiple_of(place * wide + j * COLS, COLS), COLS)]
            got = dot(normed_v[...], w, ((1,), (0,)))
            ref[:, cols] = got
            return total + jnp.sum(got * got, axis=1, keepdims=True)

        total = lax.fori_loop(0, wide // COLS, step, jnp.zeros((length, 1), F32))
        squares_v[place : place + 1, :] = to_lines(total)

    def step(j, carry):
        cols = pl.ds(pl.multiple_of(j * COLS, COLS), COLS)
        w = weights_v[:, pl.ds(pl.multiple_of(2 * wide + j * COLS, COLS), COLS)]
        value_v[:, cols] = dot(normed_v[...], w, ((1,), (0,))).astype(BF)
        return carry

    lax.fori_loop(0, wide // COLS, step, 0)
    send_out((query_v, key_v, value_v, squares_v), (query, key, value, squares), sem_o)


def raw_heads(normed, weights, wide):
    length, model = normed.shape
    shapes = [((length, wide), F32), ((length, wide), F32), ((length, wide), BF), ((2, length), F32)]
    return call(
        raw_body,
        tuple(jax.ShapeDtypeStruct(*one) for one in shapes),
        [pltpu.VMEM((length, model), BF), pltpu.VMEM((model, 3 * wide), BF)]
        + [pltpu.VMEM(*one) for one in shapes]
        + [pltpu.SemaphoreType.DMA((2,)), pltpu.SemaphoreType.DMA((4,))],
        (normed, weights),
        0,
        32,
        0,
    )


def half_turn(values):
    return pltpu.roll(values, HD // 2, 1)


def attend_body(*refs):
    ins, outs, scratch = refs[:10], refs[10:15], refs[15:]
    held, made, sem_i, sem_o = scratch[:10], scratch[10:15], scratch[15], scratch[16]
    query, key, value, scales, gains, cosines, sines, ids, weights = ins[:9]
    wide = query.shape[1]
    views = list(ins[:9])
    views[8] = weights.at[:, pl.ds(3 * wide, wide)]
    bring(views, held[:9], sem_i)
    query_v, key_v, value_v, scales_v, gains_v, cos_v, sin_v, ids_v, weights_v = held[:9]
    query_o, key_o, attended_o, log_o, out_o = made
    line = ids_v[...]
    allowed = line <= to_columns(line)
    scale_q, scale_k = to_columns(scales_v[0:1, :]), to_columns(scales_v[1:2, :])

    def step(h, carry):
        cols = pl.ds(pl.multiple_of(h * HD, HD), HD)
        cosines, sines = cos_v[...], sin_v[...]
        q = query_v[:, cols] * scale_q * gains_v[0:1, cols]
        k = key_v[:, cols] * scale_k * gains_v[1:2, cols]
        q = (q * cosines + half_turn(q) * sines).astype(BF)
        k = (k * cosines + half_turn(k) * sines).astype(BF)
        query_o[:, cols] = q
        key_o[:, cols] = k
        scores = jnp.where(allowed, dot(q, k, ((1,), (1,))) * HD**-0.5, -1e30)
        highest = jnp.max(scores, axis=1, keepdims=True)
        shifted = jnp.exp(scores - highest)
        totals = jnp.sum(shifted, axis=1, keepdims=True)
        probs = (shifted / totals).astype(BF)
        attended_o[:, cols] = dot(probs, value_v[:, cols], ((1,), (0,))).astype(BF)
        log_o[pl.ds(h, 1), :] = to_lines(highest + jnp.log(totals))
        return carry

    lax.fori_loop(0, wide // HD, step, 0)

    def out_step(j, carry):
        cols = pl.ds(pl.multiple_of(j * COLS, COLS), COLS)
        out_o[:, cols] = dot(attended_o[...], weights_v[cols, :], ((1,), (1,))).astype(BF)
        return carry

    lax.fori_loop(0, out_o.shape[1] // COLS, out_step, 0)
    send_out(made, outs, sem_o)


def attend(query, key, value, scales, gains, tables, ids, weights):
    length, wide = query.shape
    model = weights.shape[0]
    args = (query, key, value, scales, gains, *tables, ids, weights, ids)
    held = [pltpu.VMEM(x.shape, x.dtype) for x in args[:8]]
    held += [pltpu.VMEM((model, wide), BF), pltpu.VMEM(ids.shape, ids.dtype)]
    shapes = [
        ((length, wide), BF),
        ((length, wide), BF),
        ((length, wide), BF),
        ((wide // HD, length), F32),
        ((length, model), BF),
    ]
    return call(
        attend_body,
        tuple(jax.ShapeDtypeStruct(*one) for one in shapes),
        held
        + [pltpu.VMEM(*one) for one in shapes]
        + [pltpu.SemaphoreType.DMA((9,)), pltpu.SemaphoreType.DMA((5,))],
        args,
        0,
        32,
        0,
    )


def unattend_body(*refs):
    ins, outs, scratch = refs[:12], refs[12:16], refs[16:]
    held, grad_v, made, sem_i, sem_o = (
        scratch[:12], scratch[12], scratch[13:17], scratch[17], scratch[18],
    )
    wide = ins[2].shape[1]
    views = list(ins)
    views[1] = ins[1].at[:, pl.ds(3 * wide, wide)]
    bring(views, held, sem_i)
    cot_v, weights_v, query_v, key_v, value_v, log_v, ids_v, cos_v, sin_v, gains_v, raw_q, raw_k = held
    query_o, key_o, value_o, dots_o = made
    grad_v[...] = dot(cot_v[...], weights_v[...], ((1,), (0,))).astype(BF)
    line = ids_v[...]
    allowed = line <= to_columns(line)
    length = cot_v.shape[0]
    zero = jnp.zeros((length, 1), F32)

    def step(h, carry):
        dot_q, dot_k = carry
        cols = pl.ds(pl.multiple_of(h * HD, HD), HD)
        cosines, sines = cos_v[...], sin_v[...]
        q, k, v, grad = query_v[:, cols], key_v[:, cols], value_v[:, cols], grad_v[:, cols]
        scores = jnp.where(allowed, dot(q, k, ((1,), (1,))) * HD**-0.5, -1e30)
        probs = jnp.exp(scores - to_columns(log_v[pl.ds(h, 1), :]))
        prob_grad = dot(grad, v, ((1,), (1,)))
        centre = jnp.sum(probs * prob_grad, axis=1, keepdims=True)
        score_grad = (probs * (prob_grad - centre)).astype(BF)
        value_o[:, cols] = dot(probs.astype(BF), grad, ((0,), (0,))).astype(BF)
        back_q = dot(score_grad, k, ((1,), (0,))) * HD**-0.5
        back_k = dot(score_grad, q, ((0,), (0,))) * HD**-0.5
        back_q = back_q * cosines + half_turn(back_q * sines)
        back_k = back_k * cosines + half_turn(back_k * sines)
        query_o[:, cols] = back_q
        key_o[:, cols] = back_k
        dot_q += jnp.sum(gains_v[0:1, cols] * back_q * raw_q[:, cols], axis=1, keepdims=True)
        dot_k += jnp.sum(gains_v[1:2, cols] * back_k * raw_k[:, cols], axis=1, keepdims=True)
        return dot_q, dot_k

    dot_q, dot_k = lax.fori_loop(0, wide // HD, step, (zero, zero))
    dots_o[0:1, :] = to_lines(dot_q)
    dots_o[1:2, :] = to_lines(dot_k)
    send_out(made, outs, sem_o)


def unattend(out_cot, weights, query, key, value, logs, ids, tables, gains, raw_q, raw_k):
    length, wide = query.shape
    args = (out_cot, weights, query, key, value, logs, ids, *tables, gains, raw_q, raw_k)
    held = [pltpu.VMEM(x.shape, x.dtype) for x in args]
    held[1] = pltpu.VMEM((weights.shape[0], wide), BF)
    shapes = [((length, wide), F32), ((length, wide), F32), ((length, wide), BF), ((2, length), F32)]
    return call(
        unattend_body,
        tuple(jax.ShapeDtypeStruct(*one) for one in shapes),
        held
        + [pltpu.VMEM((length, wide), BF)]
        + [pltpu.VMEM(*one) for one in shapes]
        + [pltpu.SemaphoreType.DMA((12,)), pltpu.SemaphoreType.DMA((4,))],
        args,
        0,
        40,
        0,
    )


def unnorm_body(*refs):
    ins, outs, scratch = refs[:7], refs[7:9], refs[9:]
    held, made, sem_i, sem_o = scratch[:7], scratch[7:9], scratch[9], scratch[10]
    bring(ins, held, sem_i)
    back_q, back_k, raw_q, raw_k, scales_v, dots_v, gains_v = held
    grads_o, gains_o = made
    wide = raw_q.shape[1]
    for i, (back, raw) in enumerate(((back_q, raw_q), (back_k, raw_k))):
        scale = to_columns(scales_v[i : i + 1, :])
        push = to_columns(dots_v[i : i + 1, :]) * scale * scale * scale
        grad = scale * gains_v[i : i + 1, :] * back[...] - raw[...] * push
        grads_o[:, i * wide : (i + 1) * wide] = grad.astype(BF)
        gains_o[i : i + 1, :] = jnp.sum(back[...] * raw[...] * scale, axis=0, keepdims=True)
    send_out(made, outs, sem_o)


def unnorm(back_q, back_k, raw_q, raw_k, scales, dots, gains):
    length, wide = raw_q.shape
    args = (back_q, back_k, raw_q, raw_k, scales, dots, gains)
    shapes = [((length, 2 * wide), BF), ((2, wide), F32)]
    return call(
        unnorm_body,
        tuple(jax.ShapeDtypeStruct(*one) for one in shapes),
        [pltpu.VMEM(x.shape, x.dtype) for x in args]
        + [pltpu.VMEM(*one) for one in shapes]
        + [pltpu.SemaphoreType.DMA((7,)), pltpu.SemaphoreType.DMA((2,))],
        args,
        0,
        24,
        0,
    )


def after(values, *earlier):
    return lax.optimization_barrier((values, earlier))[0]


def stage(*values):
    return lax.optimization_barrier(values)


def swap(values, axis, step=1):
    count = lax.axis_size(axis)
    return lax.ppermute(values, axis, [(i, i ^ step) for i in range(count)])


def gather_four(block, axis):
    count = lax.axis_size("y") * lax.axis_size("c")
    size = block.shape[axis]
    here = lax.axis_index("y") * lax.axis_size("c") + lax.axis_index("c")
    other = swap(block, "y")
    near = swap(block, "c")
    far = swap(other, "c")
    shape = list(block.shape)
    shape[axis] = size * count
    whole = jnp.zeros(shape, block.dtype)
    for piece, place in ((block, 0), (near, 1), (other, 2), (far, 3)):
        whole = lax.dynamic_update_slice_in_dim(whole, piece, (here ^ place) * size, axis)
    return whole


def sum_near(partial):
    length, width = partial.shape
    y, c = lax.axis_index("y"), lax.axis_index("c")
    parts = partial.reshape(2, 2, length // 4, width)
    mine = lax.dynamic_index_in_dim(parts, c, 1, False)
    theirs = lax.dynamic_index_in_dim(parts, 1 - c, 1, False)
    mine = mine.astype(F32) + swap(theirs.astype(BF), "c").astype(F32)
    keep = lax.dynamic_index_in_dim(mine, y, 0, False)
    send = lax.dynamic_index_in_dim(mine, 1 - y, 0, False)
    return keep, send.astype(BF)


def add(*pieces):
    total = pieces[0].astype(F32)
    for piece in pieces[1:]:
        total = total + piece.astype(F32)
    return total


def to_experts(columns):
    sent = lax.all_to_all(columns.T, GROUP, 0, 0, tiled=True)
    v = sent.reshape((-1, 2) + sent.shape[1:])
    c = lax.axis_index("c")
    own = lax.dynamic_index_in_dim(v, c, 1, False)
    other = lax.dynamic_index_in_dim(v, 1 - c, 1, False)
    return jnp.concatenate([own, other]).reshape(sent.shape[0], -1)


def to_group(weight):
    got = lax.all_to_all(weight, GROUP, 0, 0, tiled=True)
    return got.reshape((got.shape[0] // 2, 2) + got.shape[1:])


def over_sequences(*terms):
    if lax.axis_size("t") > 1:
        terms = [lax.psum_scatter(x, "t", scatter_dimension=0, tiled=True) for x in terms]
    return [x[0] for x in terms]


def over_groups(piece):
    if lax.axis_size("t") > 1:
        piece = lax.all_gather(piece, "t", axis=0, tiled=True)
    return piece


def sum_over(values, axis):
    step = 1
    while step < lax.axis_size(axis):
        values = values + swap(values, axis, step)
        step *= 2
    return values


def to_slices(mine, theirs):
    total = (mine.astype(F32) + theirs.astype(F32)).astype(BF)
    if lax.axis_size("t") > 1:
        total = lax.psum_scatter(total, "t", scatter_dimension=0, tiled=True)
    sent = total.reshape((-1,) + total.shape[2:])
    return lax.all_to_all(sent, GROUP, 0, 0, tiled=True)


def as_output(got):
    return jnp.transpose(got, (1, 0, 2)).astype(F32)


def per_device(
    tokens,
    cotangent,
    block_ids,
    routes,
    norm_attn,
    w_query,
    w_key,
    w_value,
    norm_query,
    norm_key,
    w_out,
    norm_ffn,
    w_router,
    w_gate,
    w_up,
    w_down,
):
    experts = w_router.shape[1]
    lane_index = lax.axis_index("y") * lax.axis_size("c") + lax.axis_index("c")
    lanes = lax.axis_size("y") * lax.axis_size("c")
    length, head_cols = tokens.shape
    model_width = head_cols * lanes
    rows = length // lanes

    all_full = lax.all_gather(
        jnp.concatenate([w_query, w_key, w_value, w_out], axis=1), WIDE, axis=0, tiled=True
    )

    rows_full = gather_four(tokens, 1)
    gains = lax.all_gather(jnp.stack([norm_attn, norm_ffn]), NARROW, axis=1, tiled=True)
    down_got = to_group(jnp.transpose(w_down, (1, 0, 2)))
    gate_sent = jnp.transpose(w_gate, (1, 0, 2))
    up_sent = jnp.transpose(w_up, (1, 0, 2))
    cot_rows = lax.all_to_all(cotangent.reshape(lanes, rows, head_cols), NARROW, 0, 0, tiled=True)
    cot_rows = jnp.transpose(cot_rows, (1, 0, 2)).reshape(rows, model_width)
    rows_full, cot_rows, gate_sent, up_sent, gains = stage(
        rows_full, cot_rows, gate_sent, up_sent, gains
    )
    attn_gain = gains[0].astype(F32)
    ffn_gain = gains[1].astype(F32)
    rows_float = rows_full.astype(F32)
    normed = rms_scale(rows_float, attn_gain).astype(BF)
    down_got, gate_sent, normed, cot_sent = stage(down_got, gate_sent, normed, cot_rows)

    down_other = swap(down_got, "y")
    all_full, normed, cot_sent, gate_sent, down_other = stage(
        all_full, normed, cot_sent, gate_sent, down_other
    )

    gate_got = to_group(gate_sent)
    cot_mine = lax.all_gather(cot_sent, ("g", "p"), axis=0, tiled=True)
    qkv_full = all_full[:, : 3 * head_cols]
    raw_query, raw_key, value_bf, squares = raw_heads(normed, all_full, head_cols)
    scales = lax.rsqrt(lax.psum(squares, NARROW) / model_width + EPS)
    scales, gate_got, up_sent = stage(scales, gate_got, up_sent)
    up_got = to_group(up_sent)
    cut = gate_got.shape[0] // 2
    gate_first = swap(gate_got[:cut], "y")
    gains_here = jnp.stack([norm_query, norm_key]).astype(F32)
    tables = rope_tables(length, HD)
    ids = block_ids.astype(F32)
    query_bf, key_bf, attended, log_totals, out_partial = attend(
        raw_query, raw_key, value_bf, scales, gains_here, tables, ids, all_full
    )

    first_row = lane_index * rows
    x_rows = lax.dynamic_slice_in_dim(rows_full, first_row, rows, 0).astype(F32)
    keep, send = sum_near(out_partial)
    keep, send, gate_first = stage(keep, send, gate_first)
    residual = x_rows + keep + swap(send, "y").astype(F32)
    ffn_in = rms_scale(residual, ffn_gain).astype(BF)
    ffn_in, up_got, gate_got, cot_mine = stage(ffn_in, up_got, gate_got, cot_mine)

    up_other = swap(up_got, "y")
    gate_last = swap(gate_got[cut:], "y")
    x_mine = lax.all_gather(ffn_in, ("g", "p"), axis=0, tiled=True)
    cot_all = [cot_mine, swap(cot_mine, "c")]
    down_own = (over_groups(down_got), over_groups(down_other))
    down_grad = project(cot_all, *down_own)
    logits = jnp.dot(ffn_in, w_router, preferred_element_type=F32)
    gate_probs = jax.nn.softmax(logits, axis=-1)
    routes_rows = lax.dynamic_slice_in_dim(routes, first_row, rows, 0)
    chosen = jnp.any(
        routes_rows[:, :, None] == jnp.arange(experts, dtype=jnp.int32)[None, None, :], axis=1
    )
    own_gate = to_experts(jnp.where(chosen, gate_probs, 0.0))
    x_mine, down_grad, own_gate, up_other, gate_last = stage(
        x_mine, down_grad, own_gate, up_other, gate_last
    )
    gate_other = jnp.concatenate([gate_first, gate_last])
    x_all = [x_mine, swap(x_mine, "c")]
    gate_own = (over_groups(gate_got), over_groups(gate_other))
    up_own = (over_groups(up_got), over_groups(up_other))

    gate_grad, up_grad, hidden_gated, own_dots = expert(
        x_all, gate_own, up_own, down_grad, own_gate
    )
    half = gate_grad.shape[0] // 2
    own_index = lax.axis_index("g") * 4 + lax.axis_index("p") * 2 + lax.axis_index("c")
    depth = down_own[0].shape[2]
    own_place = (jnp.arange(128) == own_index).astype(F32)[None]
    depth = down_own[0].shape[2]
    pairs = ((gate_grad, *gate_own), (up_grad, *up_own))
    theirs = back(pairs, half, half, (own_dots, own_place))
    gate_grad, up_grad, own_dots, theirs = stage(gate_grad, up_grad, own_dots, theirs)
    pairs = ((gate_grad, *gate_own), (up_grad, *up_own))
    mine = back(pairs, 0, half, (own_dots, own_place))
    sent = add(mine, swap(theirs, "c")).astype(BF)
    sent, hidden_gated, gate_grad, up_grad = stage(sent, hidden_gated, gate_grad, up_grad)

    input_sum = lax.psum_scatter(sent, ("g", "p"), scatter_dimension=0, tiled=True)
    down_mine, down_theirs = weight_grad(cot_all, hidden_gated, depth)
    down_theirs, gate_grad, hidden_gated, up_grad = stage(
        down_theirs, gate_grad, hidden_gated, up_grad
    )
    down_theirs = swap(down_theirs, "y")
    gate_mine, gate_theirs = weight_grad(x_all, gate_grad, depth)
    up_mine, up_theirs = weight_grad(x_all, up_grad, depth)
    moe_pair = ((hidden_gated, *down_own),)
    moe_theirs = back(moe_pair, half, half)
    moe_mine = back(moe_pair, 0, half)
    down_theirs, gate_theirs, up_theirs, moe_theirs, moe_mine = stage(
        down_theirs, gate_theirs, up_theirs, moe_theirs, moe_mine
    )
    cut = gate_theirs.shape[0] // 2
    gate_first = swap(gate_theirs[:cut], "y")
    down_got = to_slices(down_mine, down_theirs)
    moe_sent = add(moe_mine, swap(moe_theirs, "c")).astype(BF)
    input_sum, moe_sent, gate_first = stage(input_sum, moe_sent, gate_first)
    moe_sum = lax.psum_scatter(moe_sent, ("g", "p"), scatter_dimension=0, tiled=True)
    input_sum = input_sum.astype(F32)
    pair_dots = jnp.where(chosen, input_sum[:, model_width : model_width + experts], 0.0)
    input_sum = input_sum[:, :model_width]

    logit_grad = (
        gate_probs * (pair_dots - jnp.sum(gate_probs * pair_dots, axis=1, keepdims=True))
    ).astype(BF)
    ffn_grad = input_sum + dot(logit_grad, w_router, ((1,), (1,)))
    router_grad = dot(logit_grad, ffn_in, ((0,), (0,)))
    _, ffn_norm_pull = jax.vjp(rms_scale, residual, ffn_gain)
    residual_norm_grad, ffn_gain_grad = ffn_norm_pull(ffn_grad)
    residual_grad = cot_rows.astype(F32) + residual_norm_grad
    out_cot = gather_four(residual_grad.astype(BF), 0)
    out_cot, up_theirs, down_got, gate_theirs = stage(out_cot, up_theirs, down_got, gate_theirs)

    gate_last = swap(gate_theirs[cut:], "y")
    back_query, back_key, value_grad, dots = unattend(
        out_cot, all_full, query_bf, key_bf, value_bf, log_totals, ids, tables, gains_here,
        raw_query, raw_key,
    )
    group_index = (lax.axis_index("g") * 2 + lax.axis_index("p")).astype(jnp.int32)[None]
    two_keep, two_near = over_sequences(
        *block_terms(((out_cot, attended), (normed, value_grad)), group_index, depth)
    )
    dots, two_near, two_keep, gate_last = stage(dots, two_near, two_keep, gate_last)
    gate_got = to_slices(gate_mine, jnp.concatenate([gate_first, gate_last]))
    two_near = swap(two_near, "p")
    dots = lax.psum(dots, NARROW) / model_width
    dots, up_theirs = stage(dots, up_theirs)

    up_theirs = swap(up_theirs, "y")
    pair_pre, pair_gains = unnorm(
        back_query, back_key, raw_query, raw_key, scales, dots, gains_here
    )
    qkv_grad = jnp.concatenate([pair_pre, value_grad], axis=1)
    pair_keep, pair_near = over_sequences(*block_terms(((normed, pair_pre),), group_index, depth))
    qkv_grad, pair_keep, pair_near = stage(qkv_grad, pair_keep, pair_near)
    pair_near = swap(pair_near, "p")
    keep, send = sum_near(dot(qkv_grad, qkv_full, ((1,), (1,))))
    keep, send, two_near, two_keep, up_theirs, gate_got = stage(
        keep, send, two_near, two_keep, up_theirs, gate_got
    )
    up_got = to_slices(up_mine, up_theirs)
    send = swap(send, "y")
    normed_grad = add(keep, send)
    two_parts = add(two_keep, two_near)
    two_far = swap(two_parts[2:].astype(BF), "g", 1)
    _, attn_norm_pull = jax.vjp(rms_scale, x_rows, attn_gain)
    rows_norm_grad, attn_gain_grad = attn_norm_pull(normed_grad)
    grad_rows = (residual_grad + rows_norm_grad).astype(BF)
    place = (jnp.arange(lanes) == lane_index).astype(F32)[:, None]
    small = jnp.concatenate(
        [
            router_grad,
            attn_gain_grad[None],
            ffn_gain_grad[None],
            (place * pair_gains[:1]).reshape(1, model_width),
            (place * pair_gains[1:]).reshape(1, model_width),
        ],
        axis=0,
    )
    small = sum_over(small, "c")
    small = sum_over(small, "y")
    grad_rows, two_far, two_parts, pair_near, pair_keep, small, moe_sum = stage(
        grad_rows, two_far, two_parts, pair_near, pair_keep, small, moe_sum
    )

    pair_parts = add(pair_keep, pair_near)
    pair_far = swap(pair_parts[2:].astype(BF), "g", 1)
    two_parts = add(two_parts[:2], two_far)
    two_far = swap(two_parts[1].astype(BF), "g", 2)
    small = sum_over(small, "p")
    pair_far, pair_parts, two_far, two_parts, small, up_got, grad_rows, moe_sum = stage(
        pair_far, pair_parts, two_far, two_parts, small, up_got, grad_rows, moe_sum
    )

    pair_parts = add(pair_parts[:2], pair_far)
    pair_far = swap(pair_parts[1].astype(BF), "g", 2)
    small = sum_over(sum_over(small, "g"), "t")
    grad_two = add(two_parts[0], two_far)
    both_rows = jnp.stack([(residual + moe_sum.astype(F32)).astype(BF), grad_rows])
    both_rows = jnp.transpose(both_rows.reshape(2, rows, lanes, head_cols), (2, 0, 1, 3))
    both_rows = lax.all_to_all(both_rows, NARROW, 0, 0, tiled=True)
    block_out = both_rows[:, 0].reshape(length, head_cols)
    grad_tokens = both_rows[:, 1].reshape(length, head_cols).astype(F32)
    grad_gate = as_output(gate_got)
    grad_down = as_output(down_got)
    grad_up = as_output(up_got)
    grad_pair = add(pair_parts[0], pair_far)
    grad_out, grad_value = grad_two[:, :head_cols], grad_two[:, head_cols:]
    grad_query, grad_key = grad_pair[:, :head_cols], grad_pair[:, head_cols:]
    grad_router = small[:experts].T
    four = lax.dynamic_slice_in_dim(small[experts:], lane_index * head_cols, head_cols, 1)
    return (
        block_out,
        grad_tokens,
        four[0],
        grad_query.astype(F32),
        grad_key.astype(F32),
        grad_value.astype(F32),
        four[2],
        four[3],
        grad_out.astype(F32),
        four[1],
        grad_router,
        grad_gate,
        grad_up,
        grad_down,
    )


def solution(mesh):
    wide, narrow = mesh.shape["wide"], mesh.shape["narrow"]
    near = 2
    middle = min(wide // near, 4)
    inner = Mesh(mesh.devices.reshape(wide // (near * middle), middle, near, narrow // 2, 2), ALL)
    both = P(WIDE, NARROW)
    cube = P(WIDE, None, NARROW)
    lane = P(NARROW)
    row = P(WIDE, None)
    return jax.shard_map(
        per_device,
        mesh=inner,
        in_specs=(
            both, both, row, row, lane, both, both, both, lane, lane, both, lane, P(),
            cube, cube, cube,
        ),
        out_specs=(
            both, both, lane, both, both, both, lane, lane, both, lane, P(), cube, cube, cube,
        ),
        check_vma=False,
    )
```

```python
import functools

import jax
import jax.numpy as jnp
from jax import lax
from jax.experimental import pallas as pl
from jax.experimental.pallas import tpu as pltpu
from jax.sharding import Mesh
from jax.sharding import PartitionSpec as P

HD = 128
EPS = 1e-05
WIDE = ("t", "g", "p")
NARROW = ("y", "c")
GROUP = ("g", "p", "c")
ALL = ("t", "g", "p", "y", "c")
BF = jnp.bfloat16
F32 = jnp.float32
ROWS = 1024
COLS = 256
WIDE_COLS = 512
COST = pl.CostEstimate(flops=1000, transcendentals=0, bytes_accessed=1000)


def rms_scale(values, scales):
    return values * lax.rsqrt(jnp.mean(values * values, axis=-1, keepdims=True) + EPS) * scales


def rope_tables(length, head_dim):
    exponent = jnp.arange(0, head_dim, 2, dtype=F32) / head_dim
    angles = jnp.arange(length, dtype=F32)[:, None] * (10000.0 ** (-exponent))[None, :]
    cosines, sines = jnp.cos(angles), jnp.sin(angles)
    return (
        jnp.concatenate([cosines, cosines], axis=-1),
        jnp.concatenate([-sines, sines], axis=-1),
    )


def dot(a, b, contract):
    return lax.dot_general(a, b, (contract, ((), ())), preferred_element_type=F32)


def place_of(array):
    large = array.size * array.dtype.itemsize > 1 << 20
    return pl.BlockSpec(memory_space=pltpu.HBM if large else pl.ANY)


def call(body, outs, scratch, args, flops, vmem, moved):
    return pl.pallas_call(
        body,
        out_shape=outs,
        in_specs=[place_of(a) for a in args],
        out_specs=jax.tree.map(lambda _: pl.BlockSpec(memory_space=pl.ANY), outs),
        scratch_shapes=scratch,
        compiler_params=pltpu.CompilerParams(vmem_limit_bytes=vmem << 20),
        cost_estimate=COST,
    )(*args)


def start_all(copies):
    for one in copies:
        one.start()
    return copies


def wait_all(copies):
    for one in copies:
        one.wait()


def weight_copies(pieces, whole, sems, stride=1, at=0):
    units = pieces[0].shape[3]
    copies = []
    for half, piece in enumerate(pieces):
        for c in range(2):
            k = half * 2 + c
            there = pl.ds((k * stride + at) * units, units)
            copies.append(
                pltpu.make_async_copy(piece.at[:, c], whole.at[:, :, there], sems.at[k])
            )
    return copies


def block_copies(blocks, whole, sems):
    rows = blocks[0].shape[0]
    return [
        pltpu.make_async_copy(b, whole.at[pl.ds(i * rows, rows)], sems.at[i])
        for i, b in enumerate(blocks)
    ]


def arrived(view, sem):
    pltpu.make_async_copy(view, view, sem).wait()


def await_weight(whole, sems, k, now):
    units = whole.shape[2] // 4

    @pl.when(now)
    def _():
        arrived(whole.at[:, :, pl.ds(pl.multiple_of(k * units, units), units)], sems.at[k])


def await_rows(whole, sems, count, r):
    rows = whole.shape[0] // count
    each = max(1, ROWS // rows)
    if rows <= ROWS:
        for i in range(each):
            b = r * each + i
            arrived(whole.at[pl.ds(pl.multiple_of(b * rows, rows), rows)], sems.at[b])
    else:

        @pl.when(r % (rows // ROWS) == 0)
        def _():
            b = r // (rows // ROWS)
            arrived(whole.at[pl.ds(pl.multiple_of(b * rows, rows), rows)], sems.at[b])


def to_column(line):
    return jnp.transpose(jnp.broadcast_to(line, (128, 128)))


def to_line(column):
    return jnp.transpose(jnp.broadcast_to(column, (128, 128)))[:1]


def take(ref, k, size=COLS):
    part = ref[:, :, pl.ds(pl.multiple_of(k * size, size), size)]
    return part.reshape(-1, size)


def take_rows(ref, n, size=COLS):
    each = size // ref.shape[1]
    return ref[pl.ds(n * each, each)].reshape(size, ref.shape[2])


def project_body(count, *refs):
    blocks, pieces, out = refs[:count], refs[count : count + 2], refs[count + 2]
    rows_v, weight_v, out_v, sem_b, sem_w, sem_o = refs[count + 3 :]
    cw = weight_copies(pieces, weight_v, sem_w)
    cb = block_copies(blocks, rows_v, sem_b)
    ahead = max(1, count * ROWS // rows_v.shape[0])
    start_all(cb[:ahead] + cw + cb[ahead:])
    steps = rows_v.shape[0] // ROWS

    def row_step(r, carry):
        here = pl.ds(pl.multiple_of(r * ROWS, ROWS), ROWS)
        await_rows(rows_v, sem_b, count, r)

        def col_step(k, carry):
            for n in range(WIDE_COLS // COLS):
                await_weight(weight_v, sem_w, k * (WIDE_COLS // COLS) + n, r == 0)
            cols = pl.ds(pl.multiple_of(k * WIDE_COLS, WIDE_COLS), WIDE_COLS)
            got = dot(rows_v[here, :], take(weight_v, k, WIDE_COLS), ((1,), (0,)))
            out_v[here, cols] = got.astype(BF)
            return carry

        lax.fori_loop(0, out_v.shape[1] // WIDE_COLS, col_step, 0)
        pltpu.make_async_copy(out_v.at[here], out.at[here], sem_o.at[r]).start()
        return carry

    lax.fori_loop(0, steps, row_step, 0)
    for r in range(steps):
        here = pl.ds(r * ROWS, ROWS)
        pltpu.make_async_copy(out_v.at[here], out.at[here], sem_o.at[r]).wait()


def project(blocks, got, other):
    rows = blocks[0].shape[0] * len(blocks)
    model = blocks[0].shape[1]
    w, _, depth, units = got.shape
    hidden = 4 * units
    return call(
        functools.partial(project_body, len(blocks)),
        jax.ShapeDtypeStruct((rows, hidden), BF),
        [
            pltpu.VMEM((rows, model), BF),
            pltpu.VMEM((w, depth, hidden), BF),
            pltpu.VMEM((rows, hidden), BF),
            pltpu.SemaphoreType.DMA((len(blocks),)),
            pltpu.SemaphoreType.DMA((4,)),
            pltpu.SemaphoreType.DMA((rows // ROWS,)),
        ],
        (*blocks, got, other),
        2 * rows * model * hidden,
        40,
        2 * (rows * model + model * hidden + rows * hidden),
    )


def expert_body(count, *refs):
    blocks = refs[:count]
    gate_p, up_p = refs[count : count + 2], refs[count + 2 : count + 4]
    down_grad, own_gate = refs[count + 4 : count + 6]
    gg, ug, hs, dots = refs[count + 6 : count + 10]
    rows_v, pair_v, grad_v, own_v, gg_v, ug_v, hs_v, dots_v = refs[count + 10 : count + 18]
    own_c, pair_a, pair_b, sem_b, sem_w, sem_i, sem_o = refs[count + 18 :]
    ci = start_all(
        [
            pltpu.make_async_copy(down_grad, grad_v, sem_i.at[0]),
            pltpu.make_async_copy(own_gate, own_v, sem_i.at[1]),
        ]
    )
    cg = weight_copies(gate_p, pair_v, sem_w.at[0], 2, 0)
    cu = weight_copies(up_p, pair_v, sem_w.at[1], 2, 1)
    cb = block_copies(blocks, rows_v, sem_b)
    ahead = max(1, count * ROWS // rows_v.shape[0])
    start_all(cb[:ahead] + [c for two in zip(cg, cu) for c in two] + cb[ahead:])
    wait_all(ci)
    steps = rows_v.shape[0] // ROWS
    lines = ROWS // 128
    outs = ((gg_v, gg, 0), (ug_v, ug, 1), (hs_v, hs, 2))
    chunks = gg_v.shape[1] // COLS
    for i in range(own_v.shape[0]):
        own_c[i * 128 : (i + 1) * 128, :] = to_column(own_v[i : i + 1, :])

    def ready(i):
        k = i % chunks

        @pl.when(k == 0)
        def _():
            await_rows(rows_v, sem_b, count, i // chunks)

        @pl.when(i < chunks)
        def _():
            for n in range(2):
                there = pl.ds(pl.multiple_of((2 * k + n) * COLS, COLS), COLS)
                arrived(pair_v.at[:, :, there], sem_w.at[n, k])

    def rows_at(i):
        return pl.ds(pl.multiple_of((i // chunks) * ROWS, ROWS), ROWS)

    def products(i, pair_s):
        pair_s[...] = dot(
            rows_v[rows_at(i), :], take(pair_v, i % chunks, 2 * COLS), ((1,), (0,))
        )

    def activate(i, pair_s, total):
        here, k = rows_at(i), i % chunks
        cols = pl.ds(pl.multiple_of(k * COLS, COLS), COLS)
        own = own_c[here, :1]
        gate, up = pair_s[:, :COLS], pair_s[:, COLS:]
        grad = grad_v[here, cols].astype(F32)
        sig = 1.0 / (1.0 + jnp.exp(-gate))
        act = gate * sig
        hidden = act * up
        hs_v[here, cols] = (own * hidden).astype(BF)
        part = jnp.sum(hidden * grad, axis=1, keepdims=True)
        grad = own * grad
        gg_v[here, cols] = (grad * up * (sig + act * (1.0 - sig))).astype(BF)
        ug_v[here, cols] = (grad * act).astype(BF)
        return jnp.where(k == 0, 0.0, total) + part

    ready(0)
    products(0, pair_a)
    most = steps * chunks - 1

    def step(j, total):
        i = 2 * j
        ready(i + 1)
        after_next = jnp.minimum(i + 2, most)

        @pl.when(i + 2 <= most)
        def _():
            ready(i + 2)

        products(i + 1, pair_b)
        total = activate(i, pair_a, total)
        products(after_next, pair_a)
        total = activate(i + 1, pair_b, total)

        @pl.when((i + 1) % chunks == chunks - 1)
        def _():
            r = i // chunks
            dots_v[pl.ds(pl.multiple_of(r * lines, lines), lines), :] = jnp.concatenate(
                [to_line(total[n * 128 : (n + 1) * 128]) for n in range(lines)], axis=0
            )
            for src, dst, n in outs:
                here = rows_at(i)
                pltpu.make_async_copy(src.at[here], dst.at[here], sem_o.at[n, r]).start()

        return total

    lax.fori_loop(0, steps * chunks // 2, step, jnp.zeros((ROWS, 1), F32))
    last = pltpu.make_async_copy(dots_v, dots, sem_i.at[2])
    last.start()
    for r in range(steps):
        here = pl.ds(r * ROWS, ROWS)
        for src, dst, i in outs:
            pltpu.make_async_copy(src.at[here], dst.at[here], sem_o.at[i, r]).wait()
    last.wait()


def expert(blocks, gate_p, up_p, down_grad, own_gate):
    rows = blocks[0].shape[0] * len(blocks)
    model = blocks[0].shape[1]
    w, _, depth, units = gate_p[0].shape
    hidden = 4 * units
    steps = rows // ROWS
    out = jax.ShapeDtypeStruct((rows, hidden), BF)
    wide = jax.ShapeDtypeStruct(own_gate.shape, F32)
    return call(
        functools.partial(expert_body, len(blocks)),
        (out, out, out, wide),
        [
            pltpu.VMEM((rows, model), BF),
            pltpu.VMEM((w, depth, 2 * hidden), BF),
            pltpu.VMEM((rows, hidden), BF),
            pltpu.VMEM(own_gate.shape, F32),
            pltpu.VMEM((rows, hidden), BF),
            pltpu.VMEM((rows, hidden), BF),
            pltpu.VMEM((rows, hidden), BF),
            pltpu.VMEM(own_gate.shape, F32),
            pltpu.VMEM((rows, 128), F32),
        ]
        + [pltpu.VMEM((ROWS, 2 * COLS), F32)] * 2
        + [
            pltpu.SemaphoreType.DMA((len(blocks),)),
            pltpu.SemaphoreType.DMA((2, 4)),
            pltpu.SemaphoreType.DMA((3,)),
            pltpu.SemaphoreType.DMA((3, steps)),
        ],
        (*blocks, *gate_p, *up_p, down_grad, own_gate),
        4 * rows * model * hidden,
        56,
        2 * (rows * model + 2 * model * hidden + 4 * rows * hidden),
    )


def back_body(first, pairs, tail, *refs):
    refs = list(refs)
    ins = [refs[3 * i : 3 * i + 3] for i in range(pairs)]
    at = 3 * pairs
    if tail:
        dots, place = refs[at : at + 2]
        at += 2
    out = refs[at]
    scratch = refs[at + 1 :]
    if tail:
        dots_v, place_v, sem_t = scratch[-3:]
        scratch = scratch[:-3]
        side = start_all(
            [
                pltpu.make_async_copy(dots, dots_v, sem_t.at[0]),
                pltpu.make_async_copy(place, place_v, sem_t.at[1]),
            ]
        )
    grads, weights = scratch[:pairs], scratch[pairs : 2 * pairs]
    out_v, sem_g, sem_w, sem_o = scratch[2 * pairs :]
    rows = out_v.shape[0]
    each = WIDE_COLS // weights[0].shape[1]
    parts = weights[0].shape[0] // each
    for i, (grad, got, other) in enumerate(ins):
        pltpu.make_async_copy(grad.at[pl.ds(first, rows)], grads[i], sem_g.at[i]).start()
    for n in range(parts):
        place = pl.ds(n * each, each)
        for i, (grad, got, other) in enumerate(ins):
            pieces = (got.at[place], other.at[place])
            start_all(weight_copies(pieces, weights[i].at[place], sem_w.at[i, n]))
    for i in range(pairs):
        arrived(grads[i], sem_g.at[i])

    def col_step(n, carry):
        for i in range(pairs):
            block = weights[i].at[pl.ds(n * each, each)]
            for k in range(4):
                await_weight(block, sem_w.at[i, n], k, n >= 0)
        cols = pl.ds(pl.multiple_of(n * WIDE_COLS, WIDE_COLS), WIDE_COLS)
        total = dot(grads[0][...], take_rows(weights[0], n, WIDE_COLS), ((1,), (1,)))
        for i in range(1, pairs):
            total += dot(grads[i][...], take_rows(weights[i], n, WIDE_COLS), ((1,), (1,)))
        out_v[:, cols] = total.astype(BF)
        pltpu.make_async_copy(out_v.at[:, cols], out.at[:, cols], sem_o.at[n]).start()
        return carry

    if tail:
        wait_all(side)
        cols = pl.ds(parts * WIDE_COLS, 128)
        for i in range(rows // 128):
            line = dots_v[first // 128 + i : first // 128 + i + 1, :]
            value = (to_column(line) * place_v[...]).astype(BF)
            out_v[i * 128 : (i + 1) * 128, parts * WIDE_COLS :] = value
        last = pltpu.make_async_copy(out_v.at[:, cols], out.at[:, cols], sem_o.at[parts])
        last.start()
    lax.fori_loop(0, parts, col_step, 0)
    for n in range(parts):
        cols = pl.ds(n * WIDE_COLS, WIDE_COLS)
        pltpu.make_async_copy(out_v.at[:, cols], out.at[:, cols], sem_o.at[n]).wait()
    if tail:
        last.wait()


def back(triples, first, rows, tail=()):
    w, _, depth, units = triples[0][1].shape
    model, hidden = w * depth, 4 * units
    n = len(triples)
    full = model + 128 if tail else model
    return call(
        functools.partial(back_body, first, n, bool(tail)),
        jax.ShapeDtypeStruct((rows, full), BF),
        [pltpu.VMEM((rows, hidden), BF)] * n
        + [pltpu.VMEM((w, depth, hidden), BF)] * n
        + [
            pltpu.VMEM((rows, full), BF),
            pltpu.SemaphoreType.DMA((n,)),
            pltpu.SemaphoreType.DMA((n, model // WIDE_COLS, 4)),
            pltpu.SemaphoreType.DMA((model // WIDE_COLS + 1,)),
        ]
        + [pltpu.VMEM(t.shape, F32) for t in tail]
        + [pltpu.SemaphoreType.DMA((2,))] * bool(tail),
        [a for t in triples for a in t] + list(tail),
        2 * n * rows * model * hidden,
        40,
        2 * (n * rows * hidden + n * model * hidden + rows * model),
    )


def weight_body(count, depth, *refs):
    blocks, grad, mine, theirs = refs[:count], refs[count], refs[count + 1], refs[count + 2]
    rows_v, grad_v, out_v, sem_b, sem_g, sem_o = refs[count + 3 :]
    cg = pltpu.make_async_copy(grad, grad_v, sem_g.at[0])
    wait_all(start_all(block_copies(blocks, rows_v, sem_b) + [cg]))
    units = COLS
    each = COLS // depth
    steps = rows_v.shape[1] // COLS

    def step(n, carry):
        cols = pl.ds(pl.multiple_of(n * COLS, COLS), COLS)
        got = dot(rows_v[:, cols], grad_v[...], ((0,), (0,))).astype(BF)
        for k in range(4):
            part = got[:, k * units : (k + 1) * units].reshape(each, depth, units)
            out_v[k // 2, pl.ds(n * each, each), k % 2] = part
        place = pl.ds(n * each, each)
        pltpu.make_async_copy(out_v.at[0, place], mine.at[place], sem_o.at[0, n]).start()
        pltpu.make_async_copy(out_v.at[1, place], theirs.at[place], sem_o.at[1, n]).start()
        return carry

    lax.fori_loop(0, steps, step, 0)
    for n in range(steps):
        place = pl.ds(n * each, each)
        pltpu.make_async_copy(out_v.at[0, place], mine.at[place], sem_o.at[0, n]).wait()
        pltpu.make_async_copy(out_v.at[1, place], theirs.at[place], sem_o.at[1, n]).wait()


def weight_grad(blocks, grad, depth):
    rows = blocks[0].shape[0] * len(blocks)
    model = blocks[0].shape[1]
    hidden = grad.shape[1]
    w = model // depth
    piece = jax.ShapeDtypeStruct((w, 2, depth, hidden // 4), BF)
    steps = model // COLS
    return call(
        functools.partial(weight_body, len(blocks), depth),
        (piece, piece),
        [
            pltpu.VMEM((rows, model), BF),
            pltpu.VMEM((rows, hidden), BF),
            pltpu.VMEM((2, w, 2, depth, hidden // 4), BF),
            pltpu.SemaphoreType.DMA((len(blocks),)),
            pltpu.SemaphoreType.DMA((1,)),
            pltpu.SemaphoreType.DMA((2, steps)),
        ],
        (*blocks, grad),
        2 * rows * model * hidden,
        40,
        2 * (rows * model + model * hidden + rows * hidden),
    )


def terms_body(pairs, *refs):
    ins, me, outs = refs[: 2 * pairs], refs[2 * pairs], refs[2 * pairs + 1 : 2 * pairs + 3]
    scratch = refs[2 * pairs + 3 :]
    held, out_v, sems, out_sem = scratch[: 2 * pairs], scratch[-3], scratch[-2], scratch[-1]
    wait_all(
        start_all(
            [pltpu.make_async_copy(ins[i], held[i], sems.at[i]) for i in range(2 * pairs)]
        )
    )
    _, count, _, depth, _ = out_v.shape
    mine = me[0]

    each = COLS // depth

    def step(n, carry):
        rows = pl.ds(pl.multiple_of(n * COLS, COLS), COLS)
        at = 0
        for i in range(pairs):
            wide = held[2 * i + 1].shape[1]
            got = dot(held[2 * i][:, rows], held[2 * i + 1][...], ((0,), (0,))).astype(BF)
            for j in range(each):
                b = n * each + j
                distance = jnp.bitwise_xor(b % 8, mine)
                half = distance % 2
                far = distance // 2
                place = (far % 2) * 2 + far // 2
                out_v[half, b // 8, place, :, at : at + wide] = got[j * depth : (j + 1) * depth]
            at += wide
        return carry

    lax.fori_loop(0, count * 8 // each, step, 0)
    wait_all(
        start_all([pltpu.make_async_copy(out_v.at[i], outs[i], out_sem.at[i]) for i in range(2)])
    )


def block_terms(pairs, me, depth):
    length, model = pairs[0][0].shape
    count = model // (8 * depth)
    n = sum(c.shape[1] for _, c in pairs)
    piece = jax.ShapeDtypeStruct((count, 4, depth, n), BF)
    flat = [x for two in pairs for x in two]
    return pl.pallas_call(
        functools.partial(terms_body, len(pairs)),
        out_shape=(piece, piece),
        in_specs=[place_of(a) for a in flat]
        + [pl.BlockSpec(memory_space=pltpu.SMEM)],
        out_specs=(pl.BlockSpec(memory_space=pl.ANY),) * 2,
        scratch_shapes=[pltpu.VMEM(x.shape, BF) for x in flat]
        + [
            pltpu.VMEM((2,) + piece.shape, BF),
            pltpu.SemaphoreType.DMA((len(flat),)),
            pltpu.SemaphoreType.DMA((2,)),
        ],
        compiler_params=pltpu.CompilerParams(vmem_limit_bytes=24 << 20),
        cost_estimate=COST,
    )(*flat, me)


def to_columns(line):
    return jnp.concatenate(
        [to_column(line[:, i : i + 128])[:, :1] for i in range(0, line.shape[1], 128)], axis=0
    )


def to_lines(column):
    return jnp.concatenate(
        [to_line(column[i : i + 128]) for i in range(0, column.shape[0], 128)], axis=1
    )


def bring(ins, held, sems):
    wait_all(
        start_all([pltpu.make_async_copy(a, b, sems.at[i]) for i, (a, b) in enumerate(zip(ins, held))])
    )


def send_out(held, outs, sems):
    wait_all(
        start_all([pltpu.make_async_copy(a, b, sems.at[i]) for i, (a, b) in enumerate(zip(held, outs))])
    )


def raw_body(normed, weights, query, key, value, squares, *scratch):
    normed_v, weights_v, query_v, key_v, value_v, squares_v, sem_i, sem_o = scratch
    wide = query_v.shape[1]
    bring((normed, weights.at[:, pl.ds(0, 3 * wide)]), (normed_v, weights_v), sem_i)
    length = query_v.shape[0]
    for place, ref in ((0, query_v), (1, key_v)):

        def step(j, total):
            cols = pl.ds(pl.multiple_of(j * COLS, COLS), COLS)
            w = weights_v[:, pl.ds(pl.multiple_of(place * wide + j * COLS, COLS), COLS)]
            got = dot(normed_v[...], w, ((1,), (0,)))
            ref[:, cols] = got
            return total + jnp.sum(got * got, axis=1, keepdims=True)

        total = lax.fori_loop(0, wide // COLS, step, jnp.zeros((length, 1), F32))
        squares_v[place : place + 1, :] = to_lines(total)

    def step(j, carry):
        cols = pl.ds(pl.multiple_of(j * COLS, COLS), COLS)
        w = weights_v[:, pl.ds(pl.multiple_of(2 * wide + j * COLS, COLS), COLS)]
        value_v[:, cols] = dot(normed_v[...], w, ((1,), (0,))).astype(BF)
        return carry

    lax.fori_loop(0, wide // COLS, step, 0)
    send_out((query_v, key_v, value_v, squares_v), (query, key, value, squares), sem_o)


def raw_heads(normed, weights, wide):
    length, model = normed.shape
    shapes = [((length, wide), F32), ((length, wide), F32), ((length, wide), BF), ((2, length), F32)]
    return call(
        raw_body,
        tuple(jax.ShapeDtypeStruct(*one) for one in shapes),
        [pltpu.VMEM((length, model), BF), pltpu.VMEM((model, 3 * wide), BF)]
        + [pltpu.VMEM(*one) for one in shapes]
        + [pltpu.SemaphoreType.DMA((2,)), pltpu.SemaphoreType.DMA((4,))],
        (normed, weights),
        0,
        32,
        0,
    )


def half_turn(values):
    return pltpu.roll(values, HD // 2, 1)


def attend_body(*refs):
    ins, outs, scratch = refs[:10], refs[10:15], refs[15:]
    held, made, sem_i, sem_o = scratch[:10], scratch[10:15], scratch[15], scratch[16]
    query, key, value, scales, gains, cosines, sines, ids, weights = ins[:9]
    wide = query.shape[1]
    views = list(ins[:9])
    views[8] = weights.at[:, pl.ds(3 * wide, wide)]
    bring(views, held[:9], sem_i)
    query_v, key_v, value_v, scales_v, gains_v, cos_v, sin_v, ids_v, weights_v = held[:9]
    query_o, key_o, attended_o, log_o, out_o = made
    line = ids_v[...]
    allowed = line <= to_columns(line)
    scale_q, scale_k = to_columns(scales_v[0:1, :]), to_columns(scales_v[1:2, :])

    def step(h, carry):
        cols = pl.ds(pl.multiple_of(h * HD, HD), HD)
        cosines, sines = cos_v[...], sin_v[...]
        q = query_v[:, cols] * scale_q * gains_v[0:1, cols]
        k = key_v[:, cols] * scale_k * gains_v[1:2, cols]
        q = (q * cosines + half_turn(q) * sines).astype(BF)
        k = (k * cosines + half_turn(k) * sines).astype(BF)
        query_o[:, cols] = q
        key_o[:, cols] = k
        scores = jnp.where(allowed, dot(q, k, ((1,), (1,))) * HD**-0.5, -1e30)
        highest = jnp.max(scores, axis=1, keepdims=True)
        shifted = jnp.exp(scores - highest)
        totals = jnp.sum(shifted, axis=1, keepdims=True)
        probs = (shifted / totals).astype(BF)
        attended_o[:, cols] = dot(probs, value_v[:, cols], ((1,), (0,))).astype(BF)
        log_o[pl.ds(h, 1), :] = to_lines(highest + jnp.log(totals))
        return carry

    lax.fori_loop(0, wide // HD, step, 0)

    def out_step(j, carry):
        cols = pl.ds(pl.multiple_of(j * COLS, COLS), COLS)
        out_o[:, cols] = dot(attended_o[...], weights_v[cols, :], ((1,), (1,))).astype(BF)
        return carry

    lax.fori_loop(0, out_o.shape[1] // COLS, out_step, 0)
    send_out(made, outs, sem_o)


def attend(query, key, value, scales, gains, tables, ids, weights):
    length, wide = query.shape
    model = weights.shape[0]
    args = (query, key, value, scales, gains, *tables, ids, weights, ids)
    held = [pltpu.VMEM(x.shape, x.dtype) for x in args[:8]]
    held += [pltpu.VMEM((model, wide), BF), pltpu.VMEM(ids.shape, ids.dtype)]
    shapes = [
        ((length, wide), BF),
        ((length, wide), BF),
        ((length, wide), BF),
        ((wide // HD, length), F32),
        ((length, model), BF),
    ]
    return call(
        attend_body,
        tuple(jax.ShapeDtypeStruct(*one) for one in shapes),
        held
        + [pltpu.VMEM(*one) for one in shapes]
        + [pltpu.SemaphoreType.DMA((9,)), pltpu.SemaphoreType.DMA((5,))],
        args,
        0,
        32,
        0,
    )


def unattend_body(*refs):
    ins, outs, scratch = refs[:12], refs[12:16], refs[16:]
    held, grad_v, made, sem_i, sem_o = (
        scratch[:12], scratch[12], scratch[13:17], scratch[17], scratch[18],
    )
    wide = ins[2].shape[1]
    views = list(ins)
    views[1] = ins[1].at[:, pl.ds(3 * wide, wide)]
    bring(views, held, sem_i)
    cot_v, weights_v, query_v, key_v, value_v, log_v, ids_v, cos_v, sin_v, gains_v, raw_q, raw_k = held
    query_o, key_o, value_o, dots_o = made
    grad_v[...] = dot(cot_v[...], weights_v[...], ((1,), (0,))).astype(BF)
    line = ids_v[...]
    allowed = line <= to_columns(line)
    length = cot_v.shape[0]
    zero = jnp.zeros((length, 1), F32)

    def step(h, carry):
        dot_q, dot_k = carry
        cols = pl.ds(pl.multiple_of(h * HD, HD), HD)
        cosines, sines = cos_v[...], sin_v[...]
        q, k, v, grad = query_v[:, cols], key_v[:, cols], value_v[:, cols], grad_v[:, cols]
        scores = jnp.where(allowed, dot(q, k, ((1,), (1,))) * HD**-0.5, -1e30)
        probs = jnp.exp(scores - to_columns(log_v[pl.ds(h, 1), :]))
        prob_grad = dot(grad, v, ((1,), (1,)))
        centre = jnp.sum(probs * prob_grad, axis=1, keepdims=True)
        score_grad = (probs * (prob_grad - centre)).astype(BF)
        value_o[:, cols] = dot(probs.astype(BF), grad, ((0,), (0,))).astype(BF)
        back_q = dot(score_grad, k, ((1,), (0,))) * HD**-0.5
        back_k = dot(score_grad, q, ((0,), (0,))) * HD**-0.5
        back_q = back_q * cosines + half_turn(back_q * sines)
        back_k = back_k * cosines + half_turn(back_k * sines)
        query_o[:, cols] = back_q
        key_o[:, cols] = back_k
        dot_q += jnp.sum(gains_v[0:1, cols] * back_q * raw_q[:, cols], axis=1, keepdims=True)
        dot_k += jnp.sum(gains_v[1:2, cols] * back_k * raw_k[:, cols], axis=1, keepdims=True)
        return dot_q, dot_k

    dot_q, dot_k = lax.fori_loop(0, wide // HD, step, (zero, zero))
    dots_o[0:1, :] = to_lines(dot_q)
    dots_o[1:2, :] = to_lines(dot_k)
    send_out(made, outs, sem_o)


def unattend(out_cot, weights, query, key, value, logs, ids, tables, gains, raw_q, raw_k):
    length, wide = query.shape
    args = (out_cot, weights, query, key, value, logs, ids, *tables, gains, raw_q, raw_k)
    held = [pltpu.VMEM(x.shape, x.dtype) for x in args]
    held[1] = pltpu.VMEM((weights.shape[0], wide), BF)
    shapes = [((length, wide), F32), ((length, wide), F32), ((length, wide), BF), ((2, length), F32)]
    return call(
        unattend_body,
        tuple(jax.ShapeDtypeStruct(*one) for one in shapes),
        held
        + [pltpu.VMEM((length, wide), BF)]
        + [pltpu.VMEM(*one) for one in shapes]
        + [pltpu.SemaphoreType.DMA((12,)), pltpu.SemaphoreType.DMA((4,))],
        args,
        0,
        40,
        0,
    )


def unnorm_body(*refs):
    ins, outs, scratch = refs[:7], refs[7:9], refs[9:]
    held, made, sem_i, sem_o = scratch[:7], scratch[7:9], scratch[9], scratch[10]
    bring(ins, held, sem_i)
    back_q, back_k, raw_q, raw_k, scales_v, dots_v, gains_v = held
    grads_o, gains_o = made
    wide = raw_q.shape[1]
    for i, (back, raw) in enumerate(((back_q, raw_q), (back_k, raw_k))):
        scale = to_columns(scales_v[i : i + 1, :])
        push = to_columns(dots_v[i : i + 1, :]) * scale * scale * scale
        grad = scale * gains_v[i : i + 1, :] * back[...] - raw[...] * push
        grads_o[:, i * wide : (i + 1) * wide] = grad.astype(BF)
        gains_o[i : i + 1, :] = jnp.sum(back[...] * raw[...] * scale, axis=0, keepdims=True)
    send_out(made, outs, sem_o)


def unnorm(back_q, back_k, raw_q, raw_k, scales, dots, gains):
    length, wide = raw_q.shape
    args = (back_q, back_k, raw_q, raw_k, scales, dots, gains)
    shapes = [((length, 2 * wide), BF), ((2, wide), F32)]
    return call(
        unnorm_body,
        tuple(jax.ShapeDtypeStruct(*one) for one in shapes),
        [pltpu.VMEM(x.shape, x.dtype) for x in args]
        + [pltpu.VMEM(*one) for one in shapes]
        + [pltpu.SemaphoreType.DMA((7,)), pltpu.SemaphoreType.DMA((2,))],
        args,
        0,
        24,
        0,
    )


def after(values, *earlier):
    return lax.optimization_barrier((values, earlier))[0]


def stage(*values):
    return lax.optimization_barrier(values)


def swap(values, axis, step=1):
    count = lax.axis_size(axis)
    return lax.ppermute(values, axis, [(i, i ^ step) for i in range(count)])


def gather_four(block, axis):
    count = lax.axis_size("y") * lax.axis_size("c")
    size = block.shape[axis]
    here = lax.axis_index("y") * lax.axis_size("c") + lax.axis_index("c")
    other = swap(block, "y")
    near = swap(block, "c")
    far = swap(other, "c")
    shape = list(block.shape)
    shape[axis] = size * count
    whole = jnp.zeros(shape, block.dtype)
    for piece, place in ((block, 0), (near, 1), (other, 2), (far, 3)):
        whole = lax.dynamic_update_slice_in_dim(whole, piece, (here ^ place) * size, axis)
    return whole


def sum_near(partial):
    length, width = partial.shape
    y, c = lax.axis_index("y"), lax.axis_index("c")
    parts = partial.reshape(2, 2, length // 4, width)
    mine = lax.dynamic_index_in_dim(parts, c, 1, False)
    theirs = lax.dynamic_index_in_dim(parts, 1 - c, 1, False)
    mine = mine.astype(F32) + swap(theirs.astype(BF), "c").astype(F32)
    keep = lax.dynamic_index_in_dim(mine, y, 0, False)
    send = lax.dynamic_index_in_dim(mine, 1 - y, 0, False)
    return keep, send.astype(BF)


def add(*pieces):
    total = pieces[0].astype(F32)
    for piece in pieces[1:]:
        total = total + piece.astype(F32)
    return total


def to_experts(columns):
    sent = lax.all_to_all(columns.T, GROUP, 0, 0, tiled=True)
    v = sent.reshape((-1, 2) + sent.shape[1:])
    c = lax.axis_index("c")
    own = lax.dynamic_index_in_dim(v, c, 1, False)
    other = lax.dynamic_index_in_dim(v, 1 - c, 1, False)
    return jnp.concatenate([own, other]).reshape(sent.shape[0], -1)


def to_group(weight):
    got = lax.all_to_all(weight, GROUP, 0, 0, tiled=True)
    return got.reshape((got.shape[0] // 2, 2) + got.shape[1:])


def over_sequences(*terms):
    if lax.axis_size("t") > 1:
        terms = [lax.psum_scatter(x, "t", scatter_dimension=0, tiled=True) for x in terms]
    return [x[0] for x in terms]


def over_groups(piece):
    if lax.axis_size("t") > 1:
        piece = lax.all_gather(piece, "t", axis=0, tiled=True)
    return piece


def sum_over(values, axis):
    step = 1
    while step < lax.axis_size(axis):
        values = values + swap(values, axis, step)
        step *= 2
    return values


def to_slices(mine, theirs):
    total = (mine.astype(F32) + theirs.astype(F32)).astype(BF)
    if lax.axis_size("t") > 1:
        total = lax.psum_scatter(total, "t", scatter_dimension=0, tiled=True)
    sent = total.reshape((-1,) + total.shape[2:])
    return lax.all_to_all(sent, GROUP, 0, 0, tiled=True)


def as_output(got):
    return jnp.transpose(got, (1, 0, 2)).astype(F32)


def per_device(
    tokens,
    cotangent,
    block_ids,
    routes,
    norm_attn,
    w_query,
    w_key,
    w_value,
    norm_query,
    norm_key,
    w_out,
    norm_ffn,
    w_router,
    w_gate,
    w_up,
    w_down,
):
    experts = w_router.shape[1]
    lane_index = lax.axis_index("y") * lax.axis_size("c") + lax.axis_index("c")
    lanes = lax.axis_size("y") * lax.axis_size("c")
    length, head_cols = tokens.shape
    model_width = head_cols * lanes
    rows = length // lanes

    all_full = lax.all_gather(
        jnp.concatenate([w_query, w_key, w_value, w_out], axis=1), WIDE, axis=0, tiled=True
    )

    rows_full = gather_four(tokens, 1)
    gains = lax.all_gather(jnp.stack([norm_attn, norm_ffn]), NARROW, axis=1, tiled=True)
    down_got = to_group(jnp.transpose(w_down, (1, 0, 2)))
    gate_sent = jnp.transpose(w_gate, (1, 0, 2))
    up_sent = jnp.transpose(w_up, (1, 0, 2))
    cot_rows = lax.all_to_all(cotangent.reshape(lanes, rows, head_cols), NARROW, 0, 0, tiled=True)
    cot_rows = jnp.transpose(cot_rows, (1, 0, 2)).reshape(rows, model_width)
    rows_full, cot_rows, gate_sent, up_sent, gains = stage(
        rows_full, cot_rows, gate_sent, up_sent, gains
    )
    attn_gain = gains[0].astype(F32)
    ffn_gain = gains[1].astype(F32)
    rows_float = rows_full.astype(F32)
    normed = rms_scale(rows_float, attn_gain).astype(BF)
    down_got, gate_sent, normed, cot_sent = stage(down_got, gate_sent, normed, cot_rows)

    down_other = swap(down_got, "y")
    all_full, normed, cot_sent, gate_sent, down_other = stage(
        all_full, normed, cot_sent, gate_sent, down_other
    )

    gate_got = to_group(gate_sent)
    cot_mine = lax.all_gather(cot_sent, ("g", "p"), axis=0, tiled=True)
    qkv_full = all_full[:, : 3 * head_cols]
    raw_query, raw_key, value_bf, squares = raw_heads(normed, all_full, head_cols)
    scales = lax.rsqrt(lax.psum(squares, NARROW) / model_width + EPS)
    scales, gate_got, up_sent = stage(scales, gate_got, up_sent)
    up_got = to_group(up_sent)
    cut = gate_got.shape[0] // 2
    gate_first = swap(gate_got[:cut], "y")
    gains_here = jnp.stack([norm_query, norm_key]).astype(F32)
    tables = rope_tables(length, HD)
    ids = block_ids.astype(F32)
    query_bf, key_bf, attended, log_totals, out_partial = attend(
        raw_query, raw_key, value_bf, scales, gains_here, tables, ids, all_full
    )

    first_row = lane_index * rows
    x_rows = lax.dynamic_slice_in_dim(rows_full, first_row, rows, 0).astype(F32)
    keep, send = sum_near(out_partial)
    keep, send, gate_first = stage(keep, send, gate_first)
    residual = x_rows + keep + swap(send, "y").astype(F32)
    ffn_in = rms_scale(residual, ffn_gain).astype(BF)
    ffn_in, up_got, gate_got, cot_mine = stage(ffn_in, up_got, gate_got, cot_mine)

    up_other = swap(up_got, "y")
    gate_last = swap(gate_got[cut:], "y")
    x_mine = lax.all_gather(ffn_in, ("g", "p"), axis=0, tiled=True)
    cot_all = [cot_mine, swap(cot_mine, "c")]
    down_own = (over_groups(down_got), over_groups(down_other))
    down_grad = project(cot_all, *down_own)
    logits = jnp.dot(ffn_in, w_router, preferred_element_type=F32)
    gate_probs = jax.nn.softmax(logits, axis=-1)
    routes_rows = lax.dynamic_slice_in_dim(routes, first_row, rows, 0)
    chosen = jnp.any(
        routes_rows[:, :, None] == jnp.arange(experts, dtype=jnp.int32)[None, None, :], axis=1
    )
    own_gate = to_experts(jnp.where(chosen, gate_probs, 0.0))
    x_mine, down_grad, own_gate, up_other, gate_last = stage(
        x_mine, down_grad, own_gate, up_other, gate_last
    )
    gate_other = jnp.concatenate([gate_first, gate_last])
    x_all = [x_mine, swap(x_mine, "c")]
    gate_own = (over_groups(gate_got), over_groups(gate_other))
    up_own = (over_groups(up_got), over_groups(up_other))

    gate_grad, up_grad, hidden_gated, own_dots = expert(
        x_all, gate_own, up_own, down_grad, own_gate
    )
    half = gate_grad.shape[0] // 2
    own_index = lax.axis_index("g") * 4 + lax.axis_index("p") * 2 + lax.axis_index("c")
    depth = down_own[0].shape[2]
    own_place = (jnp.arange(128) == own_index).astype(F32)[None]
    depth = down_own[0].shape[2]
    pairs = ((gate_grad, *gate_own), (up_grad, *up_own))
    theirs = back(pairs, half, half, (own_dots, own_place))
    gate_grad, up_grad, own_dots, theirs = stage(gate_grad, up_grad, own_dots, theirs)
    pairs = ((gate_grad, *gate_own), (up_grad, *up_own))
    mine = back(pairs, 0, half, (own_dots, own_place))
    sent = add(mine, swap(theirs, "c")).astype(BF)
    sent, hidden_gated, gate_grad, up_grad = stage(sent, hidden_gated, gate_grad, up_grad)

    input_sum = lax.psum_scatter(sent, ("g", "p"), scatter_dimension=0, tiled=True)
    down_mine, down_theirs = weight_grad(cot_all, hidden_gated, depth)
    down_theirs, gate_grad, hidden_gated, up_grad = stage(
        down_theirs, gate_grad, hidden_gated, up_grad
    )
    down_theirs = swap(down_theirs, "y")
    gate_mine, gate_theirs = weight_grad(x_all, gate_grad, depth)
    up_mine, up_theirs = weight_grad(x_all, up_grad, depth)
    moe_pair = ((hidden_gated, *down_own),)
    moe_theirs = back(moe_pair, half, half)
    moe_mine = back(moe_pair, 0, half)
    down_theirs, gate_theirs, up_theirs, moe_theirs, moe_mine = stage(
        down_theirs, gate_theirs, up_theirs, moe_theirs, moe_mine
    )
    cut = gate_theirs.shape[0] // 2
    gate_first = swap(gate_theirs[:cut], "y")
    down_got = to_slices(down_mine, down_theirs)
    moe_sent = add(moe_mine, swap(moe_theirs, "c")).astype(BF)
    input_sum, moe_sent, gate_first = stage(input_sum, moe_sent, gate_first)
    moe_sum = lax.psum_scatter(moe_sent, ("g", "p"), scatter_dimension=0, tiled=True)
    input_sum = input_sum.astype(F32)
    pair_dots = jnp.where(chosen, input_sum[:, model_width : model_width + experts], 0.0)
    input_sum = input_sum[:, :model_width]

    logit_grad = (
        gate_probs * (pair_dots - jnp.sum(gate_probs * pair_dots, axis=1, keepdims=True))
    ).astype(BF)
    ffn_grad = input_sum + dot(logit_grad, w_router, ((1,), (1,)))
    router_grad = dot(logit_grad, ffn_in, ((0,), (0,)))
    _, ffn_norm_pull = jax.vjp(rms_scale, residual, ffn_gain)
    residual_norm_grad, ffn_gain_grad = ffn_norm_pull(ffn_grad)
    residual_grad = cot_rows.astype(F32) + residual_norm_grad
    out_cot = gather_four(residual_grad.astype(BF), 0)
    out_cot, up_theirs, down_got, gate_theirs = stage(out_cot, up_theirs, down_got, gate_theirs)

    gate_last = swap(gate_theirs[cut:], "y")
    back_query, back_key, value_grad, dots = unattend(
        out_cot, all_full, query_bf, key_bf, value_bf, log_totals, ids, tables, gains_here,
        raw_query, raw_key,
    )
    group_index = (lax.axis_index("g") * 2 + lax.axis_index("p")).astype(jnp.int32)[None]
    two_keep, two_near = over_sequences(
        *block_terms(((out_cot, attended), (normed, value_grad)), group_index, depth)
    )
    dots, two_near, two_keep, gate_last = stage(dots, two_near, two_keep, gate_last)
    gate_got = to_slices(gate_mine, jnp.concatenate([gate_first, gate_last]))
    two_near = swap(two_near, "p")
    dots = lax.psum(dots, NARROW) / model_width
    dots, up_theirs = stage(dots, up_theirs)

    up_theirs = swap(up_theirs, "y")
    pair_pre, pair_gains = unnorm(
        back_query, back_key, raw_query, raw_key, scales, dots, gains_here
    )
    qkv_grad = jnp.concatenate([pair_pre, value_grad], axis=1)
    pair_keep, pair_near = over_sequences(*block_terms(((normed, pair_pre),), group_index, depth))
    qkv_grad, pair_keep, pair_near = stage(qkv_grad, pair_keep, pair_near)
    pair_near = swap(pair_near, "p")
    keep, send = sum_near(dot(qkv_grad, qkv_full, ((1,), (1,))))
    keep, send, up_theirs, gate_got = stage(keep, send, up_theirs, gate_got)
    up_got = to_slices(up_mine, up_theirs)
    send = swap(send, "y")
    send, two_near, two_keep = stage(send, two_near, two_keep)
    normed_grad = add(keep, send)
    two_parts = add(two_keep, two_near)
    two_far = swap(two_parts[2:].astype(BF), "g", 1)
    _, attn_norm_pull = jax.vjp(rms_scale, x_rows, attn_gain)
    rows_norm_grad, attn_gain_grad = attn_norm_pull(normed_grad)
    grad_rows = (residual_grad + rows_norm_grad).astype(BF)
    place = (jnp.arange(lanes) == lane_index).astype(F32)[:, None]
    small = jnp.concatenate(
        [
            router_grad,
            attn_gain_grad[None],
            ffn_gain_grad[None],
            (place * pair_gains[:1]).reshape(1, model_width),
            (place * pair_gains[1:]).reshape(1, model_width),
        ],
        axis=0,
    )
    small = sum_over(small, "g")
    grad_rows, two_far, two_parts, pair_near, pair_keep, small, moe_sum = stage(
        grad_rows, two_far, two_parts, pair_near, pair_keep, small, moe_sum
    )

    pair_parts = add(pair_keep, pair_near)
    pair_far = swap(pair_parts[2:].astype(BF), "g", 1)
    two_parts = add(two_parts[:2], two_far)
    two_far = swap(two_parts[1].astype(BF), "g", 2)
    small = sum_over(sum_over(small, "p"), "t")
    pair_far, pair_parts, two_far, two_parts, small, up_got, grad_rows, moe_sum = stage(
        pair_far, pair_parts, two_far, two_parts, small, up_got, grad_rows, moe_sum
    )

    pair_parts = add(pair_parts[:2], pair_far)
    pair_far = swap(pair_parts[1].astype(BF), "g", 2)
    small = sum_over(sum_over(small, "y"), "c")
    grad_two = add(two_parts[0], two_far)
    both_rows = jnp.stack([(residual + moe_sum.astype(F32)).astype(BF), grad_rows])
    both_rows = jnp.transpose(both_rows.reshape(2, rows, lanes, head_cols), (2, 0, 1, 3))
    both_rows = lax.all_to_all(both_rows, NARROW, 0, 0, tiled=True)
    block_out = both_rows[:, 0].reshape(length, head_cols)
    grad_tokens = both_rows[:, 1].reshape(length, head_cols).astype(F32)
    grad_gate = as_output(gate_got)
    grad_down = as_output(down_got)
    grad_up = as_output(up_got)
    grad_pair = add(pair_parts[0], pair_far)
    grad_out, grad_value = grad_two[:, :head_cols], grad_two[:, head_cols:]
    grad_query, grad_key = grad_pair[:, :head_cols], grad_pair[:, head_cols:]
    grad_router = small[:experts].T
    four = lax.dynamic_slice_in_dim(small[experts:], lane_index * head_cols, head_cols, 1)
    return (
        block_out,
        grad_tokens,
        four[0],
        grad_query.astype(F32),
        grad_key.astype(F32),
        grad_value.astype(F32),
        four[2],
        four[3],
        grad_out.astype(F32),
        four[1],
        grad_router,
        grad_gate,
        grad_up,
        grad_down,
    )


def solution(mesh):
    wide, narrow = mesh.shape["wide"], mesh.shape["narrow"]
    near = 2
    middle = min(wide // near, 4)
    inner = Mesh(mesh.devices.reshape(wide // (near * middle), middle, near, narrow // 2, 2), ALL)
    both = P(WIDE, NARROW)
    cube = P(WIDE, None, NARROW)
    lane = P(NARROW)
    row = P(WIDE, None)
    return jax.shard_map(
        per_device,
        mesh=inner,
        in_specs=(
            both, both, row, row, lane, both, both, both, lane, lane, both, lane, P(),
            cube, cube, cube,
        ),
        out_specs=(
            both, both, lane, both, both, both, lane, lane, both, lane, P(), cube, cube, cube,
        ),
        check_vma=False,
    )
```

```python
import functools

import jax
import jax.numpy as jnp
from jax import lax
from jax.experimental import pallas as pl
from jax.experimental.pallas import tpu as pltpu
from jax.sharding import Mesh
from jax.sharding import PartitionSpec as P

HD = 128
EPS = 1e-05
WIDE = ("t", "g", "p")
NARROW = ("y", "c")
GROUP = ("g", "p", "c")
ALL = ("t", "g", "p", "y", "c")
BF = jnp.bfloat16
F32 = jnp.float32
ROWS = 1024
COLS = 256
WIDE_COLS = 512
COST = pl.CostEstimate(flops=1000, transcendentals=0, bytes_accessed=1000)


def rms_scale(values, scales):
    return values * lax.rsqrt(jnp.mean(values * values, axis=-1, keepdims=True) + EPS) * scales


def rope_tables(length, head_dim):
    exponent = jnp.arange(0, head_dim, 2, dtype=F32) / head_dim
    angles = jnp.arange(length, dtype=F32)[:, None] * (10000.0 ** (-exponent))[None, :]
    cosines, sines = jnp.cos(angles), jnp.sin(angles)
    return (
        jnp.concatenate([cosines, cosines], axis=-1),
        jnp.concatenate([-sines, sines], axis=-1),
    )


def dot(a, b, contract):
    return lax.dot_general(a, b, (contract, ((), ())), preferred_element_type=F32)


def place_of(array):
    large = array.size * array.dtype.itemsize > 1 << 20
    return pl.BlockSpec(memory_space=pltpu.HBM if large else pl.ANY)


def call(body, outs, scratch, args, flops, vmem, moved):
    return pl.pallas_call(
        body,
        out_shape=outs,
        in_specs=[place_of(a) for a in args],
        out_specs=jax.tree.map(lambda _: pl.BlockSpec(memory_space=pl.ANY), outs),
        scratch_shapes=scratch,
        compiler_params=pltpu.CompilerParams(vmem_limit_bytes=vmem << 20),
        cost_estimate=COST,
    )(*args)


def start_all(copies):
    for one in copies:
        one.start()
    return copies


def wait_all(copies):
    for one in copies:
        one.wait()


def weight_copies(pieces, whole, sems, stride=1, at=0):
    units = pieces[0].shape[3]
    copies = []
    for half, piece in enumerate(pieces):
        for c in range(2):
            k = half * 2 + c
            there = pl.ds((k * stride + at) * units, units)
            copies.append(
                pltpu.make_async_copy(piece.at[:, c], whole.at[:, :, there], sems.at[k])
            )
    return copies


def block_copies(blocks, whole, sems):
    rows = blocks[0].shape[0]
    return [
        pltpu.make_async_copy(b, whole.at[pl.ds(i * rows, rows)], sems.at[i])
        for i, b in enumerate(blocks)
    ]


def arrived(view, sem):
    pltpu.make_async_copy(view, view, sem).wait()


def await_weight(whole, sems, k, now):
    units = whole.shape[2] // 4

    @pl.when(now)
    def _():
        arrived(whole.at[:, :, pl.ds(pl.multiple_of(k * units, units), units)], sems.at[k])


def await_rows(whole, sems, count, r):
    rows = whole.shape[0] // count
    each = max(1, ROWS // rows)
    if rows <= ROWS:
        for i in range(each):
            b = r * each + i
            arrived(whole.at[pl.ds(pl.multiple_of(b * rows, rows), rows)], sems.at[b])
    else:

        @pl.when(r % (rows // ROWS) == 0)
        def _():
            b = r // (rows // ROWS)
            arrived(whole.at[pl.ds(pl.multiple_of(b * rows, rows), rows)], sems.at[b])


def to_column(line):
    return jnp.transpose(jnp.broadcast_to(line, (128, 128)))


def to_line(column):
    return jnp.transpose(jnp.broadcast_to(column, (128, 128)))[:1]


def take(ref, k, size=COLS):
    part = ref[:, :, pl.ds(pl.multiple_of(k * size, size), size)]
    return part.reshape(-1, size)


def take_rows(ref, n, size=COLS):
    each = size // ref.shape[1]
    return ref[pl.ds(n * each, each)].reshape(size, ref.shape[2])


def project_body(count, *refs):
    blocks, pieces, out = refs[:count], refs[count : count + 2], refs[count + 2]
    rows_v, weight_v, out_v, sem_b, sem_w, sem_o = refs[count + 3 :]
    cw = weight_copies(pieces, weight_v, sem_w)
    cb = block_copies(blocks, rows_v, sem_b)
    ahead = max(1, count * ROWS // rows_v.shape[0])
    start_all(cb[:ahead] + cw + cb[ahead:])
    steps = rows_v.shape[0] // ROWS

    def row_step(r, carry):
        here = pl.ds(pl.multiple_of(r * ROWS, ROWS), ROWS)
        await_rows(rows_v, sem_b, count, r)

        def col_step(k, carry):
            for n in range(WIDE_COLS // COLS):
                await_weight(weight_v, sem_w, k * (WIDE_COLS // COLS) + n, r == 0)
            cols = pl.ds(pl.multiple_of(k * WIDE_COLS, WIDE_COLS), WIDE_COLS)
            got = dot(rows_v[here, :], take(weight_v, k, WIDE_COLS), ((1,), (0,)))
            out_v[here, cols] = got.astype(BF)
            return carry

        lax.fori_loop(0, out_v.shape[1] // WIDE_COLS, col_step, 0)
        pltpu.make_async_copy(out_v.at[here], out.at[here], sem_o.at[r]).start()
        return carry

    lax.fori_loop(0, steps, row_step, 0)
    for r in range(steps):
        here = pl.ds(r * ROWS, ROWS)
        pltpu.make_async_copy(out_v.at[here], out.at[here], sem_o.at[r]).wait()


def project(blocks, got, other):
    rows = blocks[0].shape[0] * len(blocks)
    model = blocks[0].shape[1]
    w, _, depth, units = got.shape
    hidden = 4 * units
    return call(
        functools.partial(project_body, len(blocks)),
        jax.ShapeDtypeStruct((rows, hidden), BF),
        [
            pltpu.VMEM((rows, model), BF),
            pltpu.VMEM((w, depth, hidden), BF),
            pltpu.VMEM((rows, hidden), BF),
            pltpu.SemaphoreType.DMA((len(blocks),)),
            pltpu.SemaphoreType.DMA((4,)),
            pltpu.SemaphoreType.DMA((rows // ROWS,)),
        ],
        (*blocks, got, other),
        2 * rows * model * hidden,
        40,
        2 * (rows * model + model * hidden + rows * hidden),
    )


def expert_body(count, *refs):
    blocks = refs[:count]
    gate_p, up_p = refs[count : count + 2], refs[count + 2 : count + 4]
    down_grad, own_gate = refs[count + 4 : count + 6]
    gg, ug, hs, dots = refs[count + 6 : count + 10]
    rows_v, pair_v, grad_v, own_v, gg_v, ug_v, hs_v, dots_v = refs[count + 10 : count + 18]
    own_c, pair_a, pair_b, sem_b, sem_w, sem_i, sem_o = refs[count + 18 :]
    ci = start_all(
        [
            pltpu.make_async_copy(down_grad, grad_v, sem_i.at[0]),
            pltpu.make_async_copy(own_gate, own_v, sem_i.at[1]),
        ]
    )
    cg = weight_copies(gate_p, pair_v, sem_w.at[0], 2, 0)
    cu = weight_copies(up_p, pair_v, sem_w.at[1], 2, 1)
    cb = block_copies(blocks, rows_v, sem_b)
    ahead = max(1, count * ROWS // rows_v.shape[0])
    start_all(cb[:ahead] + [c for two in zip(cg, cu) for c in two] + cb[ahead:])
    wait_all(ci)
    steps = rows_v.shape[0] // ROWS
    lines = ROWS // 128
    outs = ((gg_v, gg, 0), (ug_v, ug, 1), (hs_v, hs, 2))
    chunks = gg_v.shape[1] // COLS
    for i in range(own_v.shape[0]):
        own_c[i * 128 : (i + 1) * 128, :] = to_column(own_v[i : i + 1, :])

    def ready(i):
        k = i % chunks

        @pl.when(k == 0)
        def _():
            await_rows(rows_v, sem_b, count, i // chunks)

        @pl.when(i < chunks)
        def _():
            for n in range(2):
                there = pl.ds(pl.multiple_of((2 * k + n) * COLS, COLS), COLS)
                arrived(pair_v.at[:, :, there], sem_w.at[n, k])

    def rows_at(i):
        return pl.ds(pl.multiple_of((i // chunks) * ROWS, ROWS), ROWS)

    def products(i, pair_s):
        pair_s[...] = dot(
            rows_v[rows_at(i), :], take(pair_v, i % chunks, 2 * COLS), ((1,), (0,))
        )

    def activate(i, pair_s, total):
        here, k = rows_at(i), i % chunks
        cols = pl.ds(pl.multiple_of(k * COLS, COLS), COLS)
        own = own_c[here, :1]
        gate, up = pair_s[:, :COLS], pair_s[:, COLS:]
        grad = grad_v[here, cols].astype(F32)
        sig = 1.0 / (1.0 + jnp.exp(-gate))
        act = gate * sig
        hidden = act * up
        hs_v[here, cols] = (own * hidden).astype(BF)
        part = jnp.sum(hidden * grad, axis=1, keepdims=True)
        grad = own * grad
        gg_v[here, cols] = (grad * up * (sig + act * (1.0 - sig))).astype(BF)
        ug_v[here, cols] = (grad * act).astype(BF)
        return jnp.where(k == 0, 0.0, total) + part

    ready(0)
    products(0, pair_a)
    most = steps * chunks - 1

    def step(j, total):
        i = 2 * j
        ready(i + 1)
        after_next = jnp.minimum(i + 2, most)

        @pl.when(i + 2 <= most)
        def _():
            ready(i + 2)

        products(i + 1, pair_b)
        total = activate(i, pair_a, total)
        products(after_next, pair_a)
        total = activate(i + 1, pair_b, total)

        @pl.when((i + 1) % chunks == chunks - 1)
        def _():
            r = i // chunks
            dots_v[pl.ds(pl.multiple_of(r * lines, lines), lines), :] = jnp.concatenate(
                [to_line(total[n * 128 : (n + 1) * 128]) for n in range(lines)], axis=0
            )
            for src, dst, n in outs:
                here = rows_at(i)
                pltpu.make_async_copy(src.at[here], dst.at[here], sem_o.at[n, r]).start()

        return total

    lax.fori_loop(0, steps * chunks // 2, step, jnp.zeros((ROWS, 1), F32))
    last = pltpu.make_async_copy(dots_v, dots, sem_i.at[2])
    last.start()
    for r in range(steps):
        here = pl.ds(r * ROWS, ROWS)
        for src, dst, i in outs:
            pltpu.make_async_copy(src.at[here], dst.at[here], sem_o.at[i, r]).wait()
    last.wait()


def expert(blocks, gate_p, up_p, down_grad, own_gate):
    rows = blocks[0].shape[0] * len(blocks)
    model = blocks[0].shape[1]
    w, _, depth, units = gate_p[0].shape
    hidden = 4 * units
    steps = rows // ROWS
    out = jax.ShapeDtypeStruct((rows, hidden), BF)
    wide = jax.ShapeDtypeStruct(own_gate.shape, F32)
    return call(
        functools.partial(expert_body, len(blocks)),
        (out, out, out, wide),
        [
            pltpu.VMEM((rows, model), BF),
            pltpu.VMEM((w, depth, 2 * hidden), BF),
            pltpu.VMEM((rows, hidden), BF),
            pltpu.VMEM(own_gate.shape, F32),
            pltpu.VMEM((rows, hidden), BF),
            pltpu.VMEM((rows, hidden), BF),
            pltpu.VMEM((rows, hidden), BF),
            pltpu.VMEM(own_gate.shape, F32),
            pltpu.VMEM((rows, 128), F32),
        ]
        + [pltpu.VMEM((ROWS, 2 * COLS), F32)] * 2
        + [
            pltpu.SemaphoreType.DMA((len(blocks),)),
            pltpu.SemaphoreType.DMA((2, 4)),
            pltpu.SemaphoreType.DMA((3,)),
            pltpu.SemaphoreType.DMA((3, steps)),
        ],
        (*blocks, *gate_p, *up_p, down_grad, own_gate),
        4 * rows * model * hidden,
        56,
        2 * (rows * model + 2 * model * hidden + 4 * rows * hidden),
    )


def back_body(first, pairs, tail, *refs):
    refs = list(refs)
    ins = [refs[3 * i : 3 * i + 3] for i in range(pairs)]
    at = 3 * pairs
    if tail:
        dots, place = refs[at : at + 2]
        at += 2
    out = refs[at]
    scratch = refs[at + 1 :]
    if tail:
        dots_v, place_v, sem_t = scratch[-3:]
        scratch = scratch[:-3]
        side = start_all(
            [
                pltpu.make_async_copy(dots, dots_v, sem_t.at[0]),
                pltpu.make_async_copy(place, place_v, sem_t.at[1]),
            ]
        )
    grads, weights = scratch[:pairs], scratch[pairs : 2 * pairs]
    out_v, sem_g, sem_w, sem_o = scratch[2 * pairs :]
    rows = out_v.shape[0]
    each = WIDE_COLS // weights[0].shape[1]
    parts = weights[0].shape[0] // each
    for i, (grad, got, other) in enumerate(ins):
        pltpu.make_async_copy(grad.at[pl.ds(first, rows)], grads[i], sem_g.at[i]).start()
    for n in range(parts):
        place = pl.ds(n * each, each)
        for i, (grad, got, other) in enumerate(ins):
            pieces = (got.at[place], other.at[place])
            start_all(weight_copies(pieces, weights[i].at[place], sem_w.at[i, n]))
    for i in range(pairs):
        arrived(grads[i], sem_g.at[i])

    def col_step(n, carry):
        for i in range(pairs):
            block = weights[i].at[pl.ds(n * each, each)]
            for k in range(4):
                await_weight(block, sem_w.at[i, n], k, n >= 0)
        cols = pl.ds(pl.multiple_of(n * WIDE_COLS, WIDE_COLS), WIDE_COLS)
        total = dot(grads[0][...], take_rows(weights[0], n, WIDE_COLS), ((1,), (1,)))
        for i in range(1, pairs):
            total += dot(grads[i][...], take_rows(weights[i], n, WIDE_COLS), ((1,), (1,)))
        out_v[:, cols] = total.astype(BF)
        pltpu.make_async_copy(out_v.at[:, cols], out.at[:, cols], sem_o.at[n]).start()
        return carry

    if tail:
        wait_all(side)
        cols = pl.ds(parts * WIDE_COLS, 128)
        for i in range(rows // 128):
            line = dots_v[first // 128 + i : first // 128 + i + 1, :]
            value = (to_column(line) * place_v[...]).astype(BF)
            out_v[i * 128 : (i + 1) * 128, parts * WIDE_COLS :] = value
        last = pltpu.make_async_copy(out_v.at[:, cols], out.at[:, cols], sem_o.at[parts])
        last.start()
    lax.fori_loop(0, parts, col_step, 0)
    for n in range(parts):
        cols = pl.ds(n * WIDE_COLS, WIDE_COLS)
        pltpu.make_async_copy(out_v.at[:, cols], out.at[:, cols], sem_o.at[n]).wait()
    if tail:
        last.wait()


def back(triples, first, rows, tail=()):
    w, _, depth, units = triples[0][1].shape
    model, hidden = w * depth, 4 * units
    n = len(triples)
    full = model + 128 if tail else model
    return call(
        functools.partial(back_body, first, n, bool(tail)),
        jax.ShapeDtypeStruct((rows, full), BF),
        [pltpu.VMEM((rows, hidden), BF)] * n
        + [pltpu.VMEM((w, depth, hidden), BF)] * n
        + [
            pltpu.VMEM((rows, full), BF),
            pltpu.SemaphoreType.DMA((n,)),
            pltpu.SemaphoreType.DMA((n, model // WIDE_COLS, 4)),
            pltpu.SemaphoreType.DMA((model // WIDE_COLS + 1,)),
        ]
        + [pltpu.VMEM(t.shape, F32) for t in tail]
        + [pltpu.SemaphoreType.DMA((2,))] * bool(tail),
        [a for t in triples for a in t] + list(tail),
        2 * n * rows * model * hidden,
        40,
        2 * (n * rows * hidden + n * model * hidden + rows * model),
    )


def weight_body(count, depth, *refs):
    blocks, grad, mine, theirs = refs[:count], refs[count], refs[count + 1], refs[count + 2]
    rows_v, grad_v, out_v, sem_b, sem_g, sem_o = refs[count + 3 :]
    cg = pltpu.make_async_copy(grad, grad_v, sem_g.at[0])
    wait_all(start_all(block_copies(blocks, rows_v, sem_b) + [cg]))
    units = COLS
    each = COLS // depth
    steps = rows_v.shape[1] // COLS

    def step(n, carry):
        cols = pl.ds(pl.multiple_of(n * COLS, COLS), COLS)
        got = dot(rows_v[:, cols], grad_v[...], ((0,), (0,))).astype(BF)
        for k in range(4):
            part = got[:, k * units : (k + 1) * units].reshape(each, depth, units)
            out_v[k // 2, pl.ds(n * each, each), k % 2] = part
        place = pl.ds(n * each, each)
        pltpu.make_async_copy(out_v.at[0, place], mine.at[place], sem_o.at[0, n]).start()
        pltpu.make_async_copy(out_v.at[1, place], theirs.at[place], sem_o.at[1, n]).start()
        return carry

    lax.fori_loop(0, steps, step, 0)
    for n in range(steps):
        place = pl.ds(n * each, each)
        pltpu.make_async_copy(out_v.at[0, place], mine.at[place], sem_o.at[0, n]).wait()
        pltpu.make_async_copy(out_v.at[1, place], theirs.at[place], sem_o.at[1, n]).wait()


def weight_grad(blocks, grad, depth):
    rows = blocks[0].shape[0] * len(blocks)
    model = blocks[0].shape[1]
    hidden = grad.shape[1]
    w = model // depth
    piece = jax.ShapeDtypeStruct((w, 2, depth, hidden // 4), BF)
    steps = model // COLS
    return call(
        functools.partial(weight_body, len(blocks), depth),
        (piece, piece),
        [
            pltpu.VMEM((rows, model), BF),
            pltpu.VMEM((rows, hidden), BF),
            pltpu.VMEM((2, w, 2, depth, hidden // 4), BF),
            pltpu.SemaphoreType.DMA((len(blocks),)),
            pltpu.SemaphoreType.DMA((1,)),
            pltpu.SemaphoreType.DMA((2, steps)),
        ],
        (*blocks, grad),
        2 * rows * model * hidden,
        40,
        2 * (rows * model + model * hidden + rows * hidden),
    )


def terms_body(pairs, *refs):
    ins, me, outs = refs[: 2 * pairs], refs[2 * pairs], refs[2 * pairs + 1 : 2 * pairs + 3]
    scratch = refs[2 * pairs + 3 :]
    held, out_v, sems, out_sem = scratch[: 2 * pairs], scratch[-3], scratch[-2], scratch[-1]
    wait_all(
        start_all(
            [pltpu.make_async_copy(ins[i], held[i], sems.at[i]) for i in range(2 * pairs)]
        )
    )
    _, count, _, depth, _ = out_v.shape
    mine = me[0]

    each = COLS // depth

    def step(n, carry):
        rows = pl.ds(pl.multiple_of(n * COLS, COLS), COLS)
        at = 0
        for i in range(pairs):
            wide = held[2 * i + 1].shape[1]
            got = dot(held[2 * i][:, rows], held[2 * i + 1][...], ((0,), (0,))).astype(BF)
            for j in range(each):
                b = n * each + j
                distance = jnp.bitwise_xor(b % 8, mine)
                half = distance % 2
                far = distance // 2
                place = (far % 2) * 2 + far // 2
                out_v[half, b // 8, place, :, at : at + wide] = got[j * depth : (j + 1) * depth]
            at += wide
        return carry

    lax.fori_loop(0, count * 8 // each, step, 0)
    wait_all(
        start_all([pltpu.make_async_copy(out_v.at[i], outs[i], out_sem.at[i]) for i in range(2)])
    )


def block_terms(pairs, me, depth):
    length, model = pairs[0][0].shape
    count = model // (8 * depth)
    n = sum(c.shape[1] for _, c in pairs)
    piece = jax.ShapeDtypeStruct((count, 4, depth, n), BF)
    flat = [x for two in pairs for x in two]
    return pl.pallas_call(
        functools.partial(terms_body, len(pairs)),
        out_shape=(piece, piece),
        in_specs=[place_of(a) for a in flat]
        + [pl.BlockSpec(memory_space=pltpu.SMEM)],
        out_specs=(pl.BlockSpec(memory_space=pl.ANY),) * 2,
        scratch_shapes=[pltpu.VMEM(x.shape, BF) for x in flat]
        + [
            pltpu.VMEM((2,) + piece.shape, BF),
            pltpu.SemaphoreType.DMA((len(flat),)),
            pltpu.SemaphoreType.DMA((2,)),
        ],
        compiler_params=pltpu.CompilerParams(vmem_limit_bytes=24 << 20),
        cost_estimate=COST,
    )(*flat, me)


def to_columns(line):
    return jnp.concatenate(
        [to_column(line[:, i : i + 128])[:, :1] for i in range(0, line.shape[1], 128)], axis=0
    )


def to_lines(column):
    return jnp.concatenate(
        [to_line(column[i : i + 128]) for i in range(0, column.shape[0], 128)], axis=1
    )


def bring(ins, held, sems):
    wait_all(
        start_all([pltpu.make_async_copy(a, b, sems.at[i]) for i, (a, b) in enumerate(zip(ins, held))])
    )


def send_out(held, outs, sems):
    wait_all(
        start_all([pltpu.make_async_copy(a, b, sems.at[i]) for i, (a, b) in enumerate(zip(held, outs))])
    )


def raw_body(normed, weights, query, key, value, squares, *scratch):
    normed_v, weights_v, query_v, key_v, value_v, squares_v, sem_i, sem_o = scratch
    wide = query_v.shape[1]
    bring((normed, weights.at[:, pl.ds(0, 3 * wide)]), (normed_v, weights_v), sem_i)
    length = query_v.shape[0]
    for place, ref in ((0, query_v), (1, key_v)):

        def step(j, total):
            cols = pl.ds(pl.multiple_of(j * COLS, COLS), COLS)
            w = weights_v[:, pl.ds(pl.multiple_of(place * wide + j * COLS, COLS), COLS)]
            got = dot(normed_v[...], w, ((1,), (0,)))
            ref[:, cols] = got
            return total + jnp.sum(got * got, axis=1, keepdims=True)

        total = lax.fori_loop(0, wide // COLS, step, jnp.zeros((length, 1), F32))
        squares_v[place : place + 1, :] = to_lines(total)

    def step(j, carry):
        cols = pl.ds(pl.multiple_of(j * COLS, COLS), COLS)
        w = weights_v[:, pl.ds(pl.multiple_of(2 * wide + j * COLS, COLS), COLS)]
        value_v[:, cols] = dot(normed_v[...], w, ((1,), (0,))).astype(BF)
        return carry

    lax.fori_loop(0, wide // COLS, step, 0)
    send_out((query_v, key_v, value_v, squares_v), (query, key, value, squares), sem_o)


def raw_heads(normed, weights, wide):
    length, model = normed.shape
    shapes = [((length, wide), F32), ((length, wide), F32), ((length, wide), BF), ((2, length), F32)]
    return call(
        raw_body,
        tuple(jax.ShapeDtypeStruct(*one) for one in shapes),
        [pltpu.VMEM((length, model), BF), pltpu.VMEM((model, 3 * wide), BF)]
        + [pltpu.VMEM(*one) for one in shapes]
        + [pltpu.SemaphoreType.DMA((2,)), pltpu.SemaphoreType.DMA((4,))],
        (normed, weights),
        0,
        58,
        0,
    )


def half_turn(values):
    return pltpu.roll(values, HD // 2, 1)


def attend_body(*refs):
    ins, outs, scratch = refs[:10], refs[10:15], refs[15:]
    held, made, sem_i, sem_o = scratch[:10], scratch[10:15], scratch[15], scratch[16]
    query, key, value, scales, gains, cosines, sines, ids, weights = ins[:9]
    wide = query.shape[1]
    views = list(ins[:9])
    views[8] = weights.at[:, pl.ds(3 * wide, wide)]
    bring(views, held[:9], sem_i)
    query_v, key_v, value_v, scales_v, gains_v, cos_v, sin_v, ids_v, weights_v = held[:9]
    query_o, key_o, attended_o, log_o, out_o = made
    line = ids_v[...]
    allowed = line <= to_columns(line)
    scale_q, scale_k = to_columns(scales_v[0:1, :]), to_columns(scales_v[1:2, :])

    def step(h, carry):
        cols = pl.ds(pl.multiple_of(h * HD, HD), HD)
        cosines, sines = cos_v[...], sin_v[...]
        q = query_v[:, cols] * scale_q * gains_v[0:1, cols]
        k = key_v[:, cols] * scale_k * gains_v[1:2, cols]
        q = (q * cosines + half_turn(q) * sines).astype(BF)
        k = (k * cosines + half_turn(k) * sines).astype(BF)
        query_o[:, cols] = q
        key_o[:, cols] = k
        scores = jnp.where(allowed, dot(q, k, ((1,), (1,))) * HD**-0.5, -1e30)
        highest = jnp.max(scores, axis=1, keepdims=True)
        shifted = jnp.exp(scores - highest)
        totals = jnp.sum(shifted, axis=1, keepdims=True)
        probs = (shifted / totals).astype(BF)
        attended_o[:, cols] = dot(probs, value_v[:, cols], ((1,), (0,))).astype(BF)
        log_o[pl.ds(h, 1), :] = to_lines(highest + jnp.log(totals))
        return carry

    lax.fori_loop(0, wide // HD, step, 0)

    def out_step(j, carry):
        cols = pl.ds(pl.multiple_of(j * COLS, COLS), COLS)
        out_o[:, cols] = dot(attended_o[...], weights_v[cols, :], ((1,), (1,))).astype(BF)
        return carry

    lax.fori_loop(0, out_o.shape[1] // COLS, out_step, 0)
    send_out(made, outs, sem_o)


def attend(query, key, value, scales, gains, tables, ids, weights):
    length, wide = query.shape
    model = weights.shape[0]
    args = (query, key, value, scales, gains, *tables, ids, weights, ids)
    held = [pltpu.VMEM(x.shape, x.dtype) for x in args[:8]]
    held += [pltpu.VMEM((model, wide), BF), pltpu.VMEM(ids.shape, ids.dtype)]
    shapes = [
        ((length, wide), BF),
        ((length, wide), BF),
        ((length, wide), BF),
        ((wide // HD, length), F32),
        ((length, model), BF),
    ]
    return call(
        attend_body,
        tuple(jax.ShapeDtypeStruct(*one) for one in shapes),
        held
        + [pltpu.VMEM(*one) for one in shapes]
        + [pltpu.SemaphoreType.DMA((9,)), pltpu.SemaphoreType.DMA((5,))],
        args,
        0,
        58,
        0,
    )


def unattend_body(*refs):
    ins, outs, scratch = refs[:12], refs[12:16], refs[16:]
    held, grad_v, made, sem_i, sem_o = (
        scratch[:12], scratch[12], scratch[13:17], scratch[17], scratch[18],
    )
    wide = ins[2].shape[1]
    views = list(ins)
    views[1] = ins[1].at[:, pl.ds(3 * wide, wide)]
    bring(views, held, sem_i)
    cot_v, weights_v, query_v, key_v, value_v, log_v, ids_v, cos_v, sin_v, gains_v, raw_q, raw_k = held
    query_o, key_o, value_o, dots_o = made
    grad_v[...] = dot(cot_v[...], weights_v[...], ((1,), (0,))).astype(BF)
    line = ids_v[...]
    allowed = line <= to_columns(line)
    length = cot_v.shape[0]
    zero = jnp.zeros((length, 1), F32)

    def step(h, carry):
        dot_q, dot_k = carry
        cols = pl.ds(pl.multiple_of(h * HD, HD), HD)
        cosines, sines = cos_v[...], sin_v[...]
        q, k, v, grad = query_v[:, cols], key_v[:, cols], value_v[:, cols], grad_v[:, cols]
        scores = jnp.where(allowed, dot(q, k, ((1,), (1,))) * HD**-0.5, -1e30)
        probs = jnp.exp(scores - to_columns(log_v[pl.ds(h, 1), :]))
        prob_grad = dot(grad, v, ((1,), (1,)))
        centre = jnp.sum(probs * prob_grad, axis=1, keepdims=True)
        score_grad = (probs * (prob_grad - centre)).astype(BF)
        value_o[:, cols] = dot(probs.astype(BF), grad, ((0,), (0,))).astype(BF)
        back_q = dot(score_grad, k, ((1,), (0,))) * HD**-0.5
        back_k = dot(score_grad, q, ((0,), (0,))) * HD**-0.5
        back_q = back_q * cosines + half_turn(back_q * sines)
        back_k = back_k * cosines + half_turn(back_k * sines)
        query_o[:, cols] = back_q
        key_o[:, cols] = back_k
        dot_q += jnp.sum(gains_v[0:1, cols] * back_q * raw_q[:, cols], axis=1, keepdims=True)
        dot_k += jnp.sum(gains_v[1:2, cols] * back_k * raw_k[:, cols], axis=1, keepdims=True)
        return dot_q, dot_k

    dot_q, dot_k = lax.fori_loop(0, wide // HD, step, (zero, zero))
    dots_o[0:1, :] = to_lines(dot_q)
    dots_o[1:2, :] = to_lines(dot_k)
    send_out(made, outs, sem_o)


def unattend(out_cot, weights, query, key, value, logs, ids, tables, gains, raw_q, raw_k):
    length, wide = query.shape
    args = (out_cot, weights, query, key, value, logs, ids, *tables, gains, raw_q, raw_k)
    held = [pltpu.VMEM(x.shape, x.dtype) for x in args]
    held[1] = pltpu.VMEM((weights.shape[0], wide), BF)
    shapes = [((length, wide), F32), ((length, wide), F32), ((length, wide), BF), ((2, length), F32)]
    return call(
        unattend_body,
        tuple(jax.ShapeDtypeStruct(*one) for one in shapes),
        held
        + [pltpu.VMEM((length, wide), BF)]
        + [pltpu.VMEM(*one) for one in shapes]
        + [pltpu.SemaphoreType.DMA((12,)), pltpu.SemaphoreType.DMA((4,))],
        args,
        0,
        58,
        0,
    )


def unnorm_body(*refs):
    ins, outs, scratch = refs[:7], refs[7:9], refs[9:]
    held, made, sem_i, sem_o = scratch[:7], scratch[7:9], scratch[9], scratch[10]
    bring(ins, held, sem_i)
    back_q, back_k, raw_q, raw_k, scales_v, dots_v, gains_v = held
    grads_o, gains_o = made
    wide = raw_q.shape[1]
    for i, (back, raw) in enumerate(((back_q, raw_q), (back_k, raw_k))):
        scale = to_columns(scales_v[i : i + 1, :])
        push = to_columns(dots_v[i : i + 1, :]) * scale * scale * scale
        grad = scale * gains_v[i : i + 1, :] * back[...] - raw[...] * push
        grads_o[:, i * wide : (i + 1) * wide] = grad.astype(BF)
        gains_o[i : i + 1, :] = jnp.sum(back[...] * raw[...] * scale, axis=0, keepdims=True)
    send_out(made, outs, sem_o)


def unnorm(back_q, back_k, raw_q, raw_k, scales, dots, gains):
    length, wide = raw_q.shape
    args = (back_q, back_k, raw_q, raw_k, scales, dots, gains)
    shapes = [((length, 2 * wide), BF), ((2, wide), F32)]
    return call(
        unnorm_body,
        tuple(jax.ShapeDtypeStruct(*one) for one in shapes),
        [pltpu.VMEM(x.shape, x.dtype) for x in args]
        + [pltpu.VMEM(*one) for one in shapes]
        + [pltpu.SemaphoreType.DMA((7,)), pltpu.SemaphoreType.DMA((2,))],
        args,
        0,
        24,
        0,
    )


def after(values, *earlier):
    return lax.optimization_barrier((values, earlier))[0]


def stage(*values):
    return lax.optimization_barrier(values)


def swap(values, axis, step=1):
    count = lax.axis_size(axis)
    return lax.ppermute(values, axis, [(i, i ^ step) for i in range(count)])


def gather_four(block, axis):
    count = lax.axis_size("y") * lax.axis_size("c")
    size = block.shape[axis]
    here = lax.axis_index("y") * lax.axis_size("c") + lax.axis_index("c")
    other = swap(block, "y")
    near = swap(block, "c")
    far = swap(other, "c")
    shape = list(block.shape)
    shape[axis] = size * count
    whole = jnp.zeros(shape, block.dtype)
    for piece, place in ((block, 0), (near, 1), (other, 2), (far, 3)):
        whole = lax.dynamic_update_slice_in_dim(whole, piece, (here ^ place) * size, axis)
    return whole


def sum_near(partial):
    length, width = partial.shape
    y, c = lax.axis_index("y"), lax.axis_index("c")
    parts = partial.reshape(2, 2, length // 4, width)
    mine = lax.dynamic_index_in_dim(parts, c, 1, False)
    theirs = lax.dynamic_index_in_dim(parts, 1 - c, 1, False)
    mine = mine.astype(F32) + swap(theirs.astype(BF), "c").astype(F32)
    keep = lax.dynamic_index_in_dim(mine, y, 0, False)
    send = lax.dynamic_index_in_dim(mine, 1 - y, 0, False)
    return keep, send.astype(BF)


def add(*pieces):
    total = pieces[0].astype(F32)
    for piece in pieces[1:]:
        total = total + piece.astype(F32)
    return total


def to_experts(columns):
    sent = lax.all_to_all(columns.T, GROUP, 0, 0, tiled=True)
    v = sent.reshape((-1, 2) + sent.shape[1:])
    c = lax.axis_index("c")
    own = lax.dynamic_index_in_dim(v, c, 1, False)
    other = lax.dynamic_index_in_dim(v, 1 - c, 1, False)
    return jnp.concatenate([own, other]).reshape(sent.shape[0], -1)


def to_group(weight):
    got = lax.all_to_all(weight, GROUP, 0, 0, tiled=True)
    return got.reshape((got.shape[0] // 2, 2) + got.shape[1:])


def over_sequences(*terms):
    if lax.axis_size("t") > 1:
        terms = [lax.psum_scatter(x, "t", scatter_dimension=0, tiled=True) for x in terms]
    return [x[0] for x in terms]


def over_groups(piece):
    if lax.axis_size("t") > 1:
        piece = lax.all_gather(piece, "t", axis=0, tiled=True)
    return piece


def sum_over(values, axis):
    step = 1
    while step < lax.axis_size(axis):
        values = values + swap(values, axis, step)
        step *= 2
    return values


def to_slices(mine, theirs):
    total = (mine.astype(F32) + theirs.astype(F32)).astype(BF)
    if lax.axis_size("t") > 1:
        total = lax.psum_scatter(total, "t", scatter_dimension=0, tiled=True)
    sent = total.reshape((-1,) + total.shape[2:])
    return lax.all_to_all(sent, GROUP, 0, 0, tiled=True)


def as_output(got):
    return jnp.transpose(got, (1, 0, 2)).astype(F32)


def per_device(
    tokens,
    cotangent,
    block_ids,
    routes,
    norm_attn,
    w_query,
    w_key,
    w_value,
    norm_query,
    norm_key,
    w_out,
    norm_ffn,
    w_router,
    w_gate,
    w_up,
    w_down,
):
    experts = w_router.shape[1]
    lane_index = lax.axis_index("y") * lax.axis_size("c") + lax.axis_index("c")
    lanes = lax.axis_size("y") * lax.axis_size("c")
    length, head_cols = tokens.shape
    model_width = head_cols * lanes
    rows = length // lanes

    all_full = lax.all_gather(
        jnp.concatenate([w_query, w_key, w_value, w_out], axis=1), WIDE, axis=0, tiled=True
    )

    rows_full = gather_four(tokens, 1)
    gains = lax.all_gather(jnp.stack([norm_attn, norm_ffn]), NARROW, axis=1, tiled=True)
    down_got = to_group(jnp.transpose(w_down, (1, 0, 2)))
    gate_sent = jnp.transpose(w_gate, (1, 0, 2))
    up_sent = jnp.transpose(w_up, (1, 0, 2))
    cot_rows = lax.all_to_all(cotangent.reshape(lanes, rows, head_cols), NARROW, 0, 0, tiled=True)
    cot_rows = jnp.transpose(cot_rows, (1, 0, 2)).reshape(rows, model_width)
    rows_full, cot_rows, gate_sent, up_sent, gains = stage(
        rows_full, cot_rows, gate_sent, up_sent, gains
    )
    attn_gain = gains[0].astype(F32)
    ffn_gain = gains[1].astype(F32)
    rows_float = rows_full.astype(F32)
    normed = rms_scale(rows_float, attn_gain).astype(BF)
    down_got, gate_sent, normed, cot_sent = stage(down_got, gate_sent, normed, cot_rows)

    down_other = swap(down_got, "y")
    all_full, normed, cot_sent, gate_sent, down_other = stage(
        all_full, normed, cot_sent, gate_sent, down_other
    )

    gate_got = to_group(gate_sent)
    cot_mine = lax.all_gather(cot_sent, ("g", "p"), axis=0, tiled=True)
    qkv_full = all_full[:, : 3 * head_cols]
    raw_query, raw_key, value_bf, squares = raw_heads(normed, all_full, head_cols)
    scales = lax.rsqrt(lax.psum(squares, NARROW) / model_width + EPS)
    scales, gate_got, up_sent = stage(scales, gate_got, up_sent)
    up_got = to_group(up_sent)
    cut = gate_got.shape[0] // 2
    gate_first = swap(gate_got[:cut], "y")
    gains_here = jnp.stack([norm_query, norm_key]).astype(F32)
    tables = rope_tables(length, HD)
    ids = block_ids.astype(F32)
    query_bf, key_bf, attended, log_totals, out_partial = attend(
        raw_query, raw_key, value_bf, scales, gains_here, tables, ids, all_full
    )

    first_row = lane_index * rows
    x_rows = lax.dynamic_slice_in_dim(rows_full, first_row, rows, 0).astype(F32)
    keep, send = sum_near(out_partial)
    keep, send, gate_first = stage(keep, send, gate_first)
    residual = x_rows + keep + swap(send, "y").astype(F32)
    ffn_in = rms_scale(residual, ffn_gain).astype(BF)
    ffn_in, up_got, gate_got, cot_mine = stage(ffn_in, up_got, gate_got, cot_mine)

    up_other = swap(up_got, "y")
    gate_last = swap(gate_got[cut:], "y")
    x_mine = lax.all_gather(ffn_in, ("g", "p"), axis=0, tiled=True)
    cot_all = [cot_mine, swap(cot_mine, "c")]
    down_own = (over_groups(down_got), over_groups(down_other))
    down_grad = project(cot_all, *down_own)
    logits = jnp.dot(ffn_in, w_router, preferred_element_type=F32)
    gate_probs = jax.nn.softmax(logits, axis=-1)
    routes_rows = lax.dynamic_slice_in_dim(routes, first_row, rows, 0)
    chosen = jnp.any(
        routes_rows[:, :, None] == jnp.arange(experts, dtype=jnp.int32)[None, None, :], axis=1
    )
    own_gate = to_experts(jnp.where(chosen, gate_probs, 0.0))
    x_mine, down_grad, own_gate, up_other, gate_last = stage(
        x_mine, down_grad, own_gate, up_other, gate_last
    )
    gate_other = jnp.concatenate([gate_first, gate_last])
    x_all = [x_mine, swap(x_mine, "c")]
    gate_own = (over_groups(gate_got), over_groups(gate_other))
    up_own = (over_groups(up_got), over_groups(up_other))

    gate_grad, up_grad, hidden_gated, own_dots = expert(
        x_all, gate_own, up_own, down_grad, own_gate
    )
    half = gate_grad.shape[0] // 2
    own_index = lax.axis_index("g") * 4 + lax.axis_index("p") * 2 + lax.axis_index("c")
    depth = down_own[0].shape[2]
    own_place = (jnp.arange(128) == own_index).astype(F32)[None]
    depth = down_own[0].shape[2]
    pairs = ((gate_grad, *gate_own), (up_grad, *up_own))
    theirs = back(pairs, half, half, (own_dots, own_place))
    gate_grad, up_grad, own_dots, theirs = stage(gate_grad, up_grad, own_dots, theirs)
    pairs = ((gate_grad, *gate_own), (up_grad, *up_own))
    mine = back(pairs, 0, half, (own_dots, own_place))
    sent = add(mine, swap(theirs, "c")).astype(BF)
    sent, hidden_gated, gate_grad, up_grad = stage(sent, hidden_gated, gate_grad, up_grad)

    input_sum = lax.psum_scatter(sent, ("g", "p"), scatter_dimension=0, tiled=True)
    down_mine, down_theirs = weight_grad(cot_all, hidden_gated, depth)
    down_theirs, gate_grad, hidden_gated, up_grad = stage(
        down_theirs, gate_grad, hidden_gated, up_grad
    )
    down_theirs = swap(down_theirs, "y")
    gate_mine, gate_theirs = weight_grad(x_all, gate_grad, depth)
    up_mine, up_theirs = weight_grad(x_all, up_grad, depth)
    moe_pair = ((hidden_gated, *down_own),)
    moe_theirs = back(moe_pair, half, half)
    moe_mine = back(moe_pair, 0, half)
    down_theirs, gate_theirs, up_theirs, moe_theirs, moe_mine = stage(
        down_theirs, gate_theirs, up_theirs, moe_theirs, moe_mine
    )
    cut = gate_theirs.shape[0] // 2
    gate_first = swap(gate_theirs[:cut], "y")
    down_got = to_slices(down_mine, down_theirs)
    moe_sent = add(moe_mine, swap(moe_theirs, "c")).astype(BF)
    input_sum, moe_sent, gate_first = stage(input_sum, moe_sent, gate_first)
    moe_sum = lax.psum_scatter(moe_sent, ("g", "p"), scatter_dimension=0, tiled=True)
    input_sum = input_sum.astype(F32)
    pair_dots = jnp.where(chosen, input_sum[:, model_width : model_width + experts], 0.0)
    input_sum = input_sum[:, :model_width]

    logit_grad = (
        gate_probs * (pair_dots - jnp.sum(gate_probs * pair_dots, axis=1, keepdims=True))
    ).astype(BF)
    ffn_grad = input_sum + dot(logit_grad, w_router, ((1,), (1,)))
    router_grad = dot(logit_grad, ffn_in, ((0,), (0,)))
    _, ffn_norm_pull = jax.vjp(rms_scale, residual, ffn_gain)
    residual_norm_grad, ffn_gain_grad = ffn_norm_pull(ffn_grad)
    residual_grad = cot_rows.astype(F32) + residual_norm_grad
    out_cot = gather_four(residual_grad.astype(BF), 0)
    out_cot, up_theirs, down_got, gate_theirs = stage(out_cot, up_theirs, down_got, gate_theirs)

    gate_last = swap(gate_theirs[cut:], "y")
    back_query, back_key, value_grad, dots = unattend(
        out_cot, all_full, query_bf, key_bf, value_bf, log_totals, ids, tables, gains_here,
        raw_query, raw_key,
    )
    group_index = (lax.axis_index("g") * 2 + lax.axis_index("p")).astype(jnp.int32)[None]
    two_keep, two_near = over_sequences(
        *block_terms(((out_cot, attended), (normed, value_grad)), group_index, depth)
    )
    dots, two_near, two_keep, gate_last = stage(dots, two_near, two_keep, gate_last)
    gate_got = to_slices(gate_mine, jnp.concatenate([gate_first, gate_last]))
    two_near = swap(two_near, "p")
    dots = lax.psum(dots, NARROW) / model_width
    dots, up_theirs = stage(dots, up_theirs)

    up_theirs = swap(up_theirs, "y")
    pair_pre, pair_gains = unnorm(
        back_query, back_key, raw_query, raw_key, scales, dots, gains_here
    )
    qkv_grad = jnp.concatenate([pair_pre, value_grad], axis=1)
    pair_keep, pair_near = over_sequences(*block_terms(((normed, pair_pre),), group_index, depth))
    qkv_grad, pair_keep, pair_near = stage(qkv_grad, pair_keep, pair_near)
    pair_near = swap(pair_near, "p")
    keep, send = sum_near(dot(qkv_grad, qkv_full, ((1,), (1,))))
    keep, send, up_theirs, gate_got = stage(keep, send, up_theirs, gate_got)
    up_got = to_slices(up_mine, up_theirs)
    send = swap(send, "y")
    send, two_near, two_keep = stage(send, two_near, two_keep)
    normed_grad = add(keep, send)
    two_parts = add(two_keep, two_near)
    two_far = swap(two_parts[2:].astype(BF), "g", 1)
    _, attn_norm_pull = jax.vjp(rms_scale, x_rows, attn_gain)
    rows_norm_grad, attn_gain_grad = attn_norm_pull(normed_grad)
    grad_rows = (residual_grad + rows_norm_grad).astype(BF)
    place = (jnp.arange(lanes) == lane_index).astype(F32)[:, None]
    small = jnp.concatenate(
        [
            router_grad,
            attn_gain_grad[None],
            ffn_gain_grad[None],
            (place * pair_gains[:1]).reshape(1, model_width),
            (place * pair_gains[1:]).reshape(1, model_width),
        ],
        axis=0,
    )
    small = sum_over(small, "g")
    grad_rows, two_far, two_parts, pair_near, pair_keep, small, moe_sum = stage(
        grad_rows, two_far, two_parts, pair_near, pair_keep, small, moe_sum
    )

    pair_parts = add(pair_keep, pair_near)
    pair_far = swap(pair_parts[2:].astype(BF), "g", 1)
    two_parts = add(two_parts[:2], two_far)
    two_far = swap(two_parts[1].astype(BF), "g", 2)
    small = sum_over(sum_over(small, "p"), "t")
    pair_far, pair_parts, two_far, two_parts, small, up_got, grad_rows, moe_sum = stage(
        pair_far, pair_parts, two_far, two_parts, small, up_got, grad_rows, moe_sum
    )

    pair_parts = add(pair_parts[:2], pair_far)
    pair_far = swap(pair_parts[1].astype(BF), "g", 2)
    small = sum_over(sum_over(small, "y"), "c")
    grad_two = add(two_parts[0], two_far)
    both_rows = jnp.stack([(residual + moe_sum.astype(F32)).astype(BF), grad_rows])
    both_rows = jnp.transpose(both_rows.reshape(2, rows, lanes, head_cols), (2, 0, 1, 3))
    both_rows = lax.all_to_all(both_rows, NARROW, 0, 0, tiled=True)
    block_out = both_rows[:, 0].reshape(length, head_cols)
    grad_tokens = both_rows[:, 1].reshape(length, head_cols).astype(F32)
    grad_gate = as_output(gate_got)
    grad_down = as_output(down_got)
    grad_up = as_output(up_got)
    grad_pair = add(pair_parts[0], pair_far)
    grad_out, grad_value = grad_two[:, :head_cols], grad_two[:, head_cols:]
    grad_query, grad_key = grad_pair[:, :head_cols], grad_pair[:, head_cols:]
    grad_router = small[:experts].T
    four = lax.dynamic_slice_in_dim(small[experts:], lane_index * head_cols, head_cols, 1)
    return (
        block_out,
        grad_tokens,
        four[0],
        grad_query.astype(F32),
        grad_key.astype(F32),
        grad_value.astype(F32),
        four[2],
        four[3],
        grad_out.astype(F32),
        four[1],
        grad_router,
        grad_gate,
        grad_up,
        grad_down,
    )


def solution(mesh):
    wide, narrow = mesh.shape["wide"], mesh.shape["narrow"]
    near = 2
    middle = min(wide // near, 4)
    inner = Mesh(mesh.devices.reshape(wide // (near * middle), middle, near, narrow // 2, 2), ALL)
    both = P(WIDE, NARROW)
    cube = P(WIDE, None, NARROW)
    lane = P(NARROW)
    row = P(WIDE, None)
    return jax.shard_map(
        per_device,
        mesh=inner,
        in_specs=(
            both, both, row, row, lane, both, both, both, lane, lane, both, lane, P(),
            cube, cube, cube,
        ),
        out_specs=(
            both, both, lane, both, both, both, lane, lane, both, lane, P(), cube, cube, cube,
        ),
        check_vma=False,
    )
```

```python
import functools

import jax
import jax.numpy as jnp
from jax import lax
from jax.experimental import pallas as pl
from jax.experimental.pallas import tpu as pltpu
from jax.sharding import Mesh
from jax.sharding import PartitionSpec as P

HD = 128
EPS = 1e-05
WIDE = ("t", "g", "p")
NARROW = ("y", "c")
GROUP = ("g", "p", "c")
ALL = ("t", "g", "p", "y", "c")
BF = jnp.bfloat16
F32 = jnp.float32
ROWS = 1024
COLS = 256
WIDE_COLS = 512
COST = pl.CostEstimate(flops=1000, transcendentals=0, bytes_accessed=1000)


def rms_scale(values, scales):
    return values * lax.rsqrt(jnp.mean(values * values, axis=-1, keepdims=True) + EPS) * scales


def rope_tables(length, head_dim):
    exponent = jnp.arange(0, head_dim, 2, dtype=F32) / head_dim
    angles = jnp.arange(length, dtype=F32)[:, None] * (10000.0 ** (-exponent))[None, :]
    cosines, sines = jnp.cos(angles), jnp.sin(angles)
    return (
        jnp.concatenate([cosines, cosines], axis=-1),
        jnp.concatenate([-sines, sines], axis=-1),
    )


def dot(a, b, contract):
    return lax.dot_general(a, b, (contract, ((), ())), preferred_element_type=F32)


def place_of(array):
    large = array.size * array.dtype.itemsize > 1 << 20
    return pl.BlockSpec(memory_space=pltpu.HBM if large else pl.ANY)


def call(body, outs, scratch, args, flops, vmem, moved):
    return pl.pallas_call(
        body,
        out_shape=outs,
        in_specs=[place_of(a) for a in args],
        out_specs=jax.tree.map(lambda _: pl.BlockSpec(memory_space=pl.ANY), outs),
        scratch_shapes=scratch,
        compiler_params=pltpu.CompilerParams(vmem_limit_bytes=vmem << 20),
        cost_estimate=COST,
    )(*args)


def start_all(copies):
    for one in copies:
        one.start()
    return copies


def wait_all(copies):
    for one in copies:
        one.wait()


def weight_copies(pieces, whole, sems, stride=1, at=0):
    units = pieces[0].shape[3]
    copies = []
    for half, piece in enumerate(pieces):
        for c in range(2):
            k = half * 2 + c
            there = pl.ds((k * stride + at) * units, units)
            copies.append(
                pltpu.make_async_copy(piece.at[:, c], whole.at[:, :, there], sems.at[k])
            )
    return copies


def block_copies(blocks, whole, sems):
    rows = blocks[0].shape[0]
    return [
        pltpu.make_async_copy(b, whole.at[pl.ds(i * rows, rows)], sems.at[i])
        for i, b in enumerate(blocks)
    ]


def arrived(view, sem):
    pltpu.make_async_copy(view, view, sem).wait()


def await_weight(whole, sems, k, now):
    units = whole.shape[2] // 4

    @pl.when(now)
    def _():
        arrived(whole.at[:, :, pl.ds(pl.multiple_of(k * units, units), units)], sems.at[k])


def await_rows(whole, sems, count, r):
    rows = whole.shape[0] // count
    each = max(1, ROWS // rows)
    if rows <= ROWS:
        for i in range(each):
            b = r * each + i
            arrived(whole.at[pl.ds(pl.multiple_of(b * rows, rows), rows)], sems.at[b])
    else:

        @pl.when(r % (rows // ROWS) == 0)
        def _():
            b = r // (rows // ROWS)
            arrived(whole.at[pl.ds(pl.multiple_of(b * rows, rows), rows)], sems.at[b])


def to_column(line):
    return jnp.transpose(jnp.broadcast_to(line, (128, 128)))


def to_line(column):
    return jnp.transpose(jnp.broadcast_to(column, (128, 128)))[:1]


def take(ref, k, size=COLS):
    part = ref[:, :, pl.ds(pl.multiple_of(k * size, size), size)]
    return part.reshape(-1, size)


def take_rows(ref, n, size=COLS):
    each = size // ref.shape[1]
    return ref[pl.ds(n * each, each)].reshape(size, ref.shape[2])


def project_body(count, *refs):
    blocks, pieces, out = refs[:count], refs[count : count + 2], refs[count + 2]
    rows_v, weight_v, out_v, sem_b, sem_w, sem_o = refs[count + 3 :]
    cw = weight_copies(pieces, weight_v, sem_w)
    cb = block_copies(blocks, rows_v, sem_b)
    ahead = max(1, count * ROWS // rows_v.shape[0])
    start_all(cb[:ahead] + cw + cb[ahead:])
    steps = rows_v.shape[0] // ROWS

    def row_step(r, carry):
        here = pl.ds(pl.multiple_of(r * ROWS, ROWS), ROWS)
        await_rows(rows_v, sem_b, count, r)

        def col_step(k, carry):
            for n in range(WIDE_COLS // COLS):
                await_weight(weight_v, sem_w, k * (WIDE_COLS // COLS) + n, r == 0)
            cols = pl.ds(pl.multiple_of(k * WIDE_COLS, WIDE_COLS), WIDE_COLS)
            got = dot(rows_v[here, :], take(weight_v, k, WIDE_COLS), ((1,), (0,)))
            out_v[here, cols] = got.astype(BF)
            return carry

        lax.fori_loop(0, out_v.shape[1] // WIDE_COLS, col_step, 0)
        pltpu.make_async_copy(out_v.at[here], out.at[here], sem_o.at[r]).start()
        return carry

    lax.fori_loop(0, steps, row_step, 0)
    for r in range(steps):
        here = pl.ds(r * ROWS, ROWS)
        pltpu.make_async_copy(out_v.at[here], out.at[here], sem_o.at[r]).wait()


def project(blocks, got, other):
    rows = blocks[0].shape[0] * len(blocks)
    model = blocks[0].shape[1]
    w, _, depth, units = got.shape
    hidden = 4 * units
    return call(
        functools.partial(project_body, len(blocks)),
        jax.ShapeDtypeStruct((rows, hidden), BF),
        [
            pltpu.VMEM((rows, model), BF),
            pltpu.VMEM((w, depth, hidden), BF),
            pltpu.VMEM((rows, hidden), BF),
            pltpu.SemaphoreType.DMA((len(blocks),)),
            pltpu.SemaphoreType.DMA((4,)),
            pltpu.SemaphoreType.DMA((rows // ROWS,)),
        ],
        (*blocks, got, other),
        2 * rows * model * hidden,
        40,
        2 * (rows * model + model * hidden + rows * hidden),
    )


def expert_body(count, *refs):
    blocks = refs[:count]
    gate_p, up_p = refs[count : count + 2], refs[count + 2 : count + 4]
    down_grad, own_gate = refs[count + 4 : count + 6]
    gg, ug, hs, dots = refs[count + 6 : count + 10]
    rows_v, pair_v, grad_v, own_v, gg_v, ug_v, hs_v, dots_v = refs[count + 10 : count + 18]
    own_c, pair_a, pair_b, sem_b, sem_w, sem_i, sem_o = refs[count + 18 :]
    ci = start_all(
        [
            pltpu.make_async_copy(down_grad, grad_v, sem_i.at[0]),
            pltpu.make_async_copy(own_gate, own_v, sem_i.at[1]),
        ]
    )
    cg = weight_copies(gate_p, pair_v, sem_w.at[0], 2, 0)
    cu = weight_copies(up_p, pair_v, sem_w.at[1], 2, 1)
    cb = block_copies(blocks, rows_v, sem_b)
    ahead = max(1, count * ROWS // rows_v.shape[0])
    start_all(cb[:ahead] + [c for two in zip(cg, cu) for c in two] + cb[ahead:])
    wait_all(ci)
    steps = rows_v.shape[0] // ROWS
    lines = ROWS // 128
    outs = ((gg_v, gg, 0), (ug_v, ug, 1), (hs_v, hs, 2))
    chunks = gg_v.shape[1] // COLS
    for i in range(own_v.shape[0]):
        own_c[i * 128 : (i + 1) * 128, :] = to_column(own_v[i : i + 1, :])

    def ready(i):
        k = i % chunks

        @pl.when(k == 0)
        def _():
            await_rows(rows_v, sem_b, count, i // chunks)

        @pl.when(i < chunks)
        def _():
            for n in range(2):
                there = pl.ds(pl.multiple_of((2 * k + n) * COLS, COLS), COLS)
                arrived(pair_v.at[:, :, there], sem_w.at[n, k])

    def rows_at(i):
        return pl.ds(pl.multiple_of((i // chunks) * ROWS, ROWS), ROWS)

    def products(i, pair_s):
        pair_s[...] = dot(
            rows_v[rows_at(i), :], take(pair_v, i % chunks, 2 * COLS), ((1,), (0,))
        )

    def activate(i, pair_s, total):
        here, k = rows_at(i), i % chunks
        cols = pl.ds(pl.multiple_of(k * COLS, COLS), COLS)
        own = own_c[here, :1]
        gate, up = pair_s[:, :COLS], pair_s[:, COLS:]
        grad = grad_v[here, cols].astype(F32)
        sig = 1.0 / (1.0 + jnp.exp(-gate))
        act = gate * sig
        hidden = act * up
        hs_v[here, cols] = (own * hidden).astype(BF)
        part = jnp.sum(hidden * grad, axis=1, keepdims=True)
        grad = own * grad
        gg_v[here, cols] = (grad * up * (sig + act * (1.0 - sig))).astype(BF)
        ug_v[here, cols] = (grad * act).astype(BF)
        return jnp.where(k == 0, 0.0, total) + part

    ready(0)
    products(0, pair_a)
    most = steps * chunks - 1

    def step(j, total):
        i = 2 * j
        ready(i + 1)
        after_next = jnp.minimum(i + 2, most)

        @pl.when(i + 2 <= most)
        def _():
            ready(i + 2)

        products(i + 1, pair_b)
        total = activate(i, pair_a, total)
        products(after_next, pair_a)
        total = activate(i + 1, pair_b, total)

        @pl.when((i + 1) % chunks == chunks - 1)
        def _():
            r = i // chunks
            dots_v[pl.ds(pl.multiple_of(r * lines, lines), lines), :] = jnp.concatenate(
                [to_line(total[n * 128 : (n + 1) * 128]) for n in range(lines)], axis=0
            )
            for src, dst, n in outs:
                here = rows_at(i)
                pltpu.make_async_copy(src.at[here], dst.at[here], sem_o.at[n, r]).start()

        return total

    lax.fori_loop(0, steps * chunks // 2, step, jnp.zeros((ROWS, 1), F32))
    last = pltpu.make_async_copy(dots_v, dots, sem_i.at[2])
    last.start()
    for r in range(steps):
        here = pl.ds(r * ROWS, ROWS)
        for src, dst, i in outs:
            pltpu.make_async_copy(src.at[here], dst.at[here], sem_o.at[i, r]).wait()
    last.wait()


def expert(blocks, gate_p, up_p, down_grad, own_gate):
    rows = blocks[0].shape[0] * len(blocks)
    model = blocks[0].shape[1]
    w, _, depth, units = gate_p[0].shape
    hidden = 4 * units
    steps = rows // ROWS
    out = jax.ShapeDtypeStruct((rows, hidden), BF)
    wide = jax.ShapeDtypeStruct(own_gate.shape, F32)
    return call(
        functools.partial(expert_body, len(blocks)),
        (out, out, out, wide),
        [
            pltpu.VMEM((rows, model), BF),
            pltpu.VMEM((w, depth, 2 * hidden), BF),
            pltpu.VMEM((rows, hidden), BF),
            pltpu.VMEM(own_gate.shape, F32),
            pltpu.VMEM((rows, hidden), BF),
            pltpu.VMEM((rows, hidden), BF),
            pltpu.VMEM((rows, hidden), BF),
            pltpu.VMEM(own_gate.shape, F32),
            pltpu.VMEM((rows, 128), F32),
        ]
        + [pltpu.VMEM((ROWS, 2 * COLS), F32)] * 2
        + [
            pltpu.SemaphoreType.DMA((len(blocks),)),
            pltpu.SemaphoreType.DMA((2, 4)),
            pltpu.SemaphoreType.DMA((3,)),
            pltpu.SemaphoreType.DMA((3, steps)),
        ],
        (*blocks, *gate_p, *up_p, down_grad, own_gate),
        4 * rows * model * hidden,
        56,
        2 * (rows * model + 2 * model * hidden + 4 * rows * hidden),
    )


def back_body(first, pairs, tail, *refs):
    refs = list(refs)
    ins = [refs[3 * i : 3 * i + 3] for i in range(pairs)]
    at = 3 * pairs
    if tail:
        dots, place = refs[at : at + 2]
        at += 2
    out = refs[at]
    scratch = refs[at + 1 :]
    if tail:
        dots_v, place_v, sem_t = scratch[-3:]
        scratch = scratch[:-3]
        side = start_all(
            [
                pltpu.make_async_copy(dots, dots_v, sem_t.at[0]),
                pltpu.make_async_copy(place, place_v, sem_t.at[1]),
            ]
        )
    grads, weights = scratch[:pairs], scratch[pairs : 2 * pairs]
    out_v, sem_g, sem_w, sem_o = scratch[2 * pairs :]
    rows = out_v.shape[0]
    each = WIDE_COLS // weights[0].shape[1]
    parts = weights[0].shape[0] // each
    for i, (grad, got, other) in enumerate(ins):
        pltpu.make_async_copy(grad.at[pl.ds(first, rows)], grads[i], sem_g.at[i]).start()
    for n in range(parts):
        place = pl.ds(n * each, each)
        for i, (grad, got, other) in enumerate(ins):
            pieces = (got.at[place], other.at[place])
            start_all(weight_copies(pieces, weights[i].at[place], sem_w.at[i, n]))
    for i in range(pairs):
        arrived(grads[i], sem_g.at[i])

    def col_step(n, carry):
        for i in range(pairs):
            block = weights[i].at[pl.ds(n * each, each)]
            for k in range(4):
                await_weight(block, sem_w.at[i, n], k, n >= 0)
        cols = pl.ds(pl.multiple_of(n * WIDE_COLS, WIDE_COLS), WIDE_COLS)
        total = dot(grads[0][...], take_rows(weights[0], n, WIDE_COLS), ((1,), (1,)))
        for i in range(1, pairs):
            total += dot(grads[i][...], take_rows(weights[i], n, WIDE_COLS), ((1,), (1,)))
        out_v[:, cols] = total.astype(BF)
        pltpu.make_async_copy(out_v.at[:, cols], out.at[:, cols], sem_o.at[n]).start()
        return carry

    if tail:
        wait_all(side)
        cols = pl.ds(parts * WIDE_COLS, 128)
        for i in range(rows // 128):
            line = dots_v[first // 128 + i : first // 128 + i + 1, :]
            value = (to_column(line) * place_v[...]).astype(BF)
            out_v[i * 128 : (i + 1) * 128, parts * WIDE_COLS :] = value
        last = pltpu.make_async_copy(out_v.at[:, cols], out.at[:, cols], sem_o.at[parts])
        last.start()
    lax.fori_loop(0, parts, col_step, 0)
    for n in range(parts):
        cols = pl.ds(n * WIDE_COLS, WIDE_COLS)
        pltpu.make_async_copy(out_v.at[:, cols], out.at[:, cols], sem_o.at[n]).wait()
    if tail:
        last.wait()


def back(triples, first, rows, tail=()):
    w, _, depth, units = triples[0][1].shape
    model, hidden = w * depth, 4 * units
    n = len(triples)
    full = model + 128 if tail else model
    return call(
        functools.partial(back_body, first, n, bool(tail)),
        jax.ShapeDtypeStruct((rows, full), BF),
        [pltpu.VMEM((rows, hidden), BF)] * n
        + [pltpu.VMEM((w, depth, hidden), BF)] * n
        + [
            pltpu.VMEM((rows, full), BF),
            pltpu.SemaphoreType.DMA((n,)),
            pltpu.SemaphoreType.DMA((n, model // WIDE_COLS, 4)),
            pltpu.SemaphoreType.DMA((model // WIDE_COLS + 1,)),
        ]
        + [pltpu.VMEM(t.shape, F32) for t in tail]
        + [pltpu.SemaphoreType.DMA((2,))] * bool(tail),
        [a for t in triples for a in t] + list(tail),
        2 * n * rows * model * hidden,
        58 if tail else 40,
        2 * (n * rows * hidden + n * model * hidden + rows * model),
    )


def weight_body(count, depth, *refs):
    blocks, grad, mine, theirs = refs[:count], refs[count], refs[count + 1], refs[count + 2]
    rows_v, grad_v, out_v, sem_b, sem_g, sem_o = refs[count + 3 :]
    cg = pltpu.make_async_copy(grad, grad_v, sem_g.at[0])
    wait_all(start_all(block_copies(blocks, rows_v, sem_b) + [cg]))
    units = COLS
    each = COLS // depth
    steps = rows_v.shape[1] // COLS

    def step(n, carry):
        cols = pl.ds(pl.multiple_of(n * COLS, COLS), COLS)
        got = dot(rows_v[:, cols], grad_v[...], ((0,), (0,))).astype(BF)
        for k in range(4):
            part = got[:, k * units : (k + 1) * units].reshape(each, depth, units)
            out_v[k // 2, pl.ds(n * each, each), k % 2] = part
        place = pl.ds(n * each, each)
        pltpu.make_async_copy(out_v.at[0, place], mine.at[place], sem_o.at[0, n]).start()
        pltpu.make_async_copy(out_v.at[1, place], theirs.at[place], sem_o.at[1, n]).start()
        return carry

    lax.fori_loop(0, steps, step, 0)
    for n in range(steps):
        place = pl.ds(n * each, each)
        pltpu.make_async_copy(out_v.at[0, place], mine.at[place], sem_o.at[0, n]).wait()
        pltpu.make_async_copy(out_v.at[1, place], theirs.at[place], sem_o.at[1, n]).wait()


def weight_grad(blocks, grad, depth):
    rows = blocks[0].shape[0] * len(blocks)
    model = blocks[0].shape[1]
    hidden = grad.shape[1]
    w = model // depth
    piece = jax.ShapeDtypeStruct((w, 2, depth, hidden // 4), BF)
    steps = model // COLS
    return call(
        functools.partial(weight_body, len(blocks), depth),
        (piece, piece),
        [
            pltpu.VMEM((rows, model), BF),
            pltpu.VMEM((rows, hidden), BF),
            pltpu.VMEM((2, w, 2, depth, hidden // 4), BF),
            pltpu.SemaphoreType.DMA((len(blocks),)),
            pltpu.SemaphoreType.DMA((1,)),
            pltpu.SemaphoreType.DMA((2, steps)),
        ],
        (*blocks, grad),
        2 * rows * model * hidden,
        40,
        2 * (rows * model + model * hidden + rows * hidden),
    )


def terms_body(pairs, *refs):
    ins, me, outs = refs[: 2 * pairs], refs[2 * pairs], refs[2 * pairs + 1 : 2 * pairs + 3]
    scratch = refs[2 * pairs + 3 :]
    held, out_v, sems, out_sem = scratch[: 2 * pairs], scratch[-3], scratch[-2], scratch[-1]
    wait_all(
        start_all(
            [pltpu.make_async_copy(ins[i], held[i], sems.at[i]) for i in range(2 * pairs)]
        )
    )
    _, count, _, depth, _ = out_v.shape
    mine = me[0]

    each = COLS // depth

    def step(n, carry):
        rows = pl.ds(pl.multiple_of(n * COLS, COLS), COLS)
        at = 0
        for i in range(pairs):
            wide = held[2 * i + 1].shape[1]
            got = dot(held[2 * i][:, rows], held[2 * i + 1][...], ((0,), (0,))).astype(BF)
            for j in range(each):
                b = n * each + j
                distance = jnp.bitwise_xor(b % 8, mine)
                half = distance % 2
                far = distance // 2
                place = (far % 2) * 2 + far // 2
                out_v[half, b // 8, place, :, at : at + wide] = got[j * depth : (j + 1) * depth]
            at += wide
        return carry

    lax.fori_loop(0, count * 8 // each, step, 0)
    wait_all(
        start_all([pltpu.make_async_copy(out_v.at[i], outs[i], out_sem.at[i]) for i in range(2)])
    )


def block_terms(pairs, me, depth):
    length, model = pairs[0][0].shape
    count = model // (8 * depth)
    n = sum(c.shape[1] for _, c in pairs)
    piece = jax.ShapeDtypeStruct((count, 4, depth, n), BF)
    flat = [x for two in pairs for x in two]
    return pl.pallas_call(
        functools.partial(terms_body, len(pairs)),
        out_shape=(piece, piece),
        in_specs=[place_of(a) for a in flat]
        + [pl.BlockSpec(memory_space=pltpu.SMEM)],
        out_specs=(pl.BlockSpec(memory_space=pl.ANY),) * 2,
        scratch_shapes=[pltpu.VMEM(x.shape, BF) for x in flat]
        + [
            pltpu.VMEM((2,) + piece.shape, BF),
            pltpu.SemaphoreType.DMA((len(flat),)),
            pltpu.SemaphoreType.DMA((2,)),
        ],
        compiler_params=pltpu.CompilerParams(vmem_limit_bytes=24 << 20),
        cost_estimate=COST,
    )(*flat, me)


def to_columns(line):
    return jnp.concatenate(
        [to_column(line[:, i : i + 128])[:, :1] for i in range(0, line.shape[1], 128)], axis=0
    )


def to_lines(column):
    return jnp.concatenate(
        [to_line(column[i : i + 128]) for i in range(0, column.shape[0], 128)], axis=1
    )


def bring(ins, held, sems):
    wait_all(
        start_all([pltpu.make_async_copy(a, b, sems.at[i]) for i, (a, b) in enumerate(zip(ins, held))])
    )


def send_out(held, outs, sems):
    wait_all(
        start_all([pltpu.make_async_copy(a, b, sems.at[i]) for i, (a, b) in enumerate(zip(held, outs))])
    )


def raw_body(normed, weights, query, key, value, squares, *scratch):
    normed_v, weights_v, query_v, key_v, value_v, squares_v, sem_i, sem_o = scratch
    wide = query_v.shape[1]
    bring((normed, weights.at[:, pl.ds(0, 3 * wide)]), (normed_v, weights_v), sem_i)
    length = query_v.shape[0]
    for place, ref in ((0, query_v), (1, key_v)):

        def step(j, total):
            cols = pl.ds(pl.multiple_of(j * COLS, COLS), COLS)
            w = weights_v[:, pl.ds(pl.multiple_of(place * wide + j * COLS, COLS), COLS)]
            got = dot(normed_v[...], w, ((1,), (0,)))
            ref[:, cols] = got
            return total + jnp.sum(got * got, axis=1, keepdims=True)

        total = lax.fori_loop(0, wide // COLS, step, jnp.zeros((length, 1), F32))
        squares_v[place : place + 1, :] = to_lines(total)

    def step(j, carry):
        cols = pl.ds(pl.multiple_of(j * COLS, COLS), COLS)
        w = weights_v[:, pl.ds(pl.multiple_of(2 * wide + j * COLS, COLS), COLS)]
        value_v[:, cols] = dot(normed_v[...], w, ((1,), (0,))).astype(BF)
        return carry

    lax.fori_loop(0, wide // COLS, step, 0)
    send_out((query_v, key_v, value_v, squares_v), (query, key, value, squares), sem_o)


def raw_heads(normed, weights, wide):
    length, model = normed.shape
    shapes = [((length, wide), F32), ((length, wide), F32), ((length, wide), BF), ((2, length), F32)]
    return call(
        raw_body,
        tuple(jax.ShapeDtypeStruct(*one) for one in shapes),
        [pltpu.VMEM((length, model), BF), pltpu.VMEM((model, 3 * wide), BF)]
        + [pltpu.VMEM(*one) for one in shapes]
        + [pltpu.SemaphoreType.DMA((2,)), pltpu.SemaphoreType.DMA((4,))],
        (normed, weights),
        0,
        58,
        0,
    )


def half_turn(values):
    return pltpu.roll(values, HD // 2, 1)


def attend_body(*refs):
    ins, outs, scratch = refs[:10], refs[10:15], refs[15:]
    held, made, sem_i, sem_o = scratch[:10], scratch[10:15], scratch[15], scratch[16]
    query, key, value, scales, gains, cosines, sines, ids, weights = ins[:9]
    wide = query.shape[1]
    views = list(ins[:9])
    views[8] = weights.at[:, pl.ds(3 * wide, wide)]
    bring(views, held[:9], sem_i)
    query_v, key_v, value_v, scales_v, gains_v, cos_v, sin_v, ids_v, weights_v = held[:9]
    query_o, key_o, attended_o, log_o, out_o = made
    line = ids_v[...]
    allowed = line <= to_columns(line)
    scale_q, scale_k = to_columns(scales_v[0:1, :]), to_columns(scales_v[1:2, :])

    def step(h, carry):
        cols = pl.ds(pl.multiple_of(h * HD, HD), HD)
        cosines, sines = cos_v[...], sin_v[...]
        q = query_v[:, cols] * scale_q * gains_v[0:1, cols]
        k = key_v[:, cols] * scale_k * gains_v[1:2, cols]
        q = (q * cosines + half_turn(q) * sines).astype(BF)
        k = (k * cosines + half_turn(k) * sines).astype(BF)
        query_o[:, cols] = q
        key_o[:, cols] = k
        scores = jnp.where(allowed, dot(q, k, ((1,), (1,))) * HD**-0.5, -1e30)
        highest = jnp.max(scores, axis=1, keepdims=True)
        shifted = jnp.exp(scores - highest)
        totals = jnp.sum(shifted, axis=1, keepdims=True)
        probs = (shifted / totals).astype(BF)
        attended_o[:, cols] = dot(probs, value_v[:, cols], ((1,), (0,))).astype(BF)
        log_o[pl.ds(h, 1), :] = to_lines(highest + jnp.log(totals))
        return carry

    lax.fori_loop(0, wide // HD, step, 0)

    def out_step(j, carry):
        cols = pl.ds(pl.multiple_of(j * COLS, COLS), COLS)
        out_o[:, cols] = dot(attended_o[...], weights_v[cols, :], ((1,), (1,))).astype(BF)
        return carry

    lax.fori_loop(0, out_o.shape[1] // COLS, out_step, 0)
    send_out(made, outs, sem_o)


def attend(query, key, value, scales, gains, tables, ids, weights):
    length, wide = query.shape
    model = weights.shape[0]
    args = (query, key, value, scales, gains, *tables, ids, weights, ids)
    held = [pltpu.VMEM(x.shape, x.dtype) for x in args[:8]]
    held += [pltpu.VMEM((model, wide), BF), pltpu.VMEM(ids.shape, ids.dtype)]
    shapes = [
        ((length, wide), BF),
        ((length, wide), BF),
        ((length, wide), BF),
        ((wide // HD, length), F32),
        ((length, model), BF),
    ]
    return call(
        attend_body,
        tuple(jax.ShapeDtypeStruct(*one) for one in shapes),
        held
        + [pltpu.VMEM(*one) for one in shapes]
        + [pltpu.SemaphoreType.DMA((9,)), pltpu.SemaphoreType.DMA((5,))],
        args,
        0,
        58,
        0,
    )


def unattend_body(*refs):
    ins, outs, scratch = refs[:12], refs[12:16], refs[16:]
    held, grad_v, made, sem_i, sem_o = (
        scratch[:12], scratch[12], scratch[13:17], scratch[17], scratch[18],
    )
    wide = ins[2].shape[1]
    views = list(ins)
    views[1] = ins[1].at[:, pl.ds(3 * wide, wide)]
    bring(views, held, sem_i)
    cot_v, weights_v, query_v, key_v, value_v, log_v, ids_v, cos_v, sin_v, gains_v, raw_q, raw_k = held
    query_o, key_o, value_o, dots_o = made
    grad_v[...] = dot(cot_v[...], weights_v[...], ((1,), (0,))).astype(BF)
    line = ids_v[...]
    allowed = line <= to_columns(line)
    length = cot_v.shape[0]
    zero = jnp.zeros((length, 1), F32)

    def step(h, carry):
        dot_q, dot_k = carry
        cols = pl.ds(pl.multiple_of(h * HD, HD), HD)
        cosines, sines = cos_v[...], sin_v[...]
        q, k, v, grad = query_v[:, cols], key_v[:, cols], value_v[:, cols], grad_v[:, cols]
        scores = jnp.where(allowed, dot(q, k, ((1,), (1,))) * HD**-0.5, -1e30)
        probs = jnp.exp(scores - to_columns(log_v[pl.ds(h, 1), :]))
        prob_grad = dot(grad, v, ((1,), (1,)))
        centre = jnp.sum(probs * prob_grad, axis=1, keepdims=True)
        score_grad = (probs * (prob_grad - centre)).astype(BF)
        value_o[:, cols] = dot(probs.astype(BF), grad, ((0,), (0,))).astype(BF)
        back_q = dot(score_grad, k, ((1,), (0,))) * HD**-0.5
        back_k = dot(score_grad, q, ((0,), (0,))) * HD**-0.5
        back_q = back_q * cosines + half_turn(back_q * sines)
        back_k = back_k * cosines + half_turn(back_k * sines)
        query_o[:, cols] = back_q
        key_o[:, cols] = back_k
        dot_q += jnp.sum(gains_v[0:1, cols] * back_q * raw_q[:, cols], axis=1, keepdims=True)
        dot_k += jnp.sum(gains_v[1:2, cols] * back_k * raw_k[:, cols], axis=1, keepdims=True)
        return dot_q, dot_k

    dot_q, dot_k = lax.fori_loop(0, wide // HD, step, (zero, zero))
    dots_o[0:1, :] = to_lines(dot_q)
    dots_o[1:2, :] = to_lines(dot_k)
    send_out(made, outs, sem_o)


def unattend(out_cot, weights, query, key, value, logs, ids, tables, gains, raw_q, raw_k):
    length, wide = query.shape
    args = (out_cot, weights, query, key, value, logs, ids, *tables, gains, raw_q, raw_k)
    held = [pltpu.VMEM(x.shape, x.dtype) for x in args]
    held[1] = pltpu.VMEM((weights.shape[0], wide), BF)
    shapes = [((length, wide), F32), ((length, wide), F32), ((length, wide), BF), ((2, length), F32)]
    return call(
        unattend_body,
        tuple(jax.ShapeDtypeStruct(*one) for one in shapes),
        held
        + [pltpu.VMEM((length, wide), BF)]
        + [pltpu.VMEM(*one) for one in shapes]
        + [pltpu.SemaphoreType.DMA((12,)), pltpu.SemaphoreType.DMA((4,))],
        args,
        0,
        58,
        0,
    )


def unnorm_body(*refs):
    ins, outs, scratch = refs[:7], refs[7:9], refs[9:]
    held, made, sem_i, sem_o = scratch[:7], scratch[7:9], scratch[9], scratch[10]
    bring(ins, held, sem_i)
    back_q, back_k, raw_q, raw_k, scales_v, dots_v, gains_v = held
    grads_o, gains_o = made
    wide = raw_q.shape[1]
    for i, (back, raw) in enumerate(((back_q, raw_q), (back_k, raw_k))):
        scale = to_columns(scales_v[i : i + 1, :])
        push = to_columns(dots_v[i : i + 1, :]) * scale * scale * scale
        grad = scale * gains_v[i : i + 1, :] * back[...] - raw[...] * push
        grads_o[:, i * wide : (i + 1) * wide] = grad.astype(BF)
        gains_o[i : i + 1, :] = jnp.sum(back[...] * raw[...] * scale, axis=0, keepdims=True)
    send_out(made, outs, sem_o)


def unnorm(back_q, back_k, raw_q, raw_k, scales, dots, gains):
    length, wide = raw_q.shape
    args = (back_q, back_k, raw_q, raw_k, scales, dots, gains)
    shapes = [((length, 2 * wide), BF), ((2, wide), F32)]
    return call(
        unnorm_body,
        tuple(jax.ShapeDtypeStruct(*one) for one in shapes),
        [pltpu.VMEM(x.shape, x.dtype) for x in args]
        + [pltpu.VMEM(*one) for one in shapes]
        + [pltpu.SemaphoreType.DMA((7,)), pltpu.SemaphoreType.DMA((2,))],
        args,
        0,
        24,
        0,
    )


def after(values, *earlier):
    return lax.optimization_barrier((values, earlier))[0]


def stage(*values):
    return lax.optimization_barrier(values)


def swap(values, axis, step=1):
    count = lax.axis_size(axis)
    return lax.ppermute(values, axis, [(i, i ^ step) for i in range(count)])


def gather_four(block, axis):
    count = lax.axis_size("y") * lax.axis_size("c")
    size = block.shape[axis]
    here = lax.axis_index("y") * lax.axis_size("c") + lax.axis_index("c")
    other = swap(block, "y")
    near = swap(block, "c")
    far = swap(other, "c")
    shape = list(block.shape)
    shape[axis] = size * count
    whole = jnp.zeros(shape, block.dtype)
    for piece, place in ((block, 0), (near, 1), (other, 2), (far, 3)):
        whole = lax.dynamic_update_slice_in_dim(whole, piece, (here ^ place) * size, axis)
    return whole


def sum_near(partial):
    length, width = partial.shape
    y, c = lax.axis_index("y"), lax.axis_index("c")
    parts = partial.reshape(2, 2, length // 4, width)
    mine = lax.dynamic_index_in_dim(parts, c, 1, False)
    theirs = lax.dynamic_index_in_dim(parts, 1 - c, 1, False)
    mine = mine.astype(F32) + swap(theirs.astype(BF), "c").astype(F32)
    keep = lax.dynamic_index_in_dim(mine, y, 0, False)
    send = lax.dynamic_index_in_dim(mine, 1 - y, 0, False)
    return keep, send.astype(BF)


def add(*pieces):
    total = pieces[0].astype(F32)
    for piece in pieces[1:]:
        total = total + piece.astype(F32)
    return total


def to_experts(columns):
    sent = lax.all_to_all(columns.T, GROUP, 0, 0, tiled=True)
    v = sent.reshape((-1, 2) + sent.shape[1:])
    c = lax.axis_index("c")
    own = lax.dynamic_index_in_dim(v, c, 1, False)
    other = lax.dynamic_index_in_dim(v, 1 - c, 1, False)
    return jnp.concatenate([own, other]).reshape(sent.shape[0], -1)


def to_group(weight):
    got = lax.all_to_all(weight, GROUP, 0, 0, tiled=True)
    return got.reshape((got.shape[0] // 2, 2) + got.shape[1:])


def over_sequences(*terms):
    if lax.axis_size("t") > 1:
        terms = [lax.psum_scatter(x, "t", scatter_dimension=0, tiled=True) for x in terms]
    return [x[0] for x in terms]


def over_groups(piece):
    if lax.axis_size("t") > 1:
        piece = lax.all_gather(piece, "t", axis=0, tiled=True)
    return piece


def sum_over(values, axis):
    step = 1
    while step < lax.axis_size(axis):
        values = values + swap(values, axis, step)
        step *= 2
    return values


def to_slices(mine, theirs):
    total = (mine.astype(F32) + theirs.astype(F32)).astype(BF)
    if lax.axis_size("t") > 1:
        total = lax.psum_scatter(total, "t", scatter_dimension=0, tiled=True)
    sent = total.reshape((-1,) + total.shape[2:])
    return lax.all_to_all(sent, GROUP, 0, 0, tiled=True)


def as_output(got):
    return jnp.transpose(got, (1, 0, 2)).astype(F32)


def per_device(
    tokens,
    cotangent,
    block_ids,
    routes,
    norm_attn,
    w_query,
    w_key,
    w_value,
    norm_query,
    norm_key,
    w_out,
    norm_ffn,
    w_router,
    w_gate,
    w_up,
    w_down,
):
    experts = w_router.shape[1]
    lane_index = lax.axis_index("y") * lax.axis_size("c") + lax.axis_index("c")
    lanes = lax.axis_size("y") * lax.axis_size("c")
    length, head_cols = tokens.shape
    model_width = head_cols * lanes
    rows = length // lanes

    all_full = lax.all_gather(
        jnp.concatenate([w_query, w_key, w_value, w_out], axis=1), WIDE, axis=0, tiled=True
    )

    rows_full = gather_four(tokens, 1)
    gains = lax.all_gather(jnp.stack([norm_attn, norm_ffn]), NARROW, axis=1, tiled=True)
    down_got = to_group(jnp.transpose(w_down, (1, 0, 2)))
    gate_sent = jnp.transpose(w_gate, (1, 0, 2))
    up_sent = jnp.transpose(w_up, (1, 0, 2))
    cot_rows = lax.all_to_all(cotangent.reshape(lanes, rows, head_cols), NARROW, 0, 0, tiled=True)
    cot_rows = jnp.transpose(cot_rows, (1, 0, 2)).reshape(rows, model_width)
    rows_full, cot_rows, gate_sent, up_sent, gains = stage(
        rows_full, cot_rows, gate_sent, up_sent, gains
    )
    attn_gain = gains[0].astype(F32)
    ffn_gain = gains[1].astype(F32)
    rows_float = rows_full.astype(F32)
    normed = rms_scale(rows_float, attn_gain).astype(BF)
    down_got, gate_sent, normed, cot_sent = stage(down_got, gate_sent, normed, cot_rows)

    down_other = swap(down_got, "y")
    all_full, normed, cot_sent, gate_sent, down_other = stage(
        all_full, normed, cot_sent, gate_sent, down_other
    )

    gate_got = to_group(gate_sent)
    cot_mine = lax.all_gather(cot_sent, ("g", "p"), axis=0, tiled=True)
    qkv_full = all_full[:, : 3 * head_cols]
    raw_query, raw_key, value_bf, squares = raw_heads(normed, all_full, head_cols)
    scales = lax.rsqrt(lax.psum(squares, NARROW) / model_width + EPS)
    scales, gate_got, up_sent = stage(scales, gate_got, up_sent)
    up_got = to_group(up_sent)
    cut = gate_got.shape[0] // 2
    gate_first = swap(gate_got[:cut], "y")
    gains_here = jnp.stack([norm_query, norm_key]).astype(F32)
    tables = rope_tables(length, HD)
    ids = block_ids.astype(F32)
    query_bf, key_bf, attended, log_totals, out_partial = attend(
        raw_query, raw_key, value_bf, scales, gains_here, tables, ids, all_full
    )

    first_row = lane_index * rows
    x_rows = lax.dynamic_slice_in_dim(rows_full, first_row, rows, 0).astype(F32)
    keep, send = sum_near(out_partial)
    keep, send, gate_first = stage(keep, send, gate_first)
    residual = x_rows + keep + swap(send, "y").astype(F32)
    ffn_in = rms_scale(residual, ffn_gain).astype(BF)
    ffn_in, up_got, gate_got, cot_mine = stage(ffn_in, up_got, gate_got, cot_mine)

    up_other = swap(up_got, "y")
    gate_last = swap(gate_got[cut:], "y")
    x_mine = lax.all_gather(ffn_in, ("g", "p"), axis=0, tiled=True)
    cot_all = [cot_mine, swap(cot_mine, "c")]
    down_own = (over_groups(down_got), over_groups(down_other))
    down_grad = project(cot_all, *down_own)
    logits = jnp.dot(ffn_in, w_router, preferred_element_type=F32)
    gate_probs = jax.nn.softmax(logits, axis=-1)
    routes_rows = lax.dynamic_slice_in_dim(routes, first_row, rows, 0)
    chosen = jnp.any(
        routes_rows[:, :, None] == jnp.arange(experts, dtype=jnp.int32)[None, None, :], axis=1
    )
    own_gate = to_experts(jnp.where(chosen, gate_probs, 0.0))
    x_mine, down_grad, own_gate, up_other, gate_last = stage(
        x_mine, down_grad, own_gate, up_other, gate_last
    )
    gate_other = jnp.concatenate([gate_first, gate_last])
    x_all = [x_mine, swap(x_mine, "c")]
    gate_own = (over_groups(gate_got), over_groups(gate_other))
    up_own = (over_groups(up_got), over_groups(up_other))

    gate_grad, up_grad, hidden_gated, own_dots = expert(
        x_all, gate_own, up_own, down_grad, own_gate
    )
    half = gate_grad.shape[0] // 2
    own_index = lax.axis_index("g") * 4 + lax.axis_index("p") * 2 + lax.axis_index("c")
    depth = down_own[0].shape[2]
    own_place = (jnp.arange(128) == own_index).astype(F32)[None]
    depth = down_own[0].shape[2]
    pairs = ((gate_grad, *gate_own), (up_grad, *up_own))
    theirs = back(pairs, half, half, (own_dots, own_place))
    gate_grad, up_grad, own_dots, theirs = stage(gate_grad, up_grad, own_dots, theirs)
    pairs = ((gate_grad, *gate_own), (up_grad, *up_own))
    mine = back(pairs, 0, half, (own_dots, own_place))
    sent = add(mine, swap(theirs, "c")).astype(BF)
    sent, hidden_gated, gate_grad, up_grad = stage(sent, hidden_gated, gate_grad, up_grad)

    input_sum = lax.psum_scatter(sent, ("g", "p"), scatter_dimension=0, tiled=True)
    down_mine, down_theirs = weight_grad(cot_all, hidden_gated, depth)
    down_theirs, gate_grad, hidden_gated, up_grad = stage(
        down_theirs, gate_grad, hidden_gated, up_grad
    )
    down_theirs = swap(down_theirs, "y")
    gate_mine, gate_theirs = weight_grad(x_all, gate_grad, depth)
    up_mine, up_theirs = weight_grad(x_all, up_grad, depth)
    moe_pair = ((hidden_gated, *down_own),)
    moe_theirs = back(moe_pair, half, half)
    moe_mine = back(moe_pair, 0, half)
    down_theirs, gate_theirs, up_theirs, moe_theirs, moe_mine = stage(
        down_theirs, gate_theirs, up_theirs, moe_theirs, moe_mine
    )
    cut = gate_theirs.shape[0] // 2
    gate_first = swap(gate_theirs[:cut], "y")
    down_got = to_slices(down_mine, down_theirs)
    moe_sent = add(moe_mine, swap(moe_theirs, "c")).astype(BF)
    input_sum, moe_sent, gate_first = stage(input_sum, moe_sent, gate_first)
    moe_sum = lax.psum_scatter(moe_sent, ("g", "p"), scatter_dimension=0, tiled=True)
    input_sum = input_sum.astype(F32)
    pair_dots = jnp.where(chosen, input_sum[:, model_width : model_width + experts], 0.0)
    input_sum = input_sum[:, :model_width]

    logit_grad = (
        gate_probs * (pair_dots - jnp.sum(gate_probs * pair_dots, axis=1, keepdims=True))
    ).astype(BF)
    ffn_grad = input_sum + dot(logit_grad, w_router, ((1,), (1,)))
    router_grad = dot(logit_grad, ffn_in, ((0,), (0,)))
    _, ffn_norm_pull = jax.vjp(rms_scale, residual, ffn_gain)
    residual_norm_grad, ffn_gain_grad = ffn_norm_pull(ffn_grad)
    residual_grad = cot_rows.astype(F32) + residual_norm_grad
    out_cot = gather_four(residual_grad.astype(BF), 0)
    out_cot, up_theirs, down_got, gate_theirs = stage(out_cot, up_theirs, down_got, gate_theirs)

    gate_last = swap(gate_theirs[cut:], "y")
    back_query, back_key, value_grad, dots = unattend(
        out_cot, all_full, query_bf, key_bf, value_bf, log_totals, ids, tables, gains_here,
        raw_query, raw_key,
    )
    group_index = (lax.axis_index("g") * 2 + lax.axis_index("p")).astype(jnp.int32)[None]
    two_keep, two_near = over_sequences(
        *block_terms(((out_cot, attended), (normed, value_grad)), group_index, depth)
    )
    dots, two_near, two_keep, gate_last = stage(dots, two_near, two_keep, gate_last)
    gate_got = to_slices(gate_mine, jnp.concatenate([gate_first, gate_last]))
    two_near = swap(two_near, "p")
    dots = lax.psum(dots, NARROW) / model_width
    dots, up_theirs = stage(dots, up_theirs)

    up_theirs = swap(up_theirs, "y")
    pair_pre, pair_gains = unnorm(
        back_query, back_key, raw_query, raw_key, scales, dots, gains_here
    )
    qkv_grad = jnp.concatenate([pair_pre, value_grad], axis=1)
    pair_keep, pair_near = over_sequences(*block_terms(((normed, pair_pre),), group_index, depth))
    qkv_grad, pair_keep, pair_near = stage(qkv_grad, pair_keep, pair_near)
    pair_near = swap(pair_near, "p")
    keep, send = sum_near(dot(qkv_grad, qkv_full, ((1,), (1,))))
    keep, send, up_theirs, gate_got = stage(keep, send, up_theirs, gate_got)
    up_got = to_slices(up_mine, up_theirs)
    send = swap(send, "y")
    send, two_near, two_keep = stage(send, two_near, two_keep)
    normed_grad = add(keep, send)
    two_parts = add(two_keep, two_near)
    two_far = swap(two_parts[2:].astype(BF), "g", 1)
    _, attn_norm_pull = jax.vjp(rms_scale, x_rows, attn_gain)
    rows_norm_grad, attn_gain_grad = attn_norm_pull(normed_grad)
    grad_rows = (residual_grad + rows_norm_grad).astype(BF)
    place = (jnp.arange(lanes) == lane_index).astype(F32)[:, None]
    small = jnp.concatenate(
        [
            router_grad,
            attn_gain_grad[None],
            ffn_gain_grad[None],
            (place * pair_gains[:1]).reshape(1, model_width),
            (place * pair_gains[1:]).reshape(1, model_width),
        ],
        axis=0,
    )
    small = sum_over(small, "g")
    grad_rows, two_far, two_parts, pair_near, pair_keep, small, moe_sum = stage(
        grad_rows, two_far, two_parts, pair_near, pair_keep, small, moe_sum
    )

    pair_parts = add(pair_keep, pair_near)
    pair_far = swap(pair_parts[2:].astype(BF), "g", 1)
    two_parts = add(two_parts[:2], two_far)
    two_far = swap(two_parts[1].astype(BF), "g", 2)
    small = sum_over(sum_over(small, "p"), "t")
    pair_far, pair_parts, two_far, two_parts, small, up_got, grad_rows, moe_sum = stage(
        pair_far, pair_parts, two_far, two_parts, small, up_got, grad_rows, moe_sum
    )

    pair_parts = add(pair_parts[:2], pair_far)
    pair_far = swap(pair_parts[1].astype(BF), "g", 2)
    small = sum_over(sum_over(small, "y"), "c")
    grad_two = add(two_parts[0], two_far)
    both_rows = jnp.stack([(residual + moe_sum.astype(F32)).astype(BF), grad_rows])
    both_rows = jnp.transpose(both_rows.reshape(2, rows, lanes, head_cols), (2, 0, 1, 3))
    both_rows = lax.all_to_all(both_rows, NARROW, 0, 0, tiled=True)
    block_out = both_rows[:, 0].reshape(length, head_cols)
    grad_tokens = both_rows[:, 1].reshape(length, head_cols).astype(F32)
    grad_gate = as_output(gate_got)
    grad_down = as_output(down_got)
    grad_up = as_output(up_got)
    grad_pair = add(pair_parts[0], pair_far)
    grad_out, grad_value = grad_two[:, :head_cols], grad_two[:, head_cols:]
    grad_query, grad_key = grad_pair[:, :head_cols], grad_pair[:, head_cols:]
    grad_router = small[:experts].T
    four = lax.dynamic_slice_in_dim(small[experts:], lane_index * head_cols, head_cols, 1)
    return (
        block_out,
        grad_tokens,
        four[0],
        grad_query.astype(F32),
        grad_key.astype(F32),
        grad_value.astype(F32),
        four[2],
        four[3],
        grad_out.astype(F32),
        four[1],
        grad_router,
        grad_gate,
        grad_up,
        grad_down,
    )


def solution(mesh):
    wide, narrow = mesh.shape["wide"], mesh.shape["narrow"]
    near = 2
    middle = min(wide // near, 4)
    inner = Mesh(mesh.devices.reshape(wide // (near * middle), middle, near, narrow // 2, 2), ALL)
    both = P(WIDE, NARROW)
    cube = P(WIDE, None, NARROW)
    lane = P(NARROW)
    row = P(WIDE, None)
    return jax.shard_map(
        per_device,
        mesh=inner,
        in_specs=(
            both, both, row, row, lane, both, both, both, lane, lane, both, lane, P(),
            cube, cube, cube,
        ),
        out_specs=(
            both, both, lane, both, both, both, lane, lane, both, lane, P(), cube, cube, cube,
        ),
        check_vma=False,
    )
```
